32 devices in a mesh: fsdp: 4 (over y, core), ctx: 2 (over x), tp: 4 (over z).
Axes of the slice: x: 2, y: 2, z: 4, core: 2. Of those that a mesh axis runs over, the one named last changes fastest.
Arguments:
- tokens: bfloat16 [4, 1024, 2048], P('fsdp', 'ctx'), may hold values from -6 to 6
- lengths: int32 [4, 3], P('fsdp'), may hold values from 1 to 768, 960 in all within a row
- block_order: int32 [4, 4], P('fsdp'), may hold values from 0 to 3, each once within a row
- ln_gain: bfloat16 [2048], P('fsdp'), may hold values from 0.25 to 1.75
- ln_bias: bfloat16 [2048], P('fsdp'), may hold values from -3 to 3
- qkv_weight: bfloat16 [2048, 3, 2048], P('fsdp', None, 'tp'), may hold values from -0.125 to 0.125
- qkv_bias: bfloat16 [3, 2048], P(None, 'tp'), may hold values from -0.59765625 to 0.59765625
- dense_weight: bfloat16 [2048, 2048], P('fsdp', 'tp'), may hold values from -1 to 1
- dense_bias: bfloat16 [2048], P('fsdp'), may hold values from -3 to 3
- fc1_weight: bfloat16 [2048, 8192], P('fsdp', 'tp'), may hold values from -0.125 to 0.125
- fc1_bias: bfloat16 [8192], P('tp'), may hold values from -3 to 3
- fc2_weight: bfloat16 [2048, 8192], P('fsdp', 'tp'), may hold values from -0.0625 to 0.0625
- fc2_bias: bfloat16 [2048], P('fsdp'), may hold values from -3 to 3
- cotangent: bfloat16 [4, 1024, 2048], P('fsdp', 'ctx'), may hold values from -6 to 6
Outputs:
- output: bfloat16 [4, 1024, 2048], P('fsdp', 'ctx')
- input_grad: float32 [4, 1024, 2048], P('fsdp', 'ctx')
- ln_gain_grad: float32 [2048], P('fsdp')
- ln_bias_grad: float32 [2048], P('fsdp')
- qkv_weight_grad: float32 [2048, 3, 2048], P('fsdp', None, 'tp')
- qkv_bias_grad: float32 [3, 2048], P(None, 'tp')
- dense_weight_grad: float32 [2048, 2048], P('fsdp', 'tp')
- dense_bias_grad: float32 [2048], P('fsdp')
- fc1_weight_grad: float32 [2048, 8192], P('fsdp', 'tp')
- fc1_bias_grad: float32 [8192], P('tp')
- fc2_weight_grad: float32 [2048, 8192], P('fsdp', 'tp')
- fc2_bias_grad: float32 [2048], P('fsdp')
The draws below stay inside these ranges and needn't reach their ends.
Inputs may be any that keep to these rules, and one draw needn't show every extreme that they name: Each row holds the lengths of 3 sequences packed from the row's start; they sum to 960 and the largest is exactly 768. Each row is a permutation of the 4 block numbers; dealt block j holds packed block block_order[b, j].
All inputs are finite; a program needn't handle non-finite values.
Results may differ from the reference program's by a relative error of at most 0.012.
Values may be sent and summed in bfloat16 or wider, within the bound.
No kernel may reach another device: no remote copies, remote signals or barrier semaphores. Data moves between devices by JAX's collectives and lax.ppermute only.
A program may use at most 256 MiB of HBM per device.

```python
import math
import jax
import jax.numpy as jnp
import numpy as np
from jax import lax

D = 2048
H = 8
HD = 256
ROT = 64
FF = 8192
BLOCK = 256
NBLOCK = 4
GROUP = 1024
VALID = 960
LONGEST = 768
SEQS = 3
BATCH = 4


def raised(drawn, key, source, target, parts, factor):
    owner, partner = [(jnp.arange(drawn.shape[dim]) // (drawn.shape[dim] // parts)).reshape([-1 if axis == dim else 1 for axis in range(drawn.ndim)]) for dim in (source, target)]
    chosen = jax.random.permutation(key, parts)[partner]
    strong = (owner == chosen) | (owner == (partner + parts // 2) % parts)
    return jnp.where(strong, factor * drawn, drawn)


def steps_of(stream_key, extent, split, low, largest):
    loudness, own = 1.0, jax.random.fold_in(stream_key, 6)
    for dim, blocks in split:
        draws = jnp.exp(jax.random.uniform(jax.random.fold_in(own, dim), (blocks,), jnp.float32, low / len(split), largest / len(split)))
        loudness = loudness * jnp.repeat(draws, extent[dim] // blocks).reshape([-1 if axis == dim else 1 for axis in range(len(extent))])
    return loudness


def profile(amount, total, reach, lean):
    weights = [(1 << 20) // math.isqrt(rank ** lean) + 1 for rank in range(2, amount + 1)]
    rest, counts = total - reach - (amount - 1), [1] * (amount - 1)
    while rest > 0:
        candidates = [i for i in range(amount - 1) if counts[i] < reach]
        mass, left = sum([weights[i] for i in candidates]), rest
        for i in candidates:
            more = min(reach - counts[i], max(1, left * weights[i] // mass), rest)
            counts[i] = counts[i] + more
            rest = rest - more
    return np.array([reach] + counts)


def ragged(key, amount, total, reach, skew):
    if amount == 2:
        one = jax.random.randint(key, (), max(1, total - reach), min(reach, total - 1) + 1)
        return jnp.stack([one, total - one])
    sizes = jnp.asarray(profile(amount, total, reach, skew), jnp.int32)
    twos = (amount - 1) // 2
    source_of, receiver = sizes[1:1 + 2 * twos:2], sizes[2:2 + 2 * twos:2]
    margin = jnp.minimum(source_of - 1, reach - receiver)
    moved = jax.random.randint(jax.random.fold_in(key, 1), (twos,), 0, 1 << 20) % (margin + 1)
    sizes = sizes.at[1:1 + 2 * twos:2].set(source_of - moved).at[2:2 + 2 * twos:2].set(receiver + moved)
    return sizes[jax.random.permutation(jax.random.fold_in(key, 2), amount)]


def bell_draw(stream_key, shape, spread, reach, shards=(), kind=jnp.bfloat16):
    values = jax.random.normal(stream_key, shape, jnp.float32) * spread
    if len(shards) > 0:
        values = steps_of(stream_key, shape, shards, -0.22, 0.18) * values
    return jnp.clip(values, min=-reach, max=reach).astype(kind)


def gaussian_with(key, extent, scale, limit, split, heavy, kind=jnp.bfloat16):
    entries = scale * jax.random.normal(key, extent, jnp.float32)
    if split:
        entries = entries * steps_of(key, extent, split, -0.22, 0.18)
    return jnp.clip(raised(entries, jax.random.fold_in(key, 3), *heavy), -limit, limit).astype(kind)


def setup_inputs(seed: int = 0) -> dict:
    key_list = jax.random.split(jax.random.key(seed), 15)
    tokens = gaussian_with(key_list[0], (BATCH, GROUP, D), 1.0, 6.0, ((0, 4), (1, 2)), (1, 2, 2, 2.0))
    lengths = jax.vmap(lambda own: ragged(own, SEQS, VALID, LONGEST, 2))(jax.random.split(key_list[1], BATCH)).reshape((BATCH, SEQS)).astype(jnp.int32)
    block_order = jax.vmap(lambda own: jax.random.permutation(own, NBLOCK))(jax.random.split(key_list[2], BATCH)).reshape((BATCH, NBLOCK)).astype(jnp.int32)
    ln_gain = jnp.clip(1.0 + 0.15 * jax.random.normal(key_list[3], (D,), jnp.float32), 0.25, 1.75).astype(jnp.bfloat16)
    ln_bias = bell_draw(key_list[4], (D,), 0.5, 3.0, ((0, 4),))
    qkv_weight = bell_draw(key_list[5], (D, 3, D), D ** -0.5, 0.125, ((0, 4), (2, 4)))
    qkv_bias = bell_draw(key_list[6], (3, D), 0.1, 0.59765625, ((1, 4),))
    dense_weight = bell_draw(key_list[7], (D, D), (max(2, D // 64)) ** -0.5, 1.0, ((0, 4), (1, 4)))
    dense_bias = bell_draw(key_list[8], (D,), 0.5, 3.0, ((0, 4),))
    fc1_weight = bell_draw(key_list[9], (D, FF), D ** -0.5, 0.125, ((0, 4), (1, 4)))
    fc1_bias = bell_draw(key_list[10], (FF,), 0.5, 3.0, ((0, 4),))
    fc2_weight = bell_draw(key_list[11], (D, FF), FF ** -0.5, 0.0625, ((0, 4), (1, 4)))
    fc2_bias = bell_draw(key_list[12], (D,), 0.5, 3.0, ((0, 4),))
    cotangent = gaussian_with(key_list[13], (BATCH, GROUP, D), 1.0, 6.0, ((0, 4), (1, 2)), (1, 2, 2, 2.0))
    return dict(tokens=tokens, lengths=lengths, block_order=block_order, ln_gain=ln_gain, ln_bias=ln_bias, qkv_weight=qkv_weight, qkv_bias=qkv_bias, dense_weight=dense_weight, dense_bias=dense_bias, fc1_weight=fc1_weight, fc1_bias=fc1_bias, fc2_weight=fc2_weight, fc2_bias=fc2_bias, cotangent=cotangent)


NORM_EPSILON = 1e-05
MASK_FLOOR = -1000000000.0
HIGHEST = lax.Precision.HIGHEST

@jax.custom_vjp
def low(v):
    return lax.optimization_barrier(v.astype(jnp.bfloat16)).astype(jnp.float32)

@jax.custom_vjp
def low_back(v):
    return v

def low_keep(v):
    return (low(v), None)

def low_pass(kept, grad):
    return (grad,)

def back_keep(v):
    return (v, None)

def back_low(kept, grad):
    return (low(grad),)
low.defvjp(low_keep, low_pass)
low_back.defvjp(back_keep, back_low)

def rotation_tables(position):
    frequency = jnp.exp(jnp.arange(ROT // 2, dtype=jnp.float32) * (-2.0 * math.log(10000.0) / ROT))
    angles = position.astype(jnp.float32)[:, None] * frequency[None, :]
    return (jnp.cos(angles)[:, None, :], jnp.sin(angles)[:, None, :])

def rotate(values, cosine_table, sine_table):
    first_half = values[..., :ROT // 2]
    second_half = values[..., ROT // 2:ROT]
    return jnp.concatenate([first_half * cosine_table - second_half * sine_table, second_half * cosine_table + first_half * sine_table, values[..., ROT:]], axis=-1)

def row_layout(lengths_row, order_row):
    row_index = jnp.arange(GROUP, dtype=jnp.int32)
    packed_at = order_row[row_index // BLOCK] * BLOCK + row_index % BLOCK
    seq_ends = jnp.cumsum(lengths_row, dtype=jnp.int32)
    passed = packed_at[:, None] >= seq_ends[None, :]
    segment = lax.optimization_barrier(jnp.sum(passed.astype(jnp.int32), axis=1, dtype=jnp.int32))
    before = lax.optimization_barrier(jnp.sum(jnp.where(passed, lengths_row[None, :], 0), axis=1, dtype=jnp.int32))
    return (packed_at, segment, packed_at - before)

def layer_row(params, row_inputs, packed_at, segment, position):
    norm_gain, norm_bias, qkv_weight, qkv_bias, dense_weight, dense_bias, fc1_weight, fc1_bias, fc2_weight, fc2_bias = params
    row_mean = lax.optimization_barrier(jnp.mean(row_inputs, axis=1, keepdims=True))
    centred = row_inputs - row_mean
    variance = lax.optimization_barrier(jnp.mean(centred * centred, axis=1, keepdims=True))
    normed = low(centred * lax.rsqrt(variance + NORM_EPSILON) * norm_gain + norm_bias)
    projected = low_back(jnp.einsum('td,dce->tce', normed, qkv_weight, precision=HIGHEST) + qkv_bias)
    cosine_table, sine_table = rotation_tables(position)
    shaped = projected.reshape(GROUP, 3, H, HD)
    queries = low(rotate(shaped[:, 0], cosine_table, sine_table))
    keys_all = low(rotate(shaped[:, 1], cosine_table, sine_table))
    values_all = low(shaped[:, 2])
    allowed = (segment[:, None] == segment[None, :]) & (packed_at[None, :] <= packed_at[:, None])

    def attend_head(head_inputs):
        head_queries, head_keys, head_values = head_inputs
        scores = low_back(jnp.dot(head_queries, head_keys.T, precision=HIGHEST) * (1.0 / math.sqrt(HD)))
        scores = jnp.where(allowed, scores, MASK_FLOOR)
        row_max = lax.optimization_barrier(jnp.max(scores, axis=1, keepdims=True))
        exp_scores = jnp.exp(scores - row_max)
        probabilities = low(exp_scores / lax.optimization_barrier(jnp.sum(exp_scores, axis=1, keepdims=True)))
        return jnp.dot(probabilities, head_values, precision=HIGHEST)
    attended = lax.map(jax.checkpoint(attend_head), (queries.transpose(1, 0, 2), keys_all.transpose(1, 0, 2), values_all.transpose(1, 0, 2)))
    valid_rows = (segment < SEQS).astype(jnp.float32)
    attended = attended.transpose(1, 0, 2).reshape(GROUP, D) * valid_rows[:, None]
    attended = low(low_back(attended))
    pre_act = low_back(jnp.dot(normed, fc1_weight, precision=HIGHEST) + fc1_bias)
    hidden = low(jax.nn.gelu(pre_act, approximate=False))
    attn_branch = jnp.dot(attended, dense_weight.T, precision=HIGHEST) + dense_bias
    ffn_branch = jnp.dot(hidden, fc2_weight.T, precision=HIGHEST) + fc2_bias
    return row_inputs + attn_branch + ffn_branch

def reference(tokens, lengths, block_order, ln_gain, ln_bias, qkv_weight, qkv_bias, dense_weight, dense_bias, fc1_weight, fc1_bias, fc2_weight, fc2_bias, cotangent):
    params = tuple((argument.astype(jnp.float32) for argument in (ln_gain, ln_bias, qkv_weight, qkv_bias, dense_weight, dense_bias, fc1_weight, fc1_bias, fc2_weight, fc2_bias)))
    inputs = tokens.astype(jnp.float32)
    upstream = cotangent.astype(jnp.float32)
    packed_all, segments, positions = lax.map(lambda both_rows: row_layout(both_rows[0], both_rows[1]), (lengths, block_order))

    def whole_layer(layer_params, layer_inputs):
        return lax.map(lambda row_parts: layer_row(layer_params, row_parts[0], row_parts[1], row_parts[2], row_parts[3]), (layer_inputs, packed_all, segments, positions))
    outputs, pullback = jax.vjp(whole_layer, params, inputs)
    param_grads, input_grad = pullback(upstream)
    return (outputs.astype(jnp.bfloat16), input_grad, param_grads[0], param_grads[1], param_grads[2], param_grads[3], param_grads[4], param_grads[5], param_grads[6], param_grads[7], param_grads[8], param_grads[9])
```

```python
import math

import jax
import jax.numpy as jnp
from jax import lax
from jax.sharding import PartitionSpec as P

HD = 256
ROT = 64


NORM_EPSILON = 1e-05
MASK_FLOOR = -1000000000.0
F32 = jnp.float32
BF16 = jnp.bfloat16


def rotation_tables(position):
    frequency = jnp.exp(jnp.arange(ROT // 2, dtype=F32) * (-2.0 * math.log(10000.0) / ROT))
    angles = position.astype(F32)[:, None] * frequency[None, :]
    return (jnp.cos(angles), jnp.sin(angles))


def rotate(values, cosine_table, sine_table):
    first_half = values[..., : ROT // 2]
    second_half = values[..., ROT // 2 : ROT]
    return jnp.concatenate(
        [
            first_half * cosine_table - second_half * sine_table,
            second_half * cosine_table + first_half * sine_table,
            values[..., ROT:],
        ],
        axis=-1,
    )


def rotate_back(grads, cosine_table, sine_table):
    return rotate(grads, cosine_table, -sine_table)


def packed_rows(order_row, slots, block_rows):
    selector = slots[:, None] == jnp.arange(order_row.shape[0], dtype=jnp.int32)[None, :]
    source_block = jnp.sum(jnp.where(selector, order_row[None, :], 0), axis=1, dtype=jnp.int32)
    within = jnp.arange(block_rows, dtype=jnp.int32)
    return (source_block[:, None] * block_rows + within[None, :]).reshape(-1)


def place_rows(packed_at, lengths_row):
    seq_ends = jnp.cumsum(lengths_row, dtype=jnp.int32)
    passed = packed_at[:, None] >= seq_ends[None, :]
    segment = jnp.sum(passed.astype(jnp.int32), axis=1, dtype=jnp.int32)
    before = jnp.sum(jnp.where(passed, lengths_row[None, :], 0), axis=1, dtype=jnp.int32)
    return (segment, packed_at - before)


def dot(a, b, contract):
    return lax.dot_general(a, b, (contract, ((), ())), preferred_element_type=F32)


def swap(x, bit):
    size = lax.axis_size("fsdp")
    return lax.ppermute(x, "fsdp", [(i, i ^ bit) for i in range(size)])


def ctx_pair(x):
    return lax.ppermute(x, "ctx", [(0, 1), (1, 0)])


def ctx_sum(x):
    if lax.axis_size("ctx") == 2:
        return x.astype(F32) + ctx_pair(x).astype(F32)
    return lax.psum(x.astype(F32), "ctx")


def tp_shift(x, d):
    size = lax.axis_size("tp")
    return lax.ppermute(x, "tp", [(i, (i + d) % size) for i in range(size)])


def blocks(x, order):
    width = x.shape[1] // 4
    return jnp.concatenate([x[:, k * width : (k + 1) * width] for k in order], axis=1)


def framed(x, me):
    width = x.shape[1] // 4
    return jnp.concatenate(
        [lax.dynamic_slice_in_dim(x, (me ^ k) * width, width, axis=1) for k in range(4)], axis=1
    )


def half_of(x, which, axis):
    size = x.shape[axis] // 2
    return lax.dynamic_slice_in_dim(x, which * size, size, axis=axis)


def in_order(mine, other, core, axis):
    return jnp.where(
        core == 0,
        jnp.concatenate([mine, other], axis=axis),
        jnp.concatenate([other, mine], axis=axis),
    )


def gather_weight(mine, other):
    return jnp.concatenate([mine, swap(other, 1), swap(mine, 2), swap(other, 3)], axis=0)


def reduce_weight(left, right):
    rows = left.shape[1] // 2
    far = dot(left[:, rows:], right, ((0,), (0,))).astype(BF16)
    near = (dot(left[:, :rows], right, ((0,), (0,))) + swap(far, 2).astype(F32)).astype(BF16)
    kept, given = near[: rows // 2], near[rows // 2 :]
    return ctx_sum(kept), ctx_sum(swap(given, 1))


def scatter_rows(own, tp_index):
    size = lax.axis_size("tp")
    rows = own.shape[0] // size

    def part(d):
        return lax.dynamic_slice_in_dim(own, ((tp_index + d) % size) * rows, rows, axis=0)

    total = part(0)
    for d in range(1, size):
        total = total + tp_shift(part(d).astype(BF16), d).astype(F32)
    return total


def gather_rows(part, tp_index, dtype):
    size = lax.axis_size("tp")
    rows = part.shape[0]
    whole = jnp.zeros((rows * size, part.shape[1]), dtype)
    for d in range(size):
        piece = tp_shift(part, d) if d else part
        at = ((tp_index - d) % size) * rows
        whole = lax.dynamic_update_slice_in_dim(whole, piece.astype(dtype), at, axis=0)
    return whole


def per_device(
    tokens,
    lengths,
    block_order,
    ln_gain,
    ln_bias,
    qkv_weight,
    qkv_bias,
    dense_weight,
    dense_bias,
    fc1_weight,
    fc1_bias,
    fc2_weight,
    fc2_bias,
    cotangent,
):
    me = lax.axis_index("fsdp")
    core = me % 2
    tp_index = lax.axis_index("tp")
    ctx_index = lax.axis_index("ctx")
    ctx_size = lax.axis_size("ctx")
    shard = ln_gain.shape[0]
    row_count = tokens.shape[1]
    block_rows = row_count // 2
    score_scale = 1.0 / math.sqrt(HD)

    qkv_halves = [
        half_of(qkv_weight, which, 2).reshape(shard, 3 * HD) for which in (core, 1 - core)
    ]
    qkv_full = gather_weight(*qkv_halves)
    dense_full = gather_weight(*[half_of(dense_weight, w, 1) for w in (core, 1 - core)])
    fc1_full = gather_weight(*[half_of(fc1_weight, w, 1) for w in (core, 1 - core)])
    fc2_full = gather_weight(*[half_of(fc2_weight, w, 1) for w in (core, 1 - core)])

    vectors = jnp.stack([ln_gain, ln_bias, dense_bias, fc2_bias])
    vectors = jnp.concatenate([vectors] + [swap(vectors, k) for k in (1, 2, 3)], axis=1)
    norm_gain = vectors[0:1].astype(F32)
    norm_bias = vectors[1:2].astype(F32)
    out_bias = vectors[2:3].astype(F32) + vectors[3:4].astype(F32)

    layout = jnp.concatenate([lengths[0], block_order[0]])
    seq_count = lengths.shape[1]
    layouts = [layout, swap(layout, 1)]
    local_slots = ctx_index * 2 + jnp.arange(2, dtype=jnp.int32)
    if ctx_size == 2:
        key_slots = jnp.concatenate([local_slots, (1 - ctx_index) * 2 + jnp.arange(2)])
    else:
        key_slots = jnp.arange(block_order.shape[1], dtype=jnp.int32)
    allowed, valid, positions = [], [], []
    for each in layouts:
        lengths_row, order_row = each[:seq_count], each[seq_count:]
        local_packed = packed_rows(order_row, local_slots, block_rows)
        key_packed = packed_rows(order_row, key_slots, block_rows)
        segment, position = place_rows(local_packed, lengths_row)
        key_segment = place_rows(key_packed, lengths_row)[0]
        allowed.append(
            (segment[:, None] == key_segment[None, :])
            & (key_packed[None, :] <= local_packed[:, None])
        )
        valid.append((segment < seq_count).astype(F32)[:, None])
        positions.append(position)
    cosine_table, sine_table = rotation_tables(jnp.concatenate(positions))
    valid = jnp.concatenate(valid)

    inputs_low = framed(tokens[0], me)
    upstream_low = framed(cotangent[0], me)

    def normalise(rows):
        rows = rows.astype(F32)
        centred = rows - jnp.mean(rows, axis=1, keepdims=True)
        variance = jnp.mean(centred * centred, axis=1, keepdims=True)
        inverse = lax.rsqrt(variance + NORM_EPSILON)
        return centred * inverse, inverse

    normed_own = (normalise(inputs_low)[0] * norm_gain + norm_bias).astype(BF16)
    swapped = (1, 0, 3, 2)
    normed = jnp.concatenate([normed_own, blocks(swap(normed_own, 1), swapped)])
    upstream = jnp.concatenate([upstream_low, blocks(swap(upstream_low, 1), swapped)])

    projected = dot(normed, qkv_full, ((1,), (0,)))
    qkv_bias_own = half_of(qkv_bias, core, 1).astype(F32).reshape(1, 3 * HD)
    projected = projected + qkv_bias_own
    queries = rotate(projected[:, :HD], cosine_table, sine_table).astype(BF16)
    keys_local = rotate(projected[:, HD : 2 * HD], cosine_table, sine_table).astype(BF16)
    values_local = projected[:, 2 * HD :].astype(BF16)
    both_local = jnp.concatenate([keys_local, values_local], axis=1)
    both_local = both_local.reshape(2, row_count, 2 * HD)
    if ctx_size == 2:
        both_all = jnp.concatenate([both_local, ctx_pair(both_local)], axis=1)
    else:
        both_all = lax.all_gather(both_local, "ctx", axis=1, tiled=True)

    attended, probs_all = [], []
    for s in range(2):
        rows = slice(s * row_count, (s + 1) * row_count)
        keys, values = both_all[s, :, :HD], both_all[s, :, HD:]
        scores = dot(queries[rows], keys, ((1,), (1,))) * score_scale
        scores = jnp.where(allowed[s], scores, MASK_FLOOR)
        exp_scores = jnp.exp(scores - jnp.max(scores, axis=1, keepdims=True))
        probs = exp_scores / jnp.sum(exp_scores, axis=1, keepdims=True)
        probs_all.append(probs)
        attended.append(dot(probs.astype(BF16), values, ((1,), (0,))))
    attended = (jnp.concatenate(attended) * valid).astype(BF16)

    pre_act = dot(normed, fc1_full, ((1,), (0,))) + half_of(fc1_bias, core, 0).astype(F32)[None, :]
    normal_cdf = 0.5 * (1.0 + lax.erf(pre_act * (1.0 / math.sqrt(2.0))))
    density = jnp.exp(-0.5 * pre_act * pre_act) * (1.0 / math.sqrt(2.0 * math.pi))
    hidden = (pre_act * normal_cdf).astype(BF16)
    slope = normal_cdf + pre_act * density

    def share(rows, first, first_weight, second, second_weight, contract):
        return dot(first[rows], first_weight, contract) + dot(second[rows], second_weight, contract)

    own_rows, other_rows = slice(0, row_count), slice(row_count, 2 * row_count)

    def summed(first, first_weight, second, second_weight, contract):
        theirs = share(other_rows, first, first_weight, second, second_weight, contract)
        theirs = swap(blocks(theirs.astype(BF16), swapped), 1)
        own = share(own_rows, first, first_weight, second, second_weight, contract)
        return scatter_rows(own + theirs.astype(F32), tp_index)

    inputs_part = lax.dynamic_slice_in_dim(
        inputs_low, tp_index * (row_count // lax.axis_size("tp")), row_count // lax.axis_size("tp")
    )
    upstream_part = lax.dynamic_slice_in_dim(
        upstream_low,
        tp_index * (row_count // lax.axis_size("tp")),
        row_count // lax.axis_size("tp"),
    ).astype(F32)
    out_part = summed(attended, dense_full, hidden, fc2_full, ((1,), (1,)))
    out_part = (inputs_part.astype(F32) + out_part + out_bias).astype(BF16)
    output = gather_rows(framed(out_part, me), tp_index, BF16)

    fc2_grad = reduce_weight(upstream, hidden)
    hidden_grad = dot(upstream, fc2_full, ((1,), (0,)))
    pre_grad_wide = hidden_grad * slope
    pre_grad = pre_grad_wide.astype(BF16)
    fc1_grad = reduce_weight(normed, pre_grad)
    dense_grad = reduce_weight(upstream, attended)
    attended_grad = (dot(upstream, dense_full, ((1,), (0,))).astype(BF16) * valid.astype(BF16))

    query_pieces, both_pieces = [], []
    for s in range(2):
        rows = slice(s * row_count, (s + 1) * row_count)
        keys, values = both_all[s, :, :HD], both_all[s, :, HD:]
        probs = probs_all[s]
        head_grad = attended_grad[rows]
        prob_grad = dot(head_grad, values, ((1,), (1,)))
        row_delta = jnp.sum(probs * prob_grad, axis=1, keepdims=True)
        score_grad = (probs * (prob_grad - row_delta)).astype(BF16)
        query_pieces.append(dot(score_grad, keys, ((1,), (0,))) * score_scale)
        key_piece = dot(score_grad, queries[rows], ((0,), (0,))) * score_scale
        value_piece = dot(probs.astype(BF16), head_grad, ((0,), (0,)))
        both_pieces.append(jnp.concatenate([key_piece, value_piece], axis=1))
    both_grad = jnp.stack(both_pieces)
    if ctx_size == 2:
        theirs = ctx_pair(both_grad[:, row_count:].astype(BF16))
        both_grad = both_grad[:, :row_count] + theirs.astype(F32)
    else:
        both_grad = lax.psum_scatter(both_grad, "ctx", scatter_dimension=1, tiled=True)
    both_grad = both_grad.reshape(2 * row_count, 2 * HD)
    proj_grad = jnp.concatenate(
        [
            rotate_back(jnp.concatenate(query_pieces), cosine_table, sine_table),
            rotate_back(both_grad[:, :HD], cosine_table, sine_table),
            both_grad[:, HD:],
        ],
        axis=1,
    ).astype(BF16)
    qkv_grad = reduce_weight(normed, proj_grad)

    full_grad = summed(pre_grad, fc1_full, proj_grad, qkv_full, ((1,), (1,)))
    standard, inverse = normalise(inputs_part)
    scaled = full_grad * norm_gain
    input_part = upstream_part + inverse * (
        scaled
        - jnp.mean(scaled, axis=1, keepdims=True)
        - standard * jnp.mean(scaled * standard, axis=1, keepdims=True)
    )
    input_grad = gather_rows(framed(input_part.astype(BF16), me), tp_index, F32)

    column_sums = jnp.concatenate(
        [
            jnp.sum(pre_grad.astype(F32), axis=0, keepdims=True),
            jnp.sum(proj_grad.astype(F32), axis=0, keepdims=True),
        ],
        axis=1,
    )
    column_sums = column_sums + swap(column_sums, 2)
    column_sums = ctx_sum(column_sums)
    column_other = swap(column_sums, 1)
    hidden_half = fc1_bias.shape[0] // 2
    fc1_bias_grad = in_order(column_sums[0, :hidden_half], column_other[0, :hidden_half], core, 0)
    qkv_bias_grad = in_order(
        column_sums[0, hidden_half:].reshape(3, HD), column_other[0, hidden_half:].reshape(3, HD), core, 1
    )

    def to_shard(sums):
        sums = sums[:, : 2 * shard] + swap(sums[:, 2 * shard :], 2)
        sums = sums[:, :shard] + swap(sums[:, shard:], 1)
        return ctx_sum(sums)

    out_bias_grad = to_shard(jnp.sum(upstream_low.astype(F32), axis=0, keepdims=True))[0]
    norm_sums = jnp.concatenate(
        [
            jnp.sum(full_grad * standard, axis=0, keepdims=True),
            jnp.sum(full_grad, axis=0, keepdims=True),
        ]
    )
    norm_sums = to_shard(norm_sums)
    for d in (1, 2):
        norm_sums = norm_sums + lax.ppermute(norm_sums, "tp", [(i, i ^ d) for i in range(4)])

    def whole_columns(halves):
        return in_order(halves[0], halves[1], core, 1)

    qkv_whole = in_order(
        qkv_grad[0].reshape(shard, 3, HD), qkv_grad[1].reshape(shard, 3, HD), core, 2
    )
    return (
        output[None],
        input_grad[None],
        norm_sums[0],
        norm_sums[1],
        qkv_whole,
        qkv_bias_grad,
        whole_columns(dense_grad),
        out_bias_grad,
        whole_columns(fc1_grad),
        fc1_bias_grad,
        whole_columns(fc2_grad),
        out_bias_grad,
    )


def solution(mesh):
    placed = (
        P("fsdp", "ctx", None),
        P("fsdp", None),
        P("fsdp", None),
        P("fsdp"),
        P("fsdp"),
        P("fsdp", None, "tp"),
        P(None, "tp"),
        P("fsdp", "tp"),
        P("fsdp"),
        P("fsdp", "tp"),
        P("tp"),
        P("fsdp", "tp"),
        P("fsdp"),
        P("fsdp", "ctx", None),
    )
    return jax.shard_map(
        per_device,
        mesh=mesh,
        in_specs=placed,
        out_specs=(
            P("fsdp", "ctx", None),
            P("fsdp", "ctx", None),
            P("fsdp"),
            P("fsdp"),
            P("fsdp", None, "tp"),
            P(None, "tp"),
            P("fsdp", "tp"),
            P("fsdp"),
            P("fsdp", "tp"),
            P("tp"),
            P("fsdp", "tp"),
            P("fsdp"),
        ),
        check_vma=False,
    )
```

```python
import math

import jax
import jax.numpy as jnp
from jax import lax
from jax.experimental import pallas as pl
from jax.experimental.pallas import tpu as pltpu
from jax.sharding import PartitionSpec as P

HD = 256
ROT = 64


NORM_EPSILON = 1e-05
MASK_FLOOR = -1000000000.0
F32 = jnp.float32
BF16 = jnp.bfloat16
LANES = 128
RELAY = {"attention": True, "fc1": True, "fc2": False}


def rotation_tables(position):
    half = ROT // 2
    frequency = jnp.exp(jnp.arange(half, dtype=F32) * (-2.0 * math.log(10000.0) / ROT))
    angles = position.astype(F32)[:, None] * frequency[None, :]
    cosine, sine = jnp.cos(angles), jnp.sin(angles)
    rest = (position.shape[0], LANES - ROT)
    return (
        jnp.concatenate([cosine, cosine, jnp.ones(rest, F32)], axis=1),
        jnp.concatenate([-sine, sine, jnp.zeros(rest, F32)], axis=1),
    )


def packed_rows(order_row, slots, block_rows):
    selector = slots[:, None] == jnp.arange(order_row.shape[0], dtype=jnp.int32)[None, :]
    source_block = jnp.sum(jnp.where(selector, order_row[None, :], 0), axis=1, dtype=jnp.int32)
    within = jnp.arange(block_rows, dtype=jnp.int32)
    return (source_block[:, None] * block_rows + within[None, :]).reshape(-1)


def place_rows(packed_at, lengths_row):
    seq_ends = jnp.cumsum(lengths_row, dtype=jnp.int32)
    passed = packed_at[:, None] >= seq_ends[None, :]
    segment = jnp.sum(passed.astype(jnp.int32), axis=1, dtype=jnp.int32)
    before = jnp.sum(jnp.where(passed, lengths_row[None, :], 0), axis=1, dtype=jnp.int32)
    return (segment, packed_at - before)


def dot(a, b, contract):
    return lax.dot_general(a, b, (contract, ((), ())), preferred_element_type=F32)


def fsdp_permute(x, bits):
    size, lanes = lax.axis_size("fsdp"), lax.axis_size("ctx")
    perm = [
        (f * lanes + x, (f ^ bits[x % 2]) * lanes + x) for f in range(size) for x in range(lanes)
    ]
    return lax.ppermute(x, ("fsdp", "ctx"), perm)


def swap(x, bit):
    return fsdp_permute(x, (bit, bit))


def ctx_pair(x):
    return lax.ppermute(x, "ctx", [(0, 1), (1, 0)])


def ctx_terms(x):
    if lax.axis_size("ctx") == 2:
        return x, ctx_pair(x)
    return lax.psum(x.astype(F32), "ctx"), jnp.zeros_like(x)


def tp_pair(x, bit):
    return lax.ppermute(x, "tp", [(i, i ^ bit) for i in range(lax.axis_size("tp"))])


def half_of(x, which, axis):
    size = x.shape[axis] // 2
    return lax.dynamic_slice_in_dim(x, which * size, size, axis=axis)


def kernel_call(body, scalars, arrays, in_specs, out_shape, out_specs, grid, name, flops=0, scratch=()):
    outs = out_shape if isinstance(out_shape, (tuple, list)) else (out_shape,)
    size = sum(a.size * a.dtype.itemsize for a in (*arrays, *outs))
    return pl.pallas_call(
        body,
        out_shape=out_shape,
        grid_spec=pltpu.PrefetchScalarGridSpec(
            num_scalar_prefetch=1,
            grid=grid,
            in_specs=in_specs,
            out_specs=out_specs,
            scratch_shapes=scratch,
        ),
        cost_estimate=pl.CostEstimate(flops=flops, transcendentals=0, bytes_accessed=size),
        name=name,
    )(scalars, *arrays)


def aligned(index, size):
    return pl.ds(pl.multiple_of(index * size, size), size)


def frame_rows(own, other, order, norm=None):
    rows, columns = own.shape
    width, step = columns // 4, rows // 2

    def kernel(order_ref, own_ref, other_ref, *refs):
        gain_ref, bias_ref, out_ref, wide_ref = refs if norm else (None, None, refs[0], None)
        for s, ref in enumerate((own_ref, other_ref)):
            if norm:
                x = ref[...].astype(F32)
                x = x - jnp.mean(x, axis=1, keepdims=True)
                variance = jnp.mean(x * x, axis=1, keepdims=True)
                wide_ref[...] = x * lax.rsqrt(variance + NORM_EPSILON)
            for k in range(4):
                to = slice(k * width, (k + 1) * width)
                at = aligned(order_ref[k], width)
                if norm:
                    out_ref[s, :, to] = (
                        wide_ref[:, at] * gain_ref[:, to] + bias_ref[:, to]
                    ).astype(BF16)
                else:
                    out_ref[s, :, to] = ref[:, at]

    row_spec = pl.BlockSpec((step, columns), lambda r, o: (r, 0))
    vector_spec = pl.BlockSpec((1, columns), lambda r, o: (0, 0))
    out = kernel_call(
        kernel,
        order,
        (own, other, *(norm or ())),
        [row_spec, row_spec] + ([vector_spec, vector_spec] if norm else []),
        jax.ShapeDtypeStruct((2, rows, columns), BF16),
        pl.BlockSpec((2, step, columns), lambda r, o: (0, r, 0)),
        (2,),
        "norm_rows" if norm else "frame_rows",
        scratch=[pltpu.VMEM((step, columns), F32)] if norm else (),
    )
    return out.reshape(2 * rows, columns)


def place_grad(parts, core, attention):
    rows, columns = parts[0].shape
    step = rows // 2

    def kernel(core_ref, a_ref, ax_ref, b_ref, bx_ref, *out_refs):
        for h, (u_ref, ux_ref) in enumerate(((a_ref, ax_ref), (b_ref, bx_ref))):
            total = u_ref[...].astype(F32) + ux_ref[...].astype(F32)
            place = core_ref[0] ^ h
            if attention:
                for t in range(3):
                    out_refs[0][t, :, aligned(place, HD)] = total[:, t * HD : (t + 1) * HD]
                out_refs[1][:, aligned(place, HD)] = total[:, 3 * HD :]
            else:
                out_refs[0][:, aligned(place, columns)] = total

    shapes = [(rows, 2 * columns)]
    specs = [pl.BlockSpec((step, 2 * columns), lambda r, c: (r, 0))]
    if attention:
        shapes = [(3, rows, 2 * HD), (rows, 2 * HD)]
        specs = [
            pl.BlockSpec((3, step, 2 * HD), lambda r, c: (0, r, 0)),
            pl.BlockSpec((step, 2 * HD), lambda r, c: (r, 0)),
        ]
    return kernel_call(
        kernel,
        core[None],
        parts,
        [pl.BlockSpec((step, columns), lambda r, c: (r, 0))] * 4,
        [jax.ShapeDtypeStruct(shape, F32) for shape in shapes],
        specs,
        (2,),
        "place_grad",
    )


def share_rows(first, second, rows, theirs=None):
    width = first[1][0].shape[0]
    at = 1 if theirs is None else 0

    def kernel(_, f_ref, s_ref, *refs):
        f_refs, s_refs, refs = refs[:4], refs[4:8], refs[8:]
        for n in range(2):

            @pl.when(pl.program_id(0) == n)
            def _(n=n):
                for m in range(2):
                    k = 2 * n + m
                    total = dot(f_ref[...], f_refs[k][...], ((1,), (1,)))
                    total = total + dot(s_ref[...], s_refs[k][...], ((1,), (1,)))
                    if theirs is None:
                        to = slice((1 - m) * width, (2 - m) * width)
                    else:
                        to = slice(m * width, (m + 1) * width)
                        total = total + refs[0][:, to].astype(F32)
                    refs[-1][:, to] = total.astype(BF16)

    arrays, in_specs, flops = [], [], 0
    for acts, _, _, size in (first, second):
        arrays.append(acts)
        in_specs.append(pl.BlockSpec((rows, size), lambda n, b: (at, 0)))
        flops += 2 * rows * 4 * width * size
    for _, pieces, block, size in (first, second):
        arrays += pieces
        in_specs += [pl.BlockSpec((width, size), lambda n, b, block=block: (0, block))] * 4
    out_spec = pl.BlockSpec((rows, 2 * width), lambda n, b: (0, n))
    if theirs is not None:
        arrays.append(theirs)
        in_specs.append(out_spec)
    return kernel_call(
        kernel,
        jnp.zeros((1,), jnp.int32),
        arrays,
        in_specs,
        jax.ShapeDtypeStruct((rows, 4 * width), BF16),
        out_spec,
        (2,),
        "share_rows",
        flops=flops,
    )


def finish_output(order, row_block, kept, got, inputs, out_bias):
    rows, columns = kept.shape
    width = columns // 4

    def kernel(s_ref, kept_ref, got_ref, x_ref, bias_ref, out_ref):
        for k in range(4):
            cols, at = slice(k * width, (k + 1) * width), aligned(s_ref[k], width)
            total = kept_ref[:, cols] + got_ref[:, cols].astype(F32)
            out_ref[:, at] = (x_ref[:, at].astype(F32) + total + bias_ref[:, cols]).astype(BF16)

    spec = pl.BlockSpec((rows, columns), lambda i, s: (0, 0))
    return kernel_call(
        kernel,
        jnp.concatenate([order, row_block[None]]),
        (kept, got, inputs, out_bias),
        [
            spec,
            spec,
            pl.BlockSpec((rows, columns), lambda i, s: (s[4], 0)),
            pl.BlockSpec((1, columns), lambda i, s: (0, 0)),
        ],
        jax.ShapeDtypeStruct((rows, columns), BF16),
        spec,
        (1,),
        "finish_output",
    )


def finish_input_grad(order, row_block, kept, got, inputs, upstream, norm_gain):
    rows, columns = kept.shape
    width = columns // 4

    def kernel(s_ref, kept_ref, got_ref, x_ref, dy_ref, gain_ref, out_ref, std_ref):
        x = x_ref[...].astype(F32)
        x = x - jnp.mean(x, axis=1, keepdims=True)
        inverse = lax.rsqrt(jnp.mean(x * x, axis=1, keepdims=True) + NORM_EPSILON)
        std_ref[...] = x * inverse
        mean_scaled = jnp.zeros((rows, 1), F32)
        mean_product = jnp.zeros((rows, 1), F32)

        def parts(k):
            cols, at = slice(k * width, (k + 1) * width), aligned(s_ref[k], width)
            total = kept_ref[:, cols] + got_ref[:, cols].astype(F32)
            return at, total * gain_ref[:, cols], std_ref[:, at]

        for k in range(4):
            _, scaled, standard = parts(k)
            mean_scaled += jnp.sum(scaled, axis=1, keepdims=True) / columns
            mean_product += jnp.sum(scaled * standard, axis=1, keepdims=True) / columns
        for k in range(4):
            at, scaled, standard = parts(k)
            change = inverse * (scaled - mean_scaled - standard * mean_product)
            out_ref[:, at] = (dy_ref[:, at].astype(F32) + change).astype(BF16)

    spec = pl.BlockSpec((rows, columns), lambda i, s: (0, 0))
    rows_spec = pl.BlockSpec((rows, columns), lambda i, s: (s[4], 0))
    return kernel_call(
        kernel,
        jnp.concatenate([order, row_block[None]]),
        (kept, got, inputs, upstream, norm_gain),
        [spec, spec, rows_spec, rows_spec, pl.BlockSpec((1, columns), lambda i, s: (0, 0))],
        jax.ShapeDtypeStruct((rows, columns), BF16),
        spec,
        (1,),
        "finish_input_grad",
        scratch=[pltpu.VMEM((rows, columns), F32)],
    )


def norm_grads(order, inputs, share):
    rows, columns = inputs.shape
    width, step = columns // 4, rows // 2

    def kernel(order_ref, x_ref, share_ref, out_ref, std_ref):
        @pl.when(pl.program_id(0) == 0)
        def _():
            out_ref[...] = jnp.zeros_like(out_ref)

        x = x_ref[...].astype(F32)
        x = x - jnp.mean(x, axis=1, keepdims=True)
        std_ref[...] = x * lax.rsqrt(jnp.mean(x * x, axis=1, keepdims=True) + NORM_EPSILON)
        for k in range(4):
            cols = slice(k * width, (k + 1) * width)
            part = share_ref[:, cols].astype(F32)
            product = part * std_ref[:, aligned(order_ref[k], width)]
            out_ref[0:1, cols] += jnp.sum(product, axis=0, keepdims=True)
            out_ref[1:2, cols] += jnp.sum(part, axis=0, keepdims=True)

    row_spec = pl.BlockSpec((step, columns), lambda r, o: (r, 0))
    return kernel_call(
        kernel,
        order,
        (inputs, share),
        [row_spec, row_spec],
        jax.ShapeDtypeStruct((2, columns), F32),
        pl.BlockSpec((2, columns), lambda r, o: (0, 0)),
        (2,),
        "norm_grads",
        scratch=[pltpu.VMEM((step, columns), F32)],
    )


def gather_rows(pieces, places, dtype):
    size, (rows, columns) = len(pieces), pieces[0].shape

    def kernel(place_ref, *refs):
        for n in range(size):
            refs[-1][aligned(place_ref[n], rows), :] = refs[n][...].astype(dtype)

    return kernel_call(
        kernel,
        places,
        pieces,
        [pl.BlockSpec((rows, columns // 2), lambda c, p: (0, c))] * size,
        jax.ShapeDtypeStruct((rows * size, columns), dtype),
        pl.BlockSpec((rows * size, columns // 2), lambda c, p: (0, c)),
        (2,),
        "gather_rows",
    )


def turned(x, cosine, sine):
    lane = lax.broadcasted_iota(jnp.int32, x.shape, 1)
    half = ROT // 2
    partner = jnp.where(
        lane < half, pltpu.roll(x, x.shape[1] - half, axis=1), pltpu.roll(x, half, axis=1)
    )
    return x * cosine + partner * sine


def project(normed, pieces, bias, cosine, sine):
    rows = normed.shape[0] // 2
    width = pieces[0].shape[0]

    def kernel(_, x_ref, *refs):
        piece_refs, (bias_ref, cos_ref, sin_ref, q_ref, kv_ref) = refs[:4], refs[4:]
        total = dot(x_ref[:, :width], piece_refs[0][...], ((1,), (0,)))
        for k in range(1, 4):
            cols = slice(k * width, (k + 1) * width)
            total = total + dot(x_ref[:, cols], piece_refs[k][...], ((1,), (0,)))
        total = total + bias_ref[...]
        cosine, sine = cos_ref[...], sin_ref[...]
        for n, ref in enumerate((q_ref, kv_ref)):
            head = total[:, n * HD : (n + 1) * HD]
            ref[:, :LANES] = turned(head[:, :LANES], cosine, sine).astype(BF16)
            ref[:, LANES:HD] = head[:, LANES:].astype(BF16)
        kv_ref[:, HD:] = total[:, 2 * HD :].astype(BF16)

    def by_row(columns):
        return pl.BlockSpec((rows, columns), lambda s, z: (s, 0))

    return kernel_call(
        kernel,
        jnp.zeros((1,), jnp.int32),
        (normed, *pieces, bias, cosine, sine),
        [by_row(normed.shape[1])]
        + [pl.BlockSpec((width, 3 * HD), lambda s, z: (0, 0))] * 4
        + [pl.BlockSpec((1, 3 * HD), lambda s, z: (0, 0)), by_row(LANES), by_row(LANES)],
        [
            jax.ShapeDtypeStruct((2 * rows, HD), BF16),
            jax.ShapeDtypeStruct((2 * rows, 2 * HD), BF16),
        ],
        [by_row(HD), by_row(2 * HD)],
        (2,),
        "project",
        flops=2 * 2 * rows * normed.shape[1] * 3 * HD,
    )


def turn_back(query_grad, kept, got, cosine, sine):
    rows = kept.shape[1]

    def kernel(_, q_ref, kept_ref, got_ref, cos_ref, sin_ref, out_ref):
        both = kept_ref[...] + got_ref[...].astype(F32)
        cosine, sine = cos_ref[...], -sin_ref[...]
        for n, head in enumerate((q_ref[...], both[:, :HD])):
            at = n * HD
            out_ref[:, at : at + LANES] = turned(head[:, :LANES], cosine, sine).astype(BF16)
            out_ref[:, at + LANES : at + HD] = head[:, LANES:].astype(BF16)
        out_ref[:, 2 * HD :] = both[:, HD:].astype(BF16)

    def by_row(columns):
        return pl.BlockSpec((rows, columns), lambda s, z: (s, 0))

    both_spec = pl.BlockSpec((None, rows, 2 * HD), lambda s, z: (s, 0, 0))
    return kernel_call(
        kernel,
        jnp.zeros((1,), jnp.int32),
        (query_grad, kept, got, cosine, sine),
        [by_row(HD), both_spec, both_spec, by_row(LANES), by_row(LANES)],
        jax.ShapeDtypeStruct((2 * rows, 3 * HD), BF16),
        by_row(3 * HD),
        (2,),
        "turn_back",
    )


def attended_grads(upstream, pieces, valid):
    rows = upstream.shape[0] // 2
    width = pieces[0].shape[0]

    def kernel(_, dy_ref, *refs):
        piece_refs, (valid_ref, out_ref) = refs[:4], refs[4:]
        total = dot(dy_ref[:, :width], piece_refs[0][...], ((1,), (0,)))
        for k in range(1, 4):
            cols = slice(k * width, (k + 1) * width)
            total = total + dot(dy_ref[:, cols], piece_refs[k][...], ((1,), (0,)))
        out_ref[...] = total.astype(BF16) * valid_ref[...].astype(BF16)

    def by_row(columns):
        return pl.BlockSpec((rows, columns), lambda s, z: (s, 0))

    return kernel_call(
        kernel,
        jnp.zeros((1,), jnp.int32),
        (upstream, *pieces, valid),
        [by_row(upstream.shape[1])]
        + [pl.BlockSpec((width, HD), lambda s, z: (0, 3))] * 4
        + [by_row(1)],
        jax.ShapeDtypeStruct((2 * rows, HD), BF16),
        by_row(HD),
        (2,),
        "attended_grads",
        flops=2 * 2 * rows * upstream.shape[1] * HD,
    )


def pack_attention(qkv_weight, dense_weight, halves):
    rows = qkv_weight.shape[1]
    count = halves.shape[0]

    def kernel(h_ref, qkv_ref, dense_ref, *out_refs):
        for n in range(count):
            for t in range(3):
                out_refs[n][:, t * HD : (t + 1) * HD] = qkv_ref[t, :, aligned(h_ref[n], HD)]
            out_refs[n][:, 3 * HD :] = dense_ref[:, aligned(h_ref[n], HD)]

    def spec(columns):
        return pl.BlockSpec((rows // 2, columns), lambda r, h: (r, 0))

    return kernel_call(
        kernel,
        halves,
        (qkv_weight, dense_weight),
        [pl.BlockSpec((3, rows // 2, 2 * HD), lambda r, h: (0, r, 0)), spec(2 * HD)],
        [jax.ShapeDtypeStruct((rows, 4 * HD), BF16)] * count,
        [spec(4 * HD)] * count,
        (2,),
        "pack_attention",
    )


class Rounds:
    def __init__(self):
        self.last = ()

    def __call__(self, *arrays):
        got = lax.optimization_barrier((*arrays, *self.last))[: len(arrays)]
        return got if len(arrays) > 1 else got[0]

    def done(self, *arrays):
        self.last = arrays
        return arrays if len(arrays) > 1 else arrays[0]

    def close(self, *arrays):
        self.last = (*self.last, *arrays)


def per_device(
    tokens,
    lengths,
    block_order,
    ln_gain,
    ln_bias,
    qkv_weight,
    qkv_bias,
    dense_weight,
    dense_bias,
    fc1_weight,
    fc1_bias,
    fc2_weight,
    fc2_bias,
    cotangent,
):
    me = lax.axis_index("fsdp")
    core = me % 2
    tp_index = lax.axis_index("tp").astype(jnp.int32)
    tp_size = lax.axis_size("tp")
    ctx_index = lax.axis_index("ctx")
    ctx_size = lax.axis_size("ctx")
    pairs = ctx_size == 2
    side = ctx_index % 2 if pairs else 0 * ctx_index
    shard = ln_gain.shape[0]
    row_count = tokens.shape[1]
    block_rows = row_count // 2
    score_scale = 1.0 / math.sqrt(HD)
    order = jnp.stack([me, me ^ 1, me ^ (2 + side), me ^ (3 - side)]).astype(jnp.int32)
    near_bits, far_bits = ((2, 3), (3, 2)) if pairs else ((2, 2), (3, 3))
    inputs_low, upstream_low = tokens[0], cotangent[0]
    then = Rounds()

    halves = jnp.stack([core, 1 - core, core ^ side, core ^ 1 ^ side]).astype(jnp.int32)

    def relayed(name):
        return RELAY[name] and pairs

    def four(weight, name):
        return [half_of(weight, halves[n], 1) for n in range(3 if relayed(name) else 4)]

    def far_of(name, near, packs):
        return ctx_pair(near) if relayed(name) else fsdp_permute(then(packs[3]), far_bits)

    def joined(pieces):
        return jnp.concatenate(pieces, axis=0)

    seq_count, slots = lengths.shape[1], block_order.shape[1]
    vectors = jnp.concatenate(
        [
            v.astype(F32)
            for v in (ln_gain, ln_bias, dense_bias, fc2_bias, lengths[0], block_order[0])
        ]
    )
    then.done(vectors)
    vectors = [
        vectors,
        swap(vectors, 1),
        fsdp_permute(vectors, near_bits),
        fsdp_permute(vectors, far_bits),
    ]
    inputs_other = swap(inputs_low, 1)
    fc1_packs = four(then(fc1_weight), "fc1")
    then.done(*fc1_packs)
    fc1_near = fsdp_permute(fc1_packs[2], near_bits)
    packs = pack_attention(
        qkv_weight.transpose(1, 0, 2), then(dense_weight), halves[: 3 if relayed("attention") else 4]
    )
    then.done(*packs)
    then.close(inputs_other, *vectors[1:])

    def over_features(n):
        return jnp.concatenate([v[n * shard : (n + 1) * shard] for v in vectors])[None, :]

    norm_gain, norm_bias = over_features(0), over_features(1)
    out_bias = over_features(2) + over_features(3)
    their_layout = vectors[1][4 * shard :].astype(jnp.int32)

    upstream_other = swap(then(upstream_low), 1)
    fc1_core, attention_core = swap(then(fc1_packs[1]), 1), swap(then(packs[1]), 1)
    normed = then.done(frame_rows(inputs_low, then(inputs_other), order, (norm_gain, norm_bias)))
    fc2_packs = four(then(fc2_weight), "fc2")
    then.done(*fc2_packs)
    layouts = [
        (then(lengths[0]), block_order[0]),
        (their_layout[:seq_count], their_layout[seq_count:]),
    ]
    local_slots = ctx_index * 2 + jnp.arange(2, dtype=jnp.int32)
    if pairs:
        key_slots = jnp.concatenate([local_slots, (1 - ctx_index) * 2 + jnp.arange(2)])
    else:
        key_slots = jnp.arange(slots, dtype=jnp.int32)
    allowed, valid, positions = [], [], []
    for lengths_row, order_row in layouts:
        local_packed = packed_rows(order_row, local_slots, block_rows)
        key_packed = packed_rows(order_row, key_slots, block_rows)
        segment, position = place_rows(local_packed, lengths_row)
        key_segment = place_rows(key_packed, lengths_row)[0]
        allowed.append(
            (segment[:, None] == key_segment[None, :])
            & (key_packed[None, :] <= local_packed[:, None])
        )
        valid.append((segment < seq_count).astype(F32)[:, None])
        positions.append(position)
    cosine_table, sine_table = rotation_tables(jnp.concatenate(positions))
    valid = jnp.concatenate(valid)
    upstream_sum = jnp.sum(upstream_low.astype(F32), axis=0, keepdims=True)
    then.done(cosine_table, sine_table, valid, upstream_sum, *fc2_packs)
    then.close(upstream_other, fc1_core, attention_core, fc1_near)

    attention_near = fsdp_permute(then(packs[2]), near_bits)
    fc1_far = far_of("fc1", then(fc1_near), fc1_packs)
    fc2_core = swap(then(fc2_packs[1]), 1)
    upstream = then.done(frame_rows(upstream_low, then(upstream_other), order))
    fc1_pieces = [fc1_packs[0], fc1_core, fc1_near, fc1_far]
    then.close(attention_near, fc1_far, fc2_core)

    def grad_block(k, *products, kind=BF16):
        parts = []
        for left, right in products:
            rows = lax.dynamic_slice_in_dim(left, k * shard, shard, axis=1)
            parts.append(dot(rows, right, ((0,), (0,))).astype(kind))
        return jnp.concatenate(parts, axis=1)

    def grad_blocks(*products):
        far = grad_block(2 + side, *products)
        rest = [grad_block(k, *products) for k in (3 - side, 1)]
        return (far, *rest, grad_block(0, *products, kind=F32))

    def add_mine(own, far):
        return then.done((own + then(far).astype(F32)).astype(BF16))

    def add_theirs(near, farther):
        return then.done((near.astype(F32) + then(farther).astype(F32)).astype(BF16))

    def placed(mine, theirs, attention=False):
        parts = then(*mine, *theirs)
        return then.done(*place_grad(parts, core, attention))

    fc2_near = fsdp_permute(then(fc2_packs[2]), near_bits)
    attention_far = far_of("attention", then(attention_near), packs)
    attention = [packs[0], attention_core, attention_near, attention_far]
    pre_act = dot(then(normed), joined(fc1_pieces), ((1,), (0,)))
    pre_act = pre_act + half_of(fc1_bias, core, 0).astype(F32)[None, :]
    normal_cdf = 0.5 * (1.0 + lax.erf(pre_act * (1.0 / math.sqrt(2.0))))
    density = jnp.exp(-0.5 * pre_act * pre_act) * (1.0 / math.sqrt(2.0 * math.pi))
    hidden = (pre_act * normal_cdf).astype(BF16)
    slope = normal_cdf + pre_act * density
    hidden, slope = then.done(hidden, slope)
    fc2_blocks = then.done(*grad_blocks((then(upstream), hidden)))
    then.close(fc2_near, attention_far)

    fc2_far = far_of("fc2", then(fc2_near), fc2_packs)
    fc2_pieces = [fc2_packs[0], fc2_core, fc2_near, fc2_far]
    fc2_grad_near = swap(then(fc2_blocks[2]), 1)
    qkv_bias_own = half_of(qkv_bias, core, 1).astype(F32).reshape(1, 3 * HD)
    queries, both_local = then.done(
        *project(then(normed), attention, qkv_bias_own, cosine_table, sine_table)
    )
    both_local = both_local.reshape(2, row_count, 2 * HD)
    if pairs:
        both_other = ctx_pair(both_local)
    else:
        both_other = lax.all_gather(both_local, "ctx", axis=1, tiled=True)
    attended_grad = then.done(attended_grads(then(upstream), attention, valid))
    then.close(both_other, fc2_far, fc2_grad_near)
    both_all = then(both_other)
    if pairs:
        both_all = jnp.concatenate([both_local, both_all], axis=1)

    fc2_grad_far = swap(then(fc2_blocks[0]), 2)
    attended, probs_all = [], []
    for s in range(2):
        rows = slice(s * row_count, (s + 1) * row_count)
        keys, values = both_all[s, :, :HD], both_all[s, :, HD:]
        scores = dot(queries[rows], keys, ((1,), (1,))) * score_scale
        scores = jnp.where(allowed[s], scores, MASK_FLOOR)
        exp_scores = jnp.exp(scores - jnp.max(scores, axis=1, keepdims=True))
        probs = exp_scores / jnp.sum(exp_scores, axis=1, keepdims=True)
        probs_all.append(probs)
        attended.append(dot(probs.astype(BF16), values, ((1,), (0,))))
    attended = then.done((jnp.concatenate(attended) * valid).astype(BF16))
    hidden_size = hidden.shape[1]
    second = (hidden, fc2_pieces, 0, hidden_size)
    theirs = then.done(share_rows((attended, attention, 3, HD), second, row_count))
    hidden_grad = dot(then(upstream), joined(fc2_pieces), ((1,), (0,)))
    pre_grad = then.done((hidden_grad * slope).astype(BF16))
    then.close(fc2_grad_far, theirs)

    def attention_grads(s):
        rows = slice(s * row_count, (s + 1) * row_count)
        keys, values = both_all[s, :, :HD], both_all[s, :, HD:]
        probs, head_grad = probs_all[s], then(attended_grad[rows])
        prob_grad = dot(head_grad, values, ((1,), (1,)))
        row_delta = jnp.sum(probs * prob_grad, axis=1, keepdims=True)
        score_grad = (probs * (prob_grad - row_delta)).astype(BF16)
        query_piece = dot(score_grad, keys, ((1,), (0,))) * score_scale
        key_piece = dot(score_grad, queries[rows], ((0,), (0,))) * score_scale
        value_piece = dot(probs.astype(BF16), head_grad, ((0,), (0,)))
        return then.done(query_piece, jnp.concatenate([key_piece, value_piece], axis=1))

    low = tp_index % 2

    def halves(total, digit):
        return then.done(
            half_of(total, 1 - digit, 0).astype(BF16), half_of(total, digit, 0).astype(F32)
        )

    def halve_on(kept, got, bit, row_block):
        while bit < tp_size:
            total, digit = kept + got.astype(F32), (tp_index // bit) % 2
            given, kept = halves(total, digit)
            got, row_block, bit = tp_pair(given, bit), row_block * 2 + digit, bit * 2
        return kept, got, row_block

    def double_up(part):
        pieces, flips, bit = [part], [0], tp_size // 2
        while bit > 1:
            pieces += [tp_pair(p, bit) for p in pieces]
            flips += [f ^ bit for f in flips]
            bit //= 2
        return pieces, flips + [f ^ 1 for f in flips]

    fc2_grad_farther = swap(then(fc2_blocks[1]), 3)
    theirs = swap(then(theirs), 1)
    fc2_mine = ctx_terms(add_mine(fc2_blocks[3], fc2_grad_far))
    grads_first = attention_grads(0)
    first = (then(attended), attention, 3, HD)
    shared = then.done(share_rows(first, second, row_count, theirs))
    given, kept = halves(shared, low)
    fc1_far_block = then.done(grad_block(2 + side, (then(normed), pre_grad)))
    then.close(fc2_grad_farther)

    fc1_grad_far = swap(then(fc1_far_block), 2)
    out_got = tp_pair(then(given), 1)
    grads_second = attention_grads(1)
    both_grad = jnp.stack([grads_first[1], grads_second[1]])
    query_grad = jnp.concatenate([grads_first[0], grads_second[0]])
    if pairs:
        both_given = both_grad[:, row_count:].astype(BF16)
        both_grad = both_grad[:, :row_count]
    else:
        both_given = jnp.zeros((2, row_count, 2 * HD), BF16)
        both_grad = lax.psum_scatter(both_grad, "ctx", scatter_dimension=1, tiled=True)
    both_given, both_grad, query_grad = then.done(both_given, both_grad, query_grad)
    both_got = ctx_pair(both_given) if pairs else both_given
    fc1_near_block = then.done(grad_block(1, (then(normed), pre_grad)))
    fc1_grad_near = swap(fc1_near_block, 1)
    fc1_rest = then.done(
        grad_block(3 - side, (then(normed), pre_grad)),
        grad_block(0, (then(normed), pre_grad), kind=F32),
    )
    then.close(fc1_grad_far, out_got, fc2_mine[1], fc1_grad_near)

    fc1_grad_farther = swap(then(fc1_rest[0]), 3)
    out_kept, out_got, out_block = halve_on(then(kept), out_got, 2, low)
    fc2_theirs = ctx_terms(add_theirs(fc2_grad_near, fc2_grad_farther))
    proj_grad = then.done(
        turn_back(then(query_grad), both_grad, both_got, cosine_table, sine_table)
    )
    second = (pre_grad, fc1_pieces, 0, hidden_size)
    theirs = then.done(share_rows((proj_grad, attention, 0, 3 * HD), second, row_count))
    products = (proj_grad, attended)

    def attention_block(k, kind=BF16):
        return grad_block(k, (then(normed), products[0]), (upstream, products[1]), kind=kind)

    far_block = then.done(attention_block(2 + side))
    then.close(fc1_grad_farther, out_got)

    attention_grad_far = swap(then(far_block), 2)
    theirs = swap(then(theirs), 1)
    out_part = then.done(
        finish_output(order, out_block, then(out_kept), out_got, inputs_low, out_bias)
    )
    out_pieces, flips = double_up(out_part)
    out_late = [tp_pair(out_part, 1)]
    near_block = then.done(attention_block(1))
    first = (then(proj_grad), attention, 0, 3 * HD)
    shared = then.done(share_rows(first, second, row_count, theirs))
    attention_grad_near = swap(near_block, 1)
    given, kept = halves(shared, low)
    fc1_mine = then.done((then(fc1_rest[1], fc2_theirs[1])[0] + fc1_grad_far).astype(BF16))
    fc1_mine = ctx_terms(fc1_mine)
    farther_block = then.done(attention_block(3 - side))
    then.close(attention_grad_far, out_late[0], *out_pieces[1:], attention_grad_near)

    attention_grad_farther = swap(then(farther_block), 3)
    got = tp_pair(then(given), 1)
    norm_sums = then.done(norm_grads(order, then(inputs_low), shared))
    own_block = then.done(attention_block(0, kind=F32))
    column_sums = then.done(
        jnp.concatenate(
            [jnp.sum(then(pre_grad).astype(F32), axis=0), jnp.sum(proj_grad.astype(F32), axis=0)]
        )
    )
    fc1_theirs = add_theirs(fc1_grad_near, fc1_grad_farther)
    fc1_theirs = ctx_terms(then(fc1_theirs, fc1_mine[1])[0])
    then.close(attention_grad_farther, got)

    kept, got, row_block = halve_on(then(kept), got, 2, low)
    out_late += [tp_pair(p, 1) for p in out_pieces[1:]]
    norm_sums = then(norm_sums)
    norm_sums = norm_sums + tp_pair(norm_sums, 1)
    fc2_out = placed(fc2_mine, fc2_theirs)
    attention_mine = add_mine(own_block, attention_grad_far)
    attention_mine = ctx_terms(then(attention_mine, fc1_theirs[1])[0])
    then.close(got, norm_sums)

    input_part = then.done(
        finish_input_grad(order, row_block, then(kept), got, inputs_low, upstream_low, norm_gain)
    )
    pieces, _ = double_up(input_part)
    late = [tp_pair(input_part, 1)]
    bit = 2
    while bit < tp_size:
        norm_sums = norm_sums + tp_pair(then(norm_sums), bit)
        bit *= 2
    vector_sums = jnp.concatenate([norm_sums[:, k * shard : (k + 1) * shard] for k in range(4)])

    def sums_of(k):
        return [
            lax.dynamic_slice_in_dim(vector_sums, 2 * k, 2, axis=0).reshape(-1),
            lax.dynamic_slice_in_dim(upstream_sum[0], order[k] * shard, shard),
        ]

    sums_kept = jnp.concatenate([*sums_of(0), *sums_of(1), column_sums])
    sums_given = jnp.concatenate([*sums_of(2 + side), *sums_of(3 - side), column_sums])
    sums_kept = sums_kept + swap(sums_given, 2)
    fc1_out = placed(fc1_mine, fc1_theirs)
    attention_theirs = add_theirs(attention_grad_near, attention_grad_farther)
    attention_theirs = ctx_terms(then(attention_theirs, attention_mine[1])[0])
    then.close(*pieces[1:], late[0], sums_kept)

    late += [tp_pair(p, 1) for p in then(*pieces, *out_late)[1 : len(pieces)]]
    sums_kept = sum(ctx_terms(then(sums_kept)))
    other_core = swap(sums_kept[3 * shard :], 1)
    vector_sums = (sums_kept[: 3 * shard] + other_core[: 3 * shard]).reshape(3, shard)
    column_sums, column_other = sums_kept[6 * shard :], other_core[3 * shard :]

    def row_block_of(index):
        place, bit = 0 * index, 1
        while bit < tp_size:
            place = place * 2 + (index // bit) % 2
            bit *= 2
        return place

    places = jnp.stack([row_block_of(tp_index ^ f) for f in flips]).astype(jnp.int32)
    output = then.done(gather_rows(then(*out_pieces, *out_late), places, BF16))
    input_grad = then.done(gather_rows(then(*pieces, *late), places, F32))
    qkv_out, dense_out = placed(attention_mine, attention_theirs, True)

    def in_order(mine, other, axis):
        return jnp.where(
            core == 0,
            jnp.concatenate([mine, other], axis=axis),
            jnp.concatenate([other, mine], axis=axis),
        )

    hidden_half = fc1_bias.shape[0] // 2
    fc1_bias_grad = in_order(column_sums[:hidden_half], column_other[:hidden_half], 0)
    qkv_bias_grad = in_order(
        column_sums[hidden_half:].reshape(3, HD), column_other[hidden_half:].reshape(3, HD), 1
    )
    return (
        output[None],
        input_grad[None],
        vector_sums[0],
        vector_sums[1],
        qkv_out.transpose(1, 0, 2),
        qkv_bias_grad,
        dense_out,
        vector_sums[2],
        fc1_out,
        fc1_bias_grad,
        fc2_out,
        vector_sums[2],
    )


def solution(mesh):
    placed = (
        P("fsdp", "ctx", None),
        P("fsdp", None),
        P("fsdp", None),
        P("fsdp"),
        P("fsdp"),
        P("fsdp", None, "tp"),
        P(None, "tp"),
        P("fsdp", "tp"),
        P("fsdp"),
        P("fsdp", "tp"),
        P("tp"),
        P("fsdp", "tp"),
        P("fsdp"),
        P("fsdp", "ctx", None),
    )
    return jax.shard_map(
        per_device,
        mesh=mesh,
        in_specs=placed,
        out_specs=(
            P("fsdp", "ctx", None),
            P("fsdp", "ctx", None),
            P("fsdp"),
            P("fsdp"),
            P("fsdp", None, "tp"),
            P(None, "tp"),
            P("fsdp", "tp"),
            P("fsdp"),
            P("fsdp", "tp"),
            P("tp"),
            P("fsdp", "tp"),
            P("fsdp"),
        ),
        check_vma=False,
    )
```

```python
import math

import jax
import jax.numpy as jnp
from jax import lax
from jax.experimental import pallas as pl
from jax.experimental.pallas import tpu as pltpu
from jax.sharding import PartitionSpec as P

HD = 256
ROT = 64


NORM_EPSILON = 1e-05
MASK_FLOOR = -1000000000.0
F32 = jnp.float32
BF16 = jnp.bfloat16
LANES = 128
RELAY = {"attention": True, "fc1": True, "fc2": False}


def rotation_tables(position):
    half = ROT // 2
    frequency = jnp.exp(jnp.arange(half, dtype=F32) * (-2.0 * math.log(10000.0) / ROT))
    angles = position.astype(F32)[:, None] * frequency[None, :]
    cosine, sine = jnp.cos(angles), jnp.sin(angles)
    rest = (position.shape[0], LANES - ROT)
    return (
        jnp.concatenate([cosine, cosine, jnp.ones(rest, F32)], axis=1),
        jnp.concatenate([-sine, sine, jnp.zeros(rest, F32)], axis=1),
    )


def packed_rows(order_row, slots, block_rows):
    selector = slots[:, None] == jnp.arange(order_row.shape[0], dtype=jnp.int32)[None, :]
    source_block = jnp.sum(jnp.where(selector, order_row[None, :], 0), axis=1, dtype=jnp.int32)
    within = jnp.arange(block_rows, dtype=jnp.int32)
    return (source_block[:, None] * block_rows + within[None, :]).reshape(-1)


def place_rows(packed_at, lengths_row):
    seq_ends = jnp.cumsum(lengths_row, dtype=jnp.int32)
    passed = packed_at[:, None] >= seq_ends[None, :]
    segment = jnp.sum(passed.astype(jnp.int32), axis=1, dtype=jnp.int32)
    before = jnp.sum(jnp.where(passed, lengths_row[None, :], 0), axis=1, dtype=jnp.int32)
    return (segment, packed_at - before)


def dot(a, b, contract):
    return lax.dot_general(a, b, (contract, ((), ())), preferred_element_type=F32)


def fsdp_permute(x, bits):
    size, lanes = lax.axis_size("fsdp"), lax.axis_size("ctx")
    perm = [
        (f * lanes + x, (f ^ bits[x % 2]) * lanes + x) for f in range(size) for x in range(lanes)
    ]
    return lax.ppermute(x, ("fsdp", "ctx"), perm)


def swap(x, bit):
    return fsdp_permute(x, (bit, bit))


def ctx_pair(x):
    return lax.ppermute(x, "ctx", [(0, 1), (1, 0)])


def ctx_terms(x):
    if lax.axis_size("ctx") == 2:
        return x, ctx_pair(x)
    return lax.psum(x.astype(F32), "ctx"), jnp.zeros_like(x)


def tp_pair(x, bit):
    return lax.ppermute(x, "tp", [(i, i ^ bit) for i in range(lax.axis_size("tp"))])


def half_of(x, which, axis):
    size = x.shape[axis] // 2
    return lax.dynamic_slice_in_dim(x, which * size, size, axis=axis)


def kernel_call(body, scalars, arrays, in_specs, out_shape, out_specs, grid, name, scratch=()):
    return pl.pallas_call(
        body,
        out_shape=out_shape,
        grid_spec=pltpu.PrefetchScalarGridSpec(
            num_scalar_prefetch=1,
            grid=grid,
            in_specs=in_specs,
            out_specs=out_specs,
            scratch_shapes=scratch,
        ),
        cost_estimate=pl.CostEstimate(flops=0, transcendentals=0, bytes_accessed=0),
        name=name,
    )(scalars, *arrays)


def aligned(index, size):
    return pl.ds(pl.multiple_of(index * size, size), size)


def frame_rows(own, other, order, norm=None):
    rows, columns = own.shape
    width, step = columns // 4, rows // 2

    def kernel(order_ref, own_ref, other_ref, *refs):
        gain_ref, bias_ref, out_ref, wide_ref = refs if norm else (None, None, refs[0], None)
        for s, ref in enumerate((own_ref, other_ref)):
            if norm:
                x = ref[...].astype(F32)
                x = x - jnp.mean(x, axis=1, keepdims=True)
                variance = jnp.mean(x * x, axis=1, keepdims=True)
                wide_ref[...] = x * lax.rsqrt(variance + NORM_EPSILON)
            for k in range(4):
                to = slice(k * width, (k + 1) * width)
                at = aligned(order_ref[k], width)
                if norm:
                    out_ref[s, :, to] = (
                        wide_ref[:, at] * gain_ref[:, to] + bias_ref[:, to]
                    ).astype(BF16)
                else:
                    out_ref[s, :, to] = ref[:, at]

    row_spec = pl.BlockSpec((step, columns), lambda r, o: (r, 0))
    vector_spec = pl.BlockSpec((1, columns), lambda r, o: (0, 0))
    out = kernel_call(
        kernel,
        order,
        (own, other, *(norm or ())),
        [row_spec, row_spec] + ([vector_spec, vector_spec] if norm else []),
        jax.ShapeDtypeStruct((2, rows, columns), BF16),
        pl.BlockSpec((2, step, columns), lambda r, o: (0, r, 0)),
        (2,),
        "norm_rows" if norm else "frame_rows",
        scratch=[pltpu.VMEM((step, columns), F32)] if norm else (),
    )
    return out.reshape(2 * rows, columns)


def place_grad(parts, core, attention):
    rows, columns = parts[0].shape
    step = rows // 2

    def kernel(core_ref, a_ref, ax_ref, b_ref, bx_ref, *out_refs):
        for h, (u_ref, ux_ref) in enumerate(((a_ref, ax_ref), (b_ref, bx_ref))):
            total = u_ref[...].astype(F32) + ux_ref[...].astype(F32)
            place = core_ref[0] ^ h
            if attention:
                for t in range(3):
                    out_refs[0][t, :, aligned(place, HD)] = total[:, t * HD : (t + 1) * HD]
                out_refs[1][:, aligned(place, HD)] = total[:, 3 * HD :]
            else:
                out_refs[0][:, aligned(place, columns)] = total

    shapes = [(rows, 2 * columns)]
    specs = [pl.BlockSpec((step, 2 * columns), lambda r, c: (r, 0))]
    if attention:
        shapes = [(3, rows, 2 * HD), (rows, 2 * HD)]
        specs = [
            pl.BlockSpec((3, step, 2 * HD), lambda r, c: (0, r, 0)),
            pl.BlockSpec((step, 2 * HD), lambda r, c: (r, 0)),
        ]
    return kernel_call(
        kernel,
        core[None],
        parts,
        [pl.BlockSpec((step, columns), lambda r, c: (r, 0))] * 4,
        [jax.ShapeDtypeStruct(shape, F32) for shape in shapes],
        specs,
        (2,),
        "place_grad",
    )


def weight_grad(block, shard, products, kind):
    step = shard // 2
    widths = [right.shape[1] for _, right in products]

    def kernel(_, *refs):
        at = 0
        for n, width in enumerate(widths):
            left_ref, right_ref = refs[2 * n : 2 * n + 2]
            total = dot(left_ref[...], right_ref[...], ((0,), (0,)))
            refs[-1][:, at : at + width] = total.astype(kind)
            at += width

    specs = []
    for left, right in products:
        specs.append(pl.BlockSpec((left.shape[0], step), lambda n, k: (0, 2 * k[0] + n)))
        specs.append(pl.BlockSpec(right.shape, lambda n, k: (0, 0)))
    return kernel_call(
        kernel,
        jnp.asarray(block, jnp.int32)[None],
        [a for product in products for a in product],
        specs,
        jax.ShapeDtypeStruct((shard, sum(widths)), kind),
        pl.BlockSpec((step, sum(widths)), lambda n, k: (n, 0)),
        (2,),
        "weight_grad",
    )


def share_rows(first, second, rows, theirs=None, low=None):
    width = first[1][0].shape[0]
    own = theirs is not None
    at = 0 if own else 1
    half = rows // 2

    def kernel(low_ref, f_ref, s_ref, *refs):
        f_refs, s_refs, refs = refs[:4], refs[4:8], refs[8:]
        for n in range(2):

            @pl.when(pl.program_id(0) == n)
            def _(n=n):
                for m in range(2):
                    k = 2 * n + m
                    total = dot(f_ref[...], f_refs[k][...], ((1,), (1,)))
                    total = total + dot(s_ref[...], s_refs[k][...], ((1,), (1,)))
                    if not own:
                        refs[0][:, (1 - m) * width : (2 - m) * width] = total.astype(BF16)
                        continue
                    theirs_ref, given_ref, kept_ref, all_ref = refs
                    to = slice(m * width, (m + 1) * width)
                    all_ref[...] = (total + theirs_ref[:, to].astype(F32)).astype(BF16)
                    given_ref[:, to] = all_ref[aligned(1 - low_ref[0], half), :]
                    kept_ref[:, to] = all_ref[aligned(low_ref[0], half), :]

    arrays, in_specs = [], []
    for acts, _, _, size in (first, second):
        arrays.append(acts)
        in_specs.append(pl.BlockSpec((rows, size), lambda n, b: (at, 0)))
    for _, pieces, block, size in (first, second):
        arrays += pieces
        in_specs += [pl.BlockSpec((width, size), lambda n, b, block=block: (0, block))] * 4
    out_shape = jax.ShapeDtypeStruct((rows, 4 * width), BF16)
    out_spec = pl.BlockSpec((rows, 2 * width), lambda n, b: (0, n))
    scratch = ()
    if own:
        arrays.append(theirs)
        in_specs.append(out_spec)
        out_shape = [jax.ShapeDtypeStruct((half, 4 * width), BF16)] * 2
        out_spec = [pl.BlockSpec((half, 2 * width), lambda n, b: (0, n))] * 2
        scratch = [pltpu.VMEM((rows, width), BF16)]
    return kernel_call(
        kernel,
        low[None] if own else jnp.zeros((1,), jnp.int32),
        arrays,
        in_specs,
        out_shape,
        out_spec,
        (2,),
        "share_rows",
        scratch=scratch,
    )


def finish_output(order, row_block, kept, got, inputs, out_bias):
    rows, columns = kept.shape
    width = columns // 4

    def kernel(s_ref, kept_ref, got_ref, x_ref, bias_ref, out_ref):
        for k in range(4):
            cols, at = slice(k * width, (k + 1) * width), aligned(s_ref[k], width)
            total = kept_ref[:, cols] + got_ref[:, cols].astype(F32)
            out_ref[:, at] = (x_ref[:, at].astype(F32) + total + bias_ref[:, cols]).astype(BF16)

    spec = pl.BlockSpec((rows, columns), lambda i, s: (0, 0))
    return kernel_call(
        kernel,
        jnp.concatenate([order, row_block[None]]),
        (kept, got, inputs, out_bias),
        [
            spec,
            spec,
            pl.BlockSpec((rows, columns), lambda i, s: (s[4], 0)),
            pl.BlockSpec((1, columns), lambda i, s: (0, 0)),
        ],
        jax.ShapeDtypeStruct((rows, columns), BF16),
        spec,
        (1,),
        "finish_output",
    )


def finish_input_grad(order, row_block, kept, got, inputs, upstream, norm_gain):
    rows, columns = kept.shape
    width = columns // 4

    def kernel(s_ref, kept_ref, got_ref, x_ref, dy_ref, gain_ref, out_ref, std_ref):
        x = x_ref[...].astype(F32)
        x = x - jnp.mean(x, axis=1, keepdims=True)
        inverse = lax.rsqrt(jnp.mean(x * x, axis=1, keepdims=True) + NORM_EPSILON)
        std_ref[...] = x * inverse
        mean_scaled = jnp.zeros((rows, 1), F32)
        mean_product = jnp.zeros((rows, 1), F32)

        def parts(k):
            cols, at = slice(k * width, (k + 1) * width), aligned(s_ref[k], width)
            total = kept_ref[:, cols] + got_ref[:, cols].astype(F32)
            return at, total * gain_ref[:, cols], std_ref[:, at]

        for k in range(4):
            _, scaled, standard = parts(k)
            mean_scaled += jnp.sum(scaled, axis=1, keepdims=True) / columns
            mean_product += jnp.sum(scaled * standard, axis=1, keepdims=True) / columns
        for k in range(4):
            at, scaled, standard = parts(k)
            change = inverse * (scaled - mean_scaled - standard * mean_product)
            out_ref[:, at] = (dy_ref[:, at].astype(F32) + change).astype(BF16)

    spec = pl.BlockSpec((rows, columns), lambda i, s: (0, 0))
    rows_spec = pl.BlockSpec((rows, columns), lambda i, s: (s[4], 0))
    return kernel_call(
        kernel,
        jnp.concatenate([order, row_block[None]]),
        (kept, got, inputs, upstream, norm_gain),
        [spec, spec, rows_spec, rows_spec, pl.BlockSpec((1, columns), lambda i, s: (0, 0))],
        jax.ShapeDtypeStruct((rows, columns), BF16),
        spec,
        (1,),
        "finish_input_grad",
        scratch=[pltpu.VMEM((rows, columns), F32)],
    )


def norm_grads(order, low, side, inputs, given, kept):
    rows, columns = inputs.shape
    width, step = columns // 4, rows // 2

    def kernel(order_ref, x_ref, given_ref, kept_ref, near_ref, far_ref, std_ref):
        x = x_ref[...].astype(F32)
        x = x - jnp.mean(x, axis=1, keepdims=True)
        std_ref[...] = x * lax.rsqrt(jnp.mean(x * x, axis=1, keepdims=True) + NORM_EPSILON)

        def add(share_ref, first):
            for k in range(4):
                cols = slice(k * width, (k + 1) * width)
                part = share_ref[:, cols].astype(F32)
                product = part * std_ref[:, aligned(order_ref[k], width)]
                sums = jnp.sum(product, axis=0, keepdims=True), jnp.sum(part, axis=0, keepdims=True)
                out_ref, at = near_ref, cols
                if k > 1:
                    out_ref, at = far_ref, aligned((k - 2) ^ order_ref[5], width)
                for n in range(2):
                    before = 0.0 if first else out_ref[n : n + 1, at]
                    out_ref[n : n + 1, at] = before + sums[n]

        @pl.when(pl.program_id(0) == 0)
        def _():
            add(given_ref, True)

        @pl.when(pl.program_id(0) == 1)
        def _():
            add(kept_ref, False)

    half_spec = pl.BlockSpec((step, columns), lambda r, o: (0, 0))
    return kernel_call(
        kernel,
        jnp.concatenate([order, low[None], side[None].astype(jnp.int32)]),
        (inputs, given, kept),
        [
            pl.BlockSpec((step, columns), lambda r, o: (r * o[4] + (1 - r) * (1 - o[4]), 0)),
            half_spec,
            half_spec,
        ],
        [jax.ShapeDtypeStruct((2, columns // 2), F32)] * 2,
        [pl.BlockSpec((2, columns // 2), lambda r, o: (0, 0))] * 2,
        (2,),
        "norm_grads",
        scratch=[pltpu.VMEM((step, columns), F32)],
    )


def pack_sums(norm_sums, upstream_sums, pre_grad, proj_grad):
    wide = max(norm_sums[0].shape[1], pre_grad.shape[1], proj_grad.shape[1])
    step = pre_grad.shape[0] // 8

    def kernel(_, *refs):
        norm_refs, up_refs, grad_refs, out_refs = refs[:2], refs[2:4], refs[4:6], refs[6:]
        for out_ref in out_refs:
            out_ref[...] = jnp.zeros_like(out_ref)
        for norm_ref, up_ref, out_ref in zip(norm_refs, up_refs, out_refs):
            out_ref[0:2, : norm_ref.shape[1]] = norm_ref[...]
            out_ref[2:3, : up_ref.shape[1]] = up_ref[...]
        for n, ref in enumerate(grad_refs):
            total = jnp.zeros((1, ref.shape[1]), F32)
            for c in range(8):
                part = ref[c * step : (c + 1) * step, :].astype(F32)
                total = total + jnp.sum(part, axis=0, keepdims=True)
            for out_ref in out_refs:
                out_ref[3 + n : 4 + n, : ref.shape[1]] = total

    arrays = (*norm_sums, *upstream_sums, pre_grad, proj_grad)
    return kernel_call(
        kernel,
        jnp.zeros((1,), jnp.int32),
        arrays,
        [pl.BlockSpec(a.shape, lambda n, z: (0, 0)) for a in arrays],
        [jax.ShapeDtypeStruct((8, wide), F32)] * 2,
        [pl.BlockSpec((8, wide), lambda n, z: (0, 0))] * 2,
        (1,),
        "pack_sums",
    )


def gather_rows(pieces, places, dtype):
    size, (rows, columns) = len(pieces), pieces[0].shape

    def kernel(place_ref, *refs):
        for n in range(size):
            refs[-1][aligned(place_ref[n], rows), :] = refs[n][...].astype(dtype)

    return kernel_call(
        kernel,
        places,
        pieces,
        [pl.BlockSpec((rows, columns // 2), lambda c, p: (0, c))] * size,
        jax.ShapeDtypeStruct((rows * size, columns), dtype),
        pl.BlockSpec((rows * size, columns // 2), lambda c, p: (0, c)),
        (2,),
        "gather_rows",
    )


def turned(x, cosine, sine):
    lane = lax.broadcasted_iota(jnp.int32, x.shape, 1)
    half = ROT // 2
    partner = jnp.where(
        lane < half, pltpu.roll(x, x.shape[1] - half, axis=1), pltpu.roll(x, half, axis=1)
    )
    return x * cosine + partner * sine


def project(normed, pieces, bias, cosine, sine):
    rows = normed.shape[0] // 2
    width = pieces[0].shape[0]

    def kernel(_, x_ref, *refs):
        piece_refs, (bias_ref, cos_ref, sin_ref, q_ref, kv_ref) = refs[:4], refs[4:]
        total = dot(x_ref[:, :width], piece_refs[0][...], ((1,), (0,)))
        for k in range(1, 4):
            cols = slice(k * width, (k + 1) * width)
            total = total + dot(x_ref[:, cols], piece_refs[k][...], ((1,), (0,)))
        total = total + bias_ref[...]
        cosine, sine = cos_ref[...], sin_ref[...]
        for n, ref in enumerate((q_ref, kv_ref)):
            head = total[:, n * HD : (n + 1) * HD]
            ref[:, :LANES] = turned(head[:, :LANES], cosine, sine).astype(BF16)
            ref[:, LANES:HD] = head[:, LANES:].astype(BF16)
        kv_ref[:, HD:] = total[:, 2 * HD :].astype(BF16)

    def by_row(columns):
        return pl.BlockSpec((rows, columns), lambda s, z: (s, 0))

    return kernel_call(
        kernel,
        jnp.zeros((1,), jnp.int32),
        (normed, *pieces, bias, cosine, sine),
        [by_row(normed.shape[1])]
        + [pl.BlockSpec((width, 3 * HD), lambda s, z: (0, 0))] * 4
        + [pl.BlockSpec((1, 3 * HD), lambda s, z: (0, 0)), by_row(LANES), by_row(LANES)],
        [
            jax.ShapeDtypeStruct((2 * rows, HD), BF16),
            jax.ShapeDtypeStruct((2 * rows, 2 * HD), BF16),
        ],
        [by_row(HD), by_row(2 * HD)],
        (2,),
        "project",
    )


def turn_back(query_grad, kept, got, cosine, sine):
    rows = kept.shape[1]

    def kernel(_, q_ref, kept_ref, got_ref, cos_ref, sin_ref, out_ref):
        both = kept_ref[...] + got_ref[...].astype(F32)
        cosine, sine = cos_ref[...], -sin_ref[...]
        for n, head in enumerate((q_ref[...], both[:, :HD])):
            at = n * HD
            out_ref[:, at : at + LANES] = turned(head[:, :LANES], cosine, sine).astype(BF16)
            out_ref[:, at + LANES : at + HD] = head[:, LANES:].astype(BF16)
        out_ref[:, 2 * HD :] = both[:, HD:].astype(BF16)

    def by_row(columns):
        return pl.BlockSpec((rows, columns), lambda s, z: (s, 0))

    both_spec = pl.BlockSpec((None, rows, 2 * HD), lambda s, z: (s, 0, 0))
    return kernel_call(
        kernel,
        jnp.zeros((1,), jnp.int32),
        (query_grad, kept, got, cosine, sine),
        [by_row(HD), both_spec, both_spec, by_row(LANES), by_row(LANES)],
        jax.ShapeDtypeStruct((2 * rows, 3 * HD), BF16),
        by_row(3 * HD),
        (2,),
        "turn_back",
    )


def attended_grads(upstream, pieces, valid):
    rows = upstream.shape[0] // 2
    width = pieces[0].shape[0]

    def kernel(_, dy_ref, *refs):
        piece_refs, (valid_ref, out_ref) = refs[:4], refs[4:]
        total = dot(dy_ref[:, :width], piece_refs[0][...], ((1,), (0,)))
        for k in range(1, 4):
            cols = slice(k * width, (k + 1) * width)
            total = total + dot(dy_ref[:, cols], piece_refs[k][...], ((1,), (0,)))
        out_ref[...] = total.astype(BF16) * valid_ref[...].astype(BF16)

    def by_row(columns):
        return pl.BlockSpec((rows, columns), lambda s, z: (s, 0))

    return kernel_call(
        kernel,
        jnp.zeros((1,), jnp.int32),
        (upstream, *pieces, valid),
        [by_row(upstream.shape[1])]
        + [pl.BlockSpec((width, HD), lambda s, z: (0, 3))] * 4
        + [by_row(1)],
        jax.ShapeDtypeStruct((2 * rows, HD), BF16),
        by_row(HD),
        (2,),
        "attended_grads",
    )


def chances(query, keys, first, last, key_place):
    scores = []
    for part, place in zip(keys, key_place):
        score = dot(query, part, ((1,), (1,))) * (1.0 / math.sqrt(HD))
        scores.append(jnp.where((place >= first) & (place <= last), score, MASK_FLOOR))
    top = jnp.max(scores[0], axis=1, keepdims=True)
    for score in scores[1:]:
        top = jnp.maximum(top, jnp.max(score, axis=1, keepdims=True))
    exps = [jnp.exp(score - top) for score in scores]
    total = sum(jnp.sum(e, axis=1, keepdims=True) for e in exps)
    return [e / total for e in exps]


def attention_specs(rows, parts):
    return (
        [pl.BlockSpec((rows, HD), lambda n, s: (n + s[0], 0))]
        + [pl.BlockSpec((None, rows, 2 * HD), lambda n, s: (n + s[0], 0, 0))] * parts
        + [pl.BlockSpec((None, rows, 2), lambda n, s: (n + s[0], 0, 0))]
        + [pl.BlockSpec((None, 1, rows), lambda n, s: (n + s[0], 0, 0))] * parts
    )


def attend(queries, both, row_places, key_places, valid):
    rows = queries.shape[0] // 2
    parts = len(both)

    def kernel(_, q_ref, *refs):
        both_refs, place_ref, key_refs = refs[:parts], refs[parts], refs[parts + 1 : 2 * parts + 1]
        valid_ref, out_ref = refs[2 * parts + 1 :]
        step = rows // 2
        for c in range(2):
            at = slice(c * step, (c + 1) * step)
            probs = chances(
                q_ref[at, :],
                [ref[:, :HD] for ref in both_refs],
                place_ref[at, 0:1],
                place_ref[at, 1:2],
                [ref[...] for ref in key_refs],
            )
            total = 0.0
            for p, ref in zip(probs, both_refs):
                total = total + dot(p.astype(BF16), ref[:, HD:], ((1,), (0,)))
            out_ref[at, :] = (total * valid_ref[at, :]).astype(BF16)

    return kernel_call(
        kernel,
        jnp.zeros((1,), jnp.int32),
        (queries, *both, row_places, *key_places, valid),
        attention_specs(rows, parts) + [pl.BlockSpec((rows, 1), lambda n, s: (n, 0))],
        jax.ShapeDtypeStruct(queries.shape, BF16),
        pl.BlockSpec((rows, HD), lambda n, s: (n, 0)),
        (2,),
        "attend",
    )


def attend_back(s, queries, both, row_places, key_places, attended_grad):
    rows = queries.shape[0] // 2
    scale = 1.0 / math.sqrt(HD)

    def kernel(_, q_ref, own_ref, far_ref, place_ref, own_key_ref, far_key_ref, up_ref, *outs):
        query_ref, kept_ref, given_ref = outs
        step = rows // 2
        sums = [[0.0, 0.0], [0.0, 0.0]]
        for c in range(2):
            at = slice(c * step, (c + 1) * step)
            query, up = q_ref[at, :], up_ref[at, :]
            probs = chances(
                query,
                [own_ref[:, :HD], far_ref[:, :HD]],
                place_ref[at, 0:1],
                place_ref[at, 1:2],
                [own_key_ref[...], far_key_ref[...]],
            )
            grads = [dot(up, ref[:, HD:], ((1,), (1,))) for ref in (own_ref, far_ref)]
            delta = sum(jnp.sum(p * g, axis=1, keepdims=True) for p, g in zip(probs, grads))
            total = 0.0
            for n, ref in enumerate((own_ref, far_ref)):
                score_grad = (probs[n] * (grads[n] - delta)).astype(BF16)
                total = total + dot(score_grad, ref[:, :HD], ((1,), (0,)))
                sums[n][0] = sums[n][0] + dot(score_grad, query, ((0,), (0,)))
                sums[n][1] = sums[n][1] + dot(probs[n].astype(BF16), up, ((0,), (0,)))
            query_ref[at, :] = total * scale
        for n, ref in enumerate((kept_ref, given_ref)):
            ref[:, :HD] = (sums[n][0] * scale).astype(ref.dtype)
            ref[:, HD:] = sums[n][1].astype(ref.dtype)

    def whole(columns):
        return pl.BlockSpec((rows, columns), lambda n, s: (0, 0))

    return kernel_call(
        kernel,
        jnp.full((1,), s, jnp.int32),
        (queries, *both, row_places, *key_places, attended_grad),
        attention_specs(rows, 2) + [pl.BlockSpec((rows, HD), lambda n, s: (n + s[0], 0))],
        [
            jax.ShapeDtypeStruct((rows, HD), F32),
            jax.ShapeDtypeStruct((rows, 2 * HD), F32),
            jax.ShapeDtypeStruct((rows, 2 * HD), BF16),
        ],
        [whole(HD), whole(2 * HD), whole(2 * HD)],
        (1,),
        "attend_back",
    )


def pack_attention(qkv_weight, dense_weight, halves):
    rows = qkv_weight.shape[1]
    count = halves.shape[0]

    def kernel(h_ref, qkv_ref, dense_ref, *out_refs):
        for n in range(count):
            for t in range(3):
                out_refs[n][:, t * HD : (t + 1) * HD] = qkv_ref[t, :, aligned(h_ref[n], HD)]
            out_refs[n][:, 3 * HD :] = dense_ref[:, aligned(h_ref[n], HD)]

    def spec(columns):
        return pl.BlockSpec((rows // 2, columns), lambda r, h: (r, 0))

    return kernel_call(
        kernel,
        halves,
        (qkv_weight, dense_weight),
        [pl.BlockSpec((3, rows // 2, 2 * HD), lambda r, h: (0, r, 0)), spec(2 * HD)],
        [jax.ShapeDtypeStruct((rows, 4 * HD), BF16)] * count,
        [spec(4 * HD)] * count,
        (2,),
        "pack_attention",
    )


class Rounds:
    def __init__(self):
        self.last = ()

    def __call__(self, *arrays):
        got = lax.optimization_barrier((*arrays, *self.last))[: len(arrays)]
        return got if len(arrays) > 1 else got[0]

    def done(self, *arrays):
        self.last = arrays
        return arrays if len(arrays) > 1 else arrays[0]

    def close(self, *arrays):
        self.last = (*self.last, *arrays)


def per_device(
    tokens,
    lengths,
    block_order,
    ln_gain,
    ln_bias,
    qkv_weight,
    qkv_bias,
    dense_weight,
    dense_bias,
    fc1_weight,
    fc1_bias,
    fc2_weight,
    fc2_bias,
    cotangent,
):
    me = lax.axis_index("fsdp")
    core = me % 2
    tp_index = lax.axis_index("tp").astype(jnp.int32)
    tp_size = lax.axis_size("tp")
    ctx_index = lax.axis_index("ctx")
    ctx_size = lax.axis_size("ctx")
    pairs = ctx_size == 2
    side = ctx_index % 2 if pairs else 0 * ctx_index
    shard = ln_gain.shape[0]
    row_count = tokens.shape[1]
    block_rows = row_count // 2
    score_scale = 1.0 / math.sqrt(HD)
    order = jnp.stack([me, me ^ 1, me ^ (2 + side), me ^ (3 - side)]).astype(jnp.int32)
    near_bits, far_bits = ((2, 3), (3, 2)) if pairs else ((2, 2), (3, 3))
    inputs_low, upstream_low = tokens[0], cotangent[0]
    then = Rounds()

    halves = jnp.stack([core, 1 - core, core ^ side, core ^ 1 ^ side]).astype(jnp.int32)

    def relayed(name):
        return RELAY[name] and pairs

    def four(weight, name):
        return [half_of(weight, halves[n], 1) for n in range(3 if relayed(name) else 4)]

    def far_of(name, near, packs):
        return ctx_pair(near) if relayed(name) else fsdp_permute(then(packs[3]), far_bits)

    def joined(pieces):
        return jnp.concatenate(pieces, axis=0)

    seq_count, slots = lengths.shape[1], block_order.shape[1]
    vectors = jnp.concatenate(
        [
            v.astype(F32)
            for v in (ln_gain, ln_bias, dense_bias, fc2_bias, lengths[0], block_order[0])
        ]
    )
    then.done(vectors)
    vectors = [
        vectors,
        swap(vectors, 1),
        fsdp_permute(vectors, near_bits),
        fsdp_permute(vectors, far_bits),
    ]
    inputs_other = swap(inputs_low, 1)
    fc1_packs = four(then(fc1_weight), "fc1")
    then.done(*fc1_packs)
    fc1_near = fsdp_permute(fc1_packs[2], near_bits)
    packs = pack_attention(
        qkv_weight.transpose(1, 0, 2), then(dense_weight), halves[: 3 if relayed("attention") else 4]
    )
    then.done(*packs)
    then.close(inputs_other, *vectors[1:])

    def over_features(n):
        return jnp.concatenate([v[n * shard : (n + 1) * shard] for v in vectors])[None, :]

    norm_gain, norm_bias = over_features(0), over_features(1)
    out_bias = over_features(2) + over_features(3)
    their_layout = vectors[1][4 * shard :].astype(jnp.int32)

    upstream_other = swap(then(upstream_low), 1)
    fc1_core, attention_core = swap(then(fc1_packs[1]), 1), swap(then(packs[1]), 1)
    normed = then.done(frame_rows(inputs_low, then(inputs_other), order, (norm_gain, norm_bias)))
    fc2_packs = four(then(fc2_weight), "fc2")
    then.done(*fc2_packs)
    layouts = [
        (then(lengths[0]), block_order[0]),
        (their_layout[:seq_count], their_layout[seq_count:]),
    ]
    local_slots = ctx_index * 2 + jnp.arange(2, dtype=jnp.int32)
    if pairs:
        key_slots = jnp.concatenate([local_slots, (1 - ctx_index) * 2 + jnp.arange(2)])
    else:
        key_slots = jnp.arange(slots, dtype=jnp.int32)
    allowed, valid, positions, row_places, key_places = [], [], [], [], []
    for lengths_row, order_row in layouts:
        local_packed = packed_rows(order_row, local_slots, block_rows)
        key_packed = packed_rows(order_row, key_slots, block_rows)
        segment, position = place_rows(local_packed, lengths_row)
        key_segment = place_rows(key_packed, lengths_row)[0]
        allowed.append(
            (segment[:, None] == key_segment[None, :])
            & (key_packed[None, :] <= local_packed[:, None])
        )
        valid.append((segment < seq_count).astype(F32)[:, None])
        positions.append(position)
        row_places.append(jnp.stack([local_packed - position, local_packed], axis=1))
        key_places.append(key_packed[None, :])
    cosine_table, sine_table = rotation_tables(jnp.concatenate(positions))
    valid = jnp.concatenate(valid)
    upstream_sum = jnp.sum(upstream_low.astype(F32), axis=0, keepdims=True)
    row_places, key_places = jnp.stack(row_places), jnp.stack(key_places)
    upstream_near, upstream_far = [
        jnp.concatenate(
            [lax.dynamic_slice_in_dim(upstream_sum, order[k] * shard, shard, axis=1) for k in blocks],
            axis=1,
        )
        for blocks in ((0, 1), (2 + side, 3 - side))
    ]
    then.done(cosine_table, sine_table, valid, upstream_near, upstream_far, row_places, key_places, *fc2_packs)
    then.close(upstream_other, fc1_core, attention_core, fc1_near)

    attention_near = fsdp_permute(then(packs[2]), near_bits)
    fc1_far = far_of("fc1", then(fc1_near), fc1_packs)
    fc2_core = swap(then(fc2_packs[1]), 1)
    upstream = then.done(frame_rows(upstream_low, then(upstream_other), order))
    fc1_pieces = [fc1_packs[0], fc1_core, fc1_near, fc1_far]
    then.close(attention_near, fc1_far, fc2_core)

    def grad_block(k, *products, kind=BF16):
        parts = []
        for left, right in products:
            rows = lax.dynamic_slice_in_dim(left, k * shard, shard, axis=1)
            parts.append(dot(rows, right, ((0,), (0,))).astype(kind))
        return jnp.concatenate(parts, axis=1)

    def grad_blocks(*products):
        far = grad_block(2 + side, *products)
        rest = [grad_block(k, *products) for k in (3 - side, 1)]
        return (far, *rest, grad_block(0, *products, kind=F32))

    def add_mine(own, far):
        return then.done((own + then(far).astype(F32)).astype(BF16))

    def add_theirs(near, farther):
        return then.done((near.astype(F32) + then(farther).astype(F32)).astype(BF16))

    def placed(mine, theirs, attention=False):
        parts = then(*mine, *theirs)
        return then.done(*place_grad(parts, core, attention))

    fc2_near = fsdp_permute(then(fc2_packs[2]), near_bits)
    attention_far = far_of("attention", then(attention_near), packs)
    attention = [packs[0], attention_core, attention_near, attention_far]
    pre_act = dot(then(normed), joined(fc1_pieces), ((1,), (0,)))
    pre_act = pre_act + half_of(fc1_bias, core, 0).astype(F32)[None, :]
    normal_cdf = 0.5 * (1.0 + lax.erf(pre_act * (1.0 / math.sqrt(2.0))))
    density = jnp.exp(-0.5 * pre_act * pre_act) * (1.0 / math.sqrt(2.0 * math.pi))
    hidden = (pre_act * normal_cdf).astype(BF16)
    slope = normal_cdf + pre_act * density
    hidden, slope = then.done(hidden, slope)
    fc2_blocks = then.done(*grad_blocks((then(upstream), hidden)))
    then.close(fc2_near, attention_far)

    def row_block_of(index):
        place, bit = 0 * index, 1
        while bit < tp_size:
            place = place * 2 + (index // bit) % 2
            bit *= 2
        return place

    def flips_to_places(flips):
        return jnp.stack([row_block_of(tp_index ^ f) for f in flips]).astype(jnp.int32)

    fc2_far = far_of("fc2", then(fc2_near), fc2_packs)
    fc2_pieces = [fc2_packs[0], fc2_core, fc2_near, fc2_far]
    fc2_grad_near = swap(then(fc2_blocks[2]), 1)
    qkv_bias_own = half_of(qkv_bias, core, 1).astype(F32).reshape(1, 3 * HD)
    queries, both_local = then.done(
        *project(then(normed), attention, qkv_bias_own, cosine_table, sine_table)
    )
    both_local = both_local.reshape(2, row_count, 2 * HD)
    if pairs:
        both_other = ctx_pair(both_local)
    else:
        both_other = lax.all_gather(both_local, "ctx", axis=1, tiled=True)
    attended_grad = then.done(attended_grads(then(upstream), attention, valid))
    then.close(fc2_far, fc2_grad_near)

    fc2_grad_far = swap(then(fc2_blocks[0]), 2)
    hidden_grad = dot(then(upstream), joined(fc2_pieces), ((1,), (0,)))
    pre_grad = then.done((hidden_grad * slope).astype(BF16))
    both_other = then(both_other)
    attended, probs_all = [], []
    if pairs:
        both = (both_local, both_other)
        key_parts = key_places[:, :, :row_count], key_places[:, :, row_count:]
        attended = then.done(attend(queries, both, row_places, key_parts, valid))
    else:
        for s in range(2):
            rows = slice(s * row_count, (s + 1) * row_count)
            keys, values = both_other[s, :, :HD], both_other[s, :, HD:]
            scores = dot(queries[rows], keys, ((1,), (1,))) * score_scale
            scores = jnp.where(allowed[s], scores, MASK_FLOOR)
            exp_scores = jnp.exp(scores - jnp.max(scores, axis=1, keepdims=True))
            probs = exp_scores / jnp.sum(exp_scores, axis=1, keepdims=True)
            probs_all.append(probs)
            attended.append(dot(probs.astype(BF16), values, ((1,), (0,))))
        attended = then.done((jnp.concatenate(attended) * valid).astype(BF16))
    hidden_size = hidden.shape[1]
    second = (hidden, fc2_pieces, 0, hidden_size)
    theirs = then.done(share_rows((attended, attention, 3, HD), second, row_count))
    then.close(fc2_grad_far)

    def attention_grads(s):
        if pairs:
            return then.done(
                *attend_back(s, queries, both, row_places, key_parts, then(attended_grad))
            )
        rows = slice(s * row_count, (s + 1) * row_count)
        keys, values = both_other[s, :, :HD], both_other[s, :, HD:]
        probs, head_grad = probs_all[s], then(attended_grad[rows])
        prob_grad = dot(head_grad, values, ((1,), (1,)))
        row_delta = jnp.sum(probs * prob_grad, axis=1, keepdims=True)
        score_grad = (probs * (prob_grad - row_delta)).astype(BF16)
        query_piece = dot(score_grad, keys, ((1,), (0,))) * score_scale
        key_piece = dot(score_grad, queries[rows], ((0,), (0,))) * score_scale
        value_piece = dot(probs.astype(BF16), head_grad, ((0,), (0,)))
        return then.done(query_piece, jnp.concatenate([key_piece, value_piece], axis=1))

    low = tp_index % 2

    def halve_on(kept, got, bit, row_block):
        while bit < tp_size:
            total, digit = kept.astype(F32) + got.astype(F32), (tp_index // bit) % 2
            given, kept = then.done(
                half_of(total, 1 - digit, 0).astype(BF16), half_of(total, digit, 0)
            )
            got, row_block, bit = tp_pair(given, bit), row_block * 2 + digit, bit * 2
        return kept, got, row_block

    def double_up(part):
        pieces, flips, bit = [part], [0], tp_size // 2
        while bit > 1:
            pieces += [tp_pair(p, bit) for p in pieces]
            flips += [f ^ bit for f in flips]
            bit //= 2
        return pieces, flips + [f ^ 1 for f in flips]

    def fc1_block(k, kind=BF16):
        return weight_grad(k, shard, [(then(normed), pre_grad)], kind)

    fc2_grad_farther = swap(then(fc2_blocks[1]), 3)
    theirs = swap(then(theirs), 1)
    fc2_mine = ctx_terms(add_mine(fc2_blocks[3], fc2_grad_far))
    grads_first = attention_grads(0)
    first = (then(attended), attention, 3, HD)
    given, kept = then.done(*share_rows(first, second, row_count, theirs, low))
    fc1_far_block = then.done(grad_block(2 + side, (then(normed), pre_grad)))
    then.close(fc2_grad_farther)

    fc1_grad_far = swap(then(fc1_far_block), 2)
    out_got = tp_pair(then(given), 1)
    fc1_near_block = then.done(grad_block(1, (then(normed), pre_grad)))
    fc1_grad_near = swap(fc1_near_block, 1)
    grads_second = attention_grads(1)
    both_grad = jnp.stack([grads_first[1], grads_second[1]])
    query_grad = jnp.concatenate([grads_first[0], grads_second[0]])
    if pairs:
        both_given = jnp.stack([grads_first[2], grads_second[2]])
    else:
        both_given = jnp.zeros((2, row_count, 2 * HD), BF16)
        both_grad = lax.psum_scatter(both_grad, "ctx", scatter_dimension=1, tiled=True)
    both_given, both_grad, query_grad = then.done(both_given, both_grad, query_grad)
    both_got = ctx_pair(both_given) if pairs else both_given
    fc1_farther_block = then.done(grad_block(3 - side, (then(normed), pre_grad)))
    fc1_own_block = then.done(fc1_block(0, F32))
    then.close(fc1_grad_far, out_got, fc2_mine[1], fc1_grad_near)

    fc1_grad_farther = swap(then(fc1_farther_block), 3)
    out_kept, out_got, out_block = halve_on(then(kept), out_got, 2, low)
    fc2_theirs = add_theirs(fc2_grad_near, fc2_grad_farther)
    proj_grad = then.done(
        turn_back(then(query_grad), both_grad, both_got, cosine_table, sine_table)
    )
    second = (pre_grad, fc1_pieces, 0, hidden_size)
    theirs = then.done(share_rows((proj_grad, attention, 0, 3 * HD), second, row_count))

    def attention_block(k, kind=BF16):
        return weight_grad(k, shard, [(then(normed), proj_grad), (upstream, attended)], kind)

    far_block = then.done(attention_block(2 + side))
    then.close(fc1_grad_farther, out_got)

    attention_grad_far = swap(then(far_block), 2)
    theirs = swap(then(theirs), 1)
    fc2_theirs = ctx_terms(then(fc2_theirs))
    out_part = then.done(
        finish_output(order, out_block, then(out_kept), out_got, inputs_low, out_bias)
    )
    out_pieces, flips = double_up(out_part)
    out_late = [tp_pair(out_part, 1)]
    first = (then(proj_grad), attention, 0, 3 * HD)
    given, kept = then.done(*share_rows(first, second, row_count, theirs, low))
    farther_block = then.done(attention_block(3 - side))
    then.close(attention_grad_far, out_late[0], *out_pieces[1:], fc2_theirs[1])

    attention_grad_farther = swap(then(farther_block), 3)
    got = tp_pair(then(given), 1)
    fc1_mine = ctx_terms(add_mine(fc1_own_block, fc1_grad_far))
    norm_near, norm_far = then.done(*norm_grads(order, low, side, then(inputs_low), given, kept))
    sums, sums_given = then.done(
        *pack_sums(
            (norm_near, norm_far), (upstream_near, upstream_far), then(pre_grad), proj_grad
        )
    )
    sums_got = swap(sums_given, 2)
    near_block = then.done(attention_block(1))
    own_block = then.done(attention_block(0, kind=F32))
    attention_mine = add_mine(own_block, attention_grad_far)
    fc1_theirs = add_theirs(fc1_grad_near, fc1_grad_farther)
    then.close(attention_grad_farther, got, fc1_mine[1], sums_got)

    fc1_theirs = ctx_terms(then(fc1_theirs))
    kept, got, row_block = halve_on(then(kept), got, 2, low)
    out_late += [tp_pair(p, 1) for p in then(out_pieces[0], *out_pieces[1:])[1:]]
    sums = then(sums) + sums_got
    norm_sums, other_sums = sums[:2], sums[2:]
    norm_sums = norm_sums + tp_pair(norm_sums, 1)
    attention_grad_near = swap(then(near_block), 1)
    fc2_out = placed(fc2_mine, fc2_theirs)
    then.close(got, norm_sums, fc1_theirs[1], attention_grad_near, *out_late[1:])

    attention_mine = ctx_terms(then(attention_mine))
    input_part = then.done(
        finish_input_grad(order, row_block, then(kept), got, inputs_low, upstream_low, norm_gain)
    )
    pieces, _ = double_up(input_part)
    late = [tp_pair(input_part, 1)]
    bit = 2
    while bit < tp_size:
        norm_sums = norm_sums + tp_pair(then(norm_sums), bit)
        bit *= 2
    attention_theirs = add_theirs(attention_grad_near, attention_grad_farther)
    fc1_out = placed(fc1_mine, fc1_theirs)
    output = then.done(gather_rows(then(*out_pieces, *out_late), flips_to_places(flips), BF16))
    then.close(*pieces[1:], late[0], norm_sums, attention_mine[1])

    late += [tp_pair(p, 1) for p in then(*pieces, output)[1 : len(pieces)]]
    attention_theirs = ctx_terms(then(attention_theirs))
    sums = sum(ctx_terms(jnp.concatenate([then(norm_sums), other_sums])))
    then.close(*late[1:], attention_theirs[1], sums)

    sums = then(sums)
    other_core = swap(sums, 1)
    vector_sums = sums[:3, :shard] + other_core[:3, shard : 2 * shard]

    def column_sums(packed):
        return packed[3, :hidden_size], packed[4, : 3 * HD].reshape(3, HD)

    input_grad = gather_rows(then(*pieces, *late), flips_to_places(flips), F32)
    qkv_out, dense_out = placed(attention_mine, attention_theirs, True)

    def in_order(mine, other, axis):
        return jnp.where(
            core == 0,
            jnp.concatenate([mine, other], axis=axis),
            jnp.concatenate([other, mine], axis=axis),
        )

    fc1_bias_grad, qkv_bias_grad = [
        in_order(mine, other, axis)
        for axis, mine, other in zip((0, 1), column_sums(sums), column_sums(other_core))
    ]
    return (
        output[None],
        input_grad[None],
        vector_sums[0],
        vector_sums[1],
        qkv_out.transpose(1, 0, 2),
        qkv_bias_grad,
        dense_out,
        vector_sums[2],
        fc1_out,
        fc1_bias_grad,
        fc2_out,
        vector_sums[2],
    )


def solution(mesh):
    placed = (
        P("fsdp", "ctx", None),
        P("fsdp", None),
        P("fsdp", None),
        P("fsdp"),
        P("fsdp"),
        P("fsdp", None, "tp"),
        P(None, "tp"),
        P("fsdp", "tp"),
        P("fsdp"),
        P("fsdp", "tp"),
        P("tp"),
        P("fsdp", "tp"),
        P("fsdp"),
        P("fsdp", "ctx", None),
    )
    return jax.shard_map(
        per_device,
        mesh=mesh,
        in_specs=placed,
        out_specs=(
            P("fsdp", "ctx", None),
            P("fsdp", "ctx", None),
            P("fsdp"),
            P("fsdp"),
            P("fsdp", None, "tp"),
            P(None, "tp"),
            P("fsdp", "tp"),
            P("fsdp"),
            P("fsdp", "tp"),
            P("tp"),
            P("fsdp", "tp"),
            P("fsdp"),
        ),
        check_vma=False,
    )
```

```python
import math

import jax
import jax.numpy as jnp
from jax import lax
from jax.experimental import pallas as pl
from jax.experimental.pallas import tpu as pltpu
from jax.sharding import PartitionSpec as P

HD = 256
ROT = 64


NORM_EPSILON = 1e-05
MASK_FLOOR = -1000000000.0
F32 = jnp.float32
BF16 = jnp.bfloat16
LANES = 128
RELAY = {"attention": True, "fc1": True, "fc2": False}


def rotation_tables(position):
    half = ROT // 2
    frequency = jnp.exp(jnp.arange(half, dtype=F32) * (-2.0 * math.log(10000.0) / ROT))
    angles = position.astype(F32)[:, None] * frequency[None, :]
    cosine, sine = jnp.cos(angles), jnp.sin(angles)
    rest = (position.shape[0], LANES - ROT)
    return (
        jnp.concatenate([cosine, cosine, jnp.ones(rest, F32)], axis=1),
        jnp.concatenate([-sine, sine, jnp.zeros(rest, F32)], axis=1),
    )


def packed_rows(order_row, slots, block_rows):
    selector = slots[:, None] == jnp.arange(order_row.shape[0], dtype=jnp.int32)[None, :]
    source_block = jnp.sum(jnp.where(selector, order_row[None, :], 0), axis=1, dtype=jnp.int32)
    within = jnp.arange(block_rows, dtype=jnp.int32)
    return (source_block[:, None] * block_rows + within[None, :]).reshape(-1)


def place_rows(packed_at, lengths_row):
    seq_ends = jnp.cumsum(lengths_row, dtype=jnp.int32)
    passed = packed_at[:, None] >= seq_ends[None, :]
    segment = jnp.sum(passed.astype(jnp.int32), axis=1, dtype=jnp.int32)
    before = jnp.sum(jnp.where(passed, lengths_row[None, :], 0), axis=1, dtype=jnp.int32)
    return (segment, packed_at - before)


def dot(a, b, contract):
    return lax.dot_general(a, b, (contract, ((), ())), preferred_element_type=F32)


def fsdp_permute(x, bits):
    size, lanes = lax.axis_size("fsdp"), lax.axis_size("ctx")
    perm = [
        (f * lanes + x, (f ^ bits[x % 2]) * lanes + x) for f in range(size) for x in range(lanes)
    ]
    return lax.ppermute(x, ("fsdp", "ctx"), perm)


def swap(x, bit):
    return fsdp_permute(x, (bit, bit))


def ctx_pair(x):
    return lax.ppermute(x, "ctx", [(0, 1), (1, 0)])


def ctx_terms(x):
    if lax.axis_size("ctx") == 2:
        return x, ctx_pair(x)
    return lax.psum(x.astype(F32), "ctx"), jnp.zeros_like(x)


def tp_pair(x, bit):
    return lax.ppermute(x, "tp", [(i, i ^ bit) for i in range(lax.axis_size("tp"))])


def half_of(x, which, axis):
    size = x.shape[axis] // 2
    return lax.dynamic_slice_in_dim(x, which * size, size, axis=axis)


def kernel_call(body, scalars, arrays, in_specs, out_shape, out_specs, grid, name, scratch=(), aliases=None):
    return pl.pallas_call(
        body,
        out_shape=out_shape,
        grid_spec=pltpu.PrefetchScalarGridSpec(
            num_scalar_prefetch=1,
            grid=grid,
            in_specs=in_specs,
            out_specs=out_specs,
            scratch_shapes=scratch,
        ),
        input_output_aliases=aliases or {},
        cost_estimate=pl.CostEstimate(flops=0, transcendentals=0, bytes_accessed=0),
        name=name,
    )(scalars, *arrays)


def aligned(index, size):
    return pl.ds(pl.multiple_of(index * size, size), size)


def frame_rows(own, other, order, norm=None):
    rows, columns = own.shape
    width, step = columns // 4, rows // 2

    def kernel(order_ref, own_ref, other_ref, *refs):
        gain_ref, bias_ref, out_ref, wide_ref = refs if norm else (None, None, refs[0], None)
        for s, ref in enumerate((own_ref, other_ref)):
            if norm:
                x = ref[...].astype(F32)
                x = x - jnp.mean(x, axis=1, keepdims=True)
                variance = jnp.mean(x * x, axis=1, keepdims=True)
                wide_ref[...] = x * lax.rsqrt(variance + NORM_EPSILON)
            for k in range(4):
                to = slice(k * width, (k + 1) * width)
                at = aligned(order_ref[k], width)
                if norm:
                    out_ref[s, :, to] = (
                        wide_ref[:, at] * gain_ref[:, to] + bias_ref[:, to]
                    ).astype(BF16)
                else:
                    out_ref[s, :, to] = ref[:, at]

    row_spec = pl.BlockSpec((step, columns), lambda r, o: (r, 0))
    vector_spec = pl.BlockSpec((1, columns), lambda r, o: (0, 0))
    out = kernel_call(
        kernel,
        order,
        (own, other, *(norm or ())),
        [row_spec, row_spec] + ([vector_spec, vector_spec] if norm else []),
        jax.ShapeDtypeStruct((2, rows, columns), BF16),
        pl.BlockSpec((2, step, columns), lambda r, o: (0, r, 0)),
        (2,),
        "norm_rows" if norm else "frame_rows",
        scratch=[pltpu.VMEM((step, columns), F32)] if norm else (),
    )
    return out.reshape(2 * rows, columns)


def place_grad(parts, core, attention):
    rows, columns = parts[0].shape
    step = rows // 2

    def kernel(core_ref, a_ref, ax_ref, b_ref, bx_ref, *out_refs):
        for h, (u_ref, ux_ref) in enumerate(((a_ref, ax_ref), (b_ref, bx_ref))):
            total = u_ref[...].astype(F32) + ux_ref[...].astype(F32)
            place = core_ref[0] ^ h
            if attention:
                for t in range(3):
                    out_refs[0][t, :, aligned(place, HD)] = total[:, t * HD : (t + 1) * HD]
                out_refs[1][:, aligned(place, HD)] = total[:, 3 * HD :]
            else:
                out_refs[0][:, aligned(place, columns)] = total

    shapes = [(rows, 2 * columns)]
    specs = [pl.BlockSpec((step, 2 * columns), lambda r, c: (r, 0))]
    if attention:
        shapes = [(3, rows, 2 * HD), (rows, 2 * HD)]
        specs = [
            pl.BlockSpec((3, step, 2 * HD), lambda r, c: (0, r, 0)),
            pl.BlockSpec((step, 2 * HD), lambda r, c: (r, 0)),
        ]
    return kernel_call(
        kernel,
        core[None],
        parts,
        [pl.BlockSpec((step, columns), lambda r, c: (r, 0))] * 4,
        [jax.ShapeDtypeStruct(shape, F32) for shape in shapes],
        specs,
        (2,),
        "place_grad",
    )


def weight_grad(block, shard, products, kind):
    step = shard // 2
    widths = [right.shape[1] for _, right in products]

    def kernel(_, *refs):
        at = 0
        for n, width in enumerate(widths):
            left_ref, right_ref = refs[2 * n : 2 * n + 2]
            total = dot(left_ref[...], right_ref[...], ((0,), (0,)))
            refs[-1][:, at : at + width] = total.astype(kind)
            at += width

    specs = []
    for left, right in products:
        specs.append(pl.BlockSpec((left.shape[0], step), lambda n, k: (0, 2 * k[0] + n)))
        specs.append(pl.BlockSpec(right.shape, lambda n, k: (0, 0)))
    return kernel_call(
        kernel,
        jnp.asarray(block, jnp.int32)[None],
        [a for product in products for a in product],
        specs,
        jax.ShapeDtypeStruct((shard, sum(widths)), kind),
        pl.BlockSpec((step, sum(widths)), lambda n, k: (n, 0)),
        (2,),
        "weight_grad",
    )


def share_rows(first, second, rows, theirs=None, low=None):
    width = first[1][0].shape[0]
    own = theirs is not None
    at = 0 if own else 1
    half = rows // 2

    def kernel(low_ref, f_ref, s_ref, *refs):
        f_refs, s_refs, refs = refs[:4], refs[4:8], refs[8:]
        for n in range(2):

            @pl.when(pl.program_id(0) == n)
            def _(n=n):
                for m in range(2):
                    k = 2 * n + m
                    total = dot(f_ref[...], f_refs[k][...], ((1,), (1,)))
                    total = total + dot(s_ref[...], s_refs[k][...], ((1,), (1,)))
                    if not own:
                        refs[0][:, (1 - m) * width : (2 - m) * width] = total.astype(BF16)
                        continue
                    theirs_ref, given_ref, kept_ref, all_ref = refs
                    to = slice(m * width, (m + 1) * width)
                    all_ref[...] = (total + theirs_ref[:, to].astype(F32)).astype(BF16)
                    given_ref[:, to] = all_ref[aligned(1 - low_ref[0], half), :]
                    kept_ref[:, to] = all_ref[aligned(low_ref[0], half), :]

    arrays, in_specs = [], []
    for acts, _, _, size in (first, second):
        arrays.append(acts)
        in_specs.append(pl.BlockSpec((rows, size), lambda n, b: (at, 0)))
    for _, pieces, block, size in (first, second):
        arrays += pieces
        in_specs += [pl.BlockSpec((width, size), lambda n, b, block=block: (0, block))] * 4
    out_shape = jax.ShapeDtypeStruct((rows, 4 * width), BF16)
    out_spec = pl.BlockSpec((rows, 2 * width), lambda n, b: (0, n))
    scratch = ()
    if own:
        arrays.append(theirs)
        in_specs.append(out_spec)
        out_shape = [jax.ShapeDtypeStruct((half, 4 * width), BF16)] * 2
        out_spec = [pl.BlockSpec((half, 2 * width), lambda n, b: (0, n))] * 2
        scratch = [pltpu.VMEM((rows, width), BF16)]
    return kernel_call(
        kernel,
        low[None] if own else jnp.zeros((1,), jnp.int32),
        arrays,
        in_specs,
        out_shape,
        out_spec,
        (2,),
        "share_rows",
        scratch=scratch,
    )


def finish_output(order, row_block, kept, got, inputs, out_bias):
    rows, columns = kept.shape
    width, steps = columns // 4, 4
    step = rows // steps

    def kernel(s_ref, kept_ref, got_ref, x_ref, bias_ref, out_ref):
        for k in range(4):
            cols, at = slice(k * width, (k + 1) * width), aligned(s_ref[k], width)
            total = kept_ref[:, cols] + got_ref[:, cols].astype(F32)
            out_ref[:, at] = (x_ref[:, at].astype(F32) + total + bias_ref[:, cols]).astype(BF16)

    spec = pl.BlockSpec((step, columns), lambda i, s: (i, 0))
    return kernel_call(
        kernel,
        jnp.concatenate([order, row_block[None]]),
        (kept, got, inputs, out_bias),
        [
            spec,
            spec,
            pl.BlockSpec((step, columns), lambda i, s: (s[4] * steps + i, 0)),
            pl.BlockSpec((1, columns), lambda i, s: (0, 0)),
        ],
        jax.ShapeDtypeStruct((rows, columns), BF16),
        spec,
        (steps,),
        "finish_output",
    )


def finish_input_grad(order, row_block, kept, got, inputs, upstream, norm_gain):
    rows, columns = kept.shape
    width, steps = columns // 4, 4
    step = rows // steps

    def kernel(s_ref, kept_ref, got_ref, x_ref, dy_ref, gain_ref, out_ref, std_ref):
        x = x_ref[...].astype(F32)
        x = x - jnp.mean(x, axis=1, keepdims=True)
        inverse = lax.rsqrt(jnp.mean(x * x, axis=1, keepdims=True) + NORM_EPSILON)
        std_ref[...] = x * inverse
        mean_scaled = jnp.zeros((step, 1), F32)
        mean_product = jnp.zeros((step, 1), F32)

        def parts(k):
            cols, at = slice(k * width, (k + 1) * width), aligned(s_ref[k], width)
            total = kept_ref[:, cols] + got_ref[:, cols].astype(F32)
            return at, total * gain_ref[:, cols], std_ref[:, at]

        for k in range(4):
            _, scaled, standard = parts(k)
            mean_scaled += jnp.sum(scaled, axis=1, keepdims=True) / columns
            mean_product += jnp.sum(scaled * standard, axis=1, keepdims=True) / columns
        for k in range(4):
            at, scaled, standard = parts(k)
            change = inverse * (scaled - mean_scaled - standard * mean_product)
            out_ref[:, at] = (dy_ref[:, at].astype(F32) + change).astype(BF16)

    spec = pl.BlockSpec((step, columns), lambda i, s: (i, 0))
    rows_spec = pl.BlockSpec((step, columns), lambda i, s: (s[4] * steps + i, 0))
    return kernel_call(
        kernel,
        jnp.concatenate([order, row_block[None]]),
        (kept, got, inputs, upstream, norm_gain),
        [spec, spec, rows_spec, rows_spec, pl.BlockSpec((1, columns), lambda i, s: (0, 0))],
        jax.ShapeDtypeStruct((rows, columns), BF16),
        spec,
        (steps,),
        "finish_input_grad",
        scratch=[pltpu.VMEM((step, columns), F32)],
    )


def norm_grads(order, low, side, inputs, given, kept):
    rows, columns = inputs.shape
    width, step = columns // 4, rows // 2

    def kernel(order_ref, x_ref, given_ref, kept_ref, near_ref, far_ref, std_ref):
        x = x_ref[...].astype(F32)
        x = x - jnp.mean(x, axis=1, keepdims=True)
        std_ref[...] = x * lax.rsqrt(jnp.mean(x * x, axis=1, keepdims=True) + NORM_EPSILON)

        def add(share_ref, first):
            for k in range(4):
                cols = slice(k * width, (k + 1) * width)
                part = share_ref[:, cols].astype(F32)
                product = part * std_ref[:, aligned(order_ref[k], width)]
                sums = jnp.sum(product, axis=0, keepdims=True), jnp.sum(part, axis=0, keepdims=True)
                out_ref, at = near_ref, cols
                if k > 1:
                    out_ref, at = far_ref, aligned((k - 2) ^ order_ref[5], width)
                for n in range(2):
                    before = 0.0 if first else out_ref[n : n + 1, at]
                    out_ref[n : n + 1, at] = before + sums[n]

        @pl.when(pl.program_id(0) == 0)
        def _():
            add(given_ref, True)

        @pl.when(pl.program_id(0) == 1)
        def _():
            add(kept_ref, False)

    half_spec = pl.BlockSpec((step, columns), lambda r, o: (0, 0))
    return kernel_call(
        kernel,
        jnp.concatenate([order, low[None], side[None].astype(jnp.int32)]),
        (inputs, given, kept),
        [
            pl.BlockSpec((step, columns), lambda r, o: (r * o[4] + (1 - r) * (1 - o[4]), 0)),
            half_spec,
            half_spec,
        ],
        [jax.ShapeDtypeStruct((2, columns // 2), F32)] * 2,
        [pl.BlockSpec((2, columns // 2), lambda r, o: (0, 0))] * 2,
        (2,),
        "norm_grads",
        scratch=[pltpu.VMEM((step, columns), F32)],
    )


def halve_rows(digit, kept, got):
    rows, columns = kept.shape

    def kernel(_, a_ref, b_ref, c_ref, d_ref, given_ref, kept_ref):
        given_ref[...] = (a_ref[...].astype(F32) + b_ref[...].astype(F32)).astype(BF16)
        kept_ref[...] = c_ref[...].astype(F32) + d_ref[...].astype(F32)

    block = rows // 2, columns // 2
    leaves = pl.BlockSpec(block, lambda n, d: (1 - d[0], n))
    stays = pl.BlockSpec(block, lambda n, d: (d[0], n))
    out_spec = pl.BlockSpec(block, lambda n, d: (0, n))
    return kernel_call(
        kernel,
        digit[None],
        (kept, got, kept, got),
        [leaves, leaves, stays, stays],
        [jax.ShapeDtypeStruct((rows // 2, columns), kind) for kind in (BF16, F32)],
        [out_spec, out_spec],
        (2,),
        "halve_rows",
    )


def pack_sums(norm_sums, upstream_sums, pre_grad, proj_grad):
    wide = max(norm_sums[0].shape[1], pre_grad.shape[1], proj_grad.shape[1])
    step = pre_grad.shape[0] // 8

    def kernel(_, *refs):
        norm_refs, up_refs, grad_refs, out_refs = refs[:2], refs[2:4], refs[4:6], refs[6:]
        for out_ref in out_refs:
            out_ref[...] = jnp.zeros_like(out_ref)
        for norm_ref, up_ref, out_ref in zip(norm_refs, up_refs, out_refs):
            out_ref[0:2, : norm_ref.shape[1]] = norm_ref[...]
            out_ref[2:3, : up_ref.shape[1]] = up_ref[...]
        for n, ref in enumerate(grad_refs):
            total = jnp.zeros((1, ref.shape[1]), F32)
            for c in range(8):
                part = ref[c * step : (c + 1) * step, :].astype(F32)
                total = total + jnp.sum(part, axis=0, keepdims=True)
            for out_ref in out_refs:
                out_ref[3 + n : 4 + n, : ref.shape[1]] = total

    arrays = (*norm_sums, *upstream_sums, pre_grad, proj_grad)
    return kernel_call(
        kernel,
        jnp.zeros((1,), jnp.int32),
        arrays,
        [pl.BlockSpec(a.shape, lambda n, z: (0, 0)) for a in arrays],
        [jax.ShapeDtypeStruct((8, wide), F32)] * 2,
        [pl.BlockSpec((8, wide), lambda n, z: (0, 0))] * 2,
        (1,),
        "pack_sums",
    )


def gather_rows(pieces, places, dtype):
    size, (rows, columns) = len(pieces), pieces[0].shape

    def kernel(place_ref, *refs):
        for n in range(size):
            refs[-1][aligned(place_ref[n], rows), :] = refs[n][...].astype(dtype)

    return kernel_call(
        kernel,
        places,
        pieces,
        [pl.BlockSpec((rows, columns // 4), lambda c, p: (0, c))] * size,
        jax.ShapeDtypeStruct((rows * size, columns), dtype),
        pl.BlockSpec((rows * size, columns // 4), lambda c, p: (0, c)),
        (4,),
        "gather_rows",
    )


def turned(x, cosine, sine):
    lane = lax.broadcasted_iota(jnp.int32, x.shape, 1)
    half = ROT // 2
    partner = jnp.where(
        lane < half, pltpu.roll(x, x.shape[1] - half, axis=1), pltpu.roll(x, half, axis=1)
    )
    return x * cosine + partner * sine


def project(normed, pieces, bias, cosine, sine):
    rows = normed.shape[0] // 2
    width = pieces[0].shape[0]

    def kernel(_, x_ref, *refs):
        piece_refs, (bias_ref, cos_ref, sin_ref, q_ref, kv_ref) = refs[:4], refs[4:]
        total = dot(x_ref[:, :width], piece_refs[0][...], ((1,), (0,)))
        for k in range(1, 4):
            cols = slice(k * width, (k + 1) * width)
            total = total + dot(x_ref[:, cols], piece_refs[k][...], ((1,), (0,)))
        total = total + bias_ref[...]
        cosine, sine = cos_ref[...], sin_ref[...]
        for n, ref in enumerate((q_ref, kv_ref)):
            head = total[:, n * HD : (n + 1) * HD]
            ref[:, :LANES] = turned(head[:, :LANES], cosine, sine).astype(BF16)
            ref[:, LANES:HD] = head[:, LANES:].astype(BF16)
        kv_ref[:, HD:] = total[:, 2 * HD :].astype(BF16)

    def by_row(columns):
        return pl.BlockSpec((rows, columns), lambda s, z: (s, 0))

    return kernel_call(
        kernel,
        jnp.zeros((1,), jnp.int32),
        (normed, *pieces, bias, cosine, sine),
        [by_row(normed.shape[1])]
        + [pl.BlockSpec((width, 3 * HD), lambda s, z: (0, 0))] * 4
        + [pl.BlockSpec((1, 3 * HD), lambda s, z: (0, 0)), by_row(LANES), by_row(LANES)],
        [
            jax.ShapeDtypeStruct((2 * rows, HD), BF16),
            jax.ShapeDtypeStruct((2 * rows, 2 * HD), BF16),
        ],
        [by_row(HD), by_row(2 * HD)],
        (2,),
        "project",
    )


def turn_back(query_grad, kept, got, cosine, sine):
    rows = kept.shape[1]

    def kernel(_, q_ref, kept_ref, got_ref, cos_ref, sin_ref, out_ref):
        both = kept_ref[...] + got_ref[...].astype(F32)
        cosine, sine = cos_ref[...], -sin_ref[...]
        for n, head in enumerate((q_ref[...], both[:, :HD])):
            at = n * HD
            out_ref[:, at : at + LANES] = turned(head[:, :LANES], cosine, sine).astype(BF16)
            out_ref[:, at + LANES : at + HD] = head[:, LANES:].astype(BF16)
        out_ref[:, 2 * HD :] = both[:, HD:].astype(BF16)

    def by_row(columns):
        return pl.BlockSpec((rows, columns), lambda s, z: (s, 0))

    both_spec = pl.BlockSpec((None, rows, 2 * HD), lambda s, z: (s, 0, 0))
    return kernel_call(
        kernel,
        jnp.zeros((1,), jnp.int32),
        (query_grad, kept, got, cosine, sine),
        [by_row(HD), both_spec, both_spec, by_row(LANES), by_row(LANES)],
        jax.ShapeDtypeStruct((2 * rows, 3 * HD), BF16),
        by_row(3 * HD),
        (2,),
        "turn_back",
    )


def attended_grads(upstream, pieces, valid):
    rows = upstream.shape[0] // 2
    width = pieces[0].shape[0]

    def kernel(_, dy_ref, *refs):
        piece_refs, (valid_ref, out_ref) = refs[:4], refs[4:]
        total = dot(dy_ref[:, :width], piece_refs[0][...], ((1,), (0,)))
        for k in range(1, 4):
            cols = slice(k * width, (k + 1) * width)
            total = total + dot(dy_ref[:, cols], piece_refs[k][...], ((1,), (0,)))
        out_ref[...] = total.astype(BF16) * valid_ref[...].astype(BF16)

    def by_row(columns):
        return pl.BlockSpec((rows, columns), lambda s, z: (s, 0))

    return kernel_call(
        kernel,
        jnp.zeros((1,), jnp.int32),
        (upstream, *pieces, valid),
        [by_row(upstream.shape[1])]
        + [pl.BlockSpec((width, HD), lambda s, z: (0, 3))] * 4
        + [by_row(1)],
        jax.ShapeDtypeStruct((2 * rows, HD), BF16),
        by_row(HD),
        (2,),
        "attended_grads",
    )


def chances(query, keys, first, last, key_place):
    scores = []
    for part, place in zip(keys, key_place):
        score = dot(query, part, ((1,), (1,))) * (1.0 / math.sqrt(HD))
        scores.append(jnp.where((place >= first) & (place <= last), score, MASK_FLOOR))
    top = jnp.max(scores[0], axis=1, keepdims=True)
    for score in scores[1:]:
        top = jnp.maximum(top, jnp.max(score, axis=1, keepdims=True))
    exps = [jnp.exp(score - top) for score in scores]
    total = sum(jnp.sum(e, axis=1, keepdims=True) for e in exps)
    return [e / total for e in exps]


def attention_specs(rows, parts):
    return (
        [pl.BlockSpec((rows, HD), lambda n, s: (n + s[0], 0))]
        + [pl.BlockSpec((None, rows, 2 * HD), lambda n, s: (n + s[0], 0, 0))] * parts
        + [pl.BlockSpec((None, rows, 2), lambda n, s: (n + s[0], 0, 0))]
        + [pl.BlockSpec((None, 1, rows), lambda n, s: (n + s[0], 0, 0))] * parts
    )


def attend(queries, both, row_places, key_places, valid):
    rows = queries.shape[0] // 2
    parts = len(both)

    def kernel(_, q_ref, *refs):
        both_refs, place_ref, key_refs = refs[:parts], refs[parts], refs[parts + 1 : 2 * parts + 1]
        valid_ref, out_ref = refs[2 * parts + 1 :]
        step = rows // 2
        for c in range(2):
            at = slice(c * step, (c + 1) * step)
            probs = chances(
                q_ref[at, :],
                [ref[:, :HD] for ref in both_refs],
                place_ref[at, 0:1],
                place_ref[at, 1:2],
                [ref[...] for ref in key_refs],
            )
            total = 0.0
            for p, ref in zip(probs, both_refs):
                total = total + dot(p.astype(BF16), ref[:, HD:], ((1,), (0,)))
            out_ref[at, :] = (total * valid_ref[at, :]).astype(BF16)

    return kernel_call(
        kernel,
        jnp.zeros((1,), jnp.int32),
        (queries, *both, row_places, *key_places, valid),
        attention_specs(rows, parts) + [pl.BlockSpec((rows, 1), lambda n, s: (n, 0))],
        jax.ShapeDtypeStruct(queries.shape, BF16),
        pl.BlockSpec((rows, HD), lambda n, s: (n, 0)),
        (2,),
        "attend",
    )


def attend_back(s, queries, both, row_places, key_places, attended_grad, into=()):
    rows = queries.shape[0] // 2
    scale = 1.0 / math.sqrt(HD)

    def kernel(_, q_ref, own_ref, far_ref, place_ref, own_key_ref, far_key_ref, up_ref, *outs):
        query_ref, kept_ref, given_ref = outs[-3:]
        step = rows // 2
        sums = [[0.0, 0.0], [0.0, 0.0]]
        for c in range(2):
            at = slice(c * step, (c + 1) * step)
            query, up = q_ref[at, :], up_ref[at, :]
            probs = chances(
                query,
                [own_ref[:, :HD], far_ref[:, :HD]],
                place_ref[at, 0:1],
                place_ref[at, 1:2],
                [own_key_ref[...], far_key_ref[...]],
            )
            grads = [dot(up, ref[:, HD:], ((1,), (1,))) for ref in (own_ref, far_ref)]
            delta = sum(jnp.sum(p * g, axis=1, keepdims=True) for p, g in zip(probs, grads))
            total = 0.0
            for n, ref in enumerate((own_ref, far_ref)):
                score_grad = (probs[n] * (grads[n] - delta)).astype(BF16)
                total = total + dot(score_grad, ref[:, :HD], ((1,), (0,)))
                sums[n][0] = sums[n][0] + dot(score_grad, query, ((0,), (0,)))
                sums[n][1] = sums[n][1] + dot(probs[n].astype(BF16), up, ((0,), (0,)))
            query_ref[at, :] = total * scale
        for n, ref in enumerate((kept_ref, given_ref)):
            ref[:, :HD] = (sums[n][0] * scale).astype(ref.dtype)
            ref[:, HD:] = sums[n][1].astype(ref.dtype)

    both_spec = pl.BlockSpec((None, rows, 2 * HD), lambda n, s: (n + s[0], 0, 0))
    row_spec = pl.BlockSpec((rows, HD), lambda n, s: (n + s[0], 0))
    arrays = (queries, *both, row_places, *key_places, attended_grad)
    return kernel_call(
        kernel,
        jnp.full((1,), s, jnp.int32),
        (*arrays, *into),
        attention_specs(rows, 2) + [row_spec] + [pl.BlockSpec(memory_space=pl.ANY)] * len(into),
        [
            jax.ShapeDtypeStruct(queries.shape, F32),
            jax.ShapeDtypeStruct(both[0].shape, F32),
            jax.ShapeDtypeStruct(both[0].shape, BF16),
        ],
        [row_spec, both_spec, both_spec],
        (1,),
        "attend_back",
        aliases={1 + len(arrays) + n: n for n in range(len(into))},
    )


def pack_attention(qkv_weight, dense_weight, halves):
    rows = qkv_weight.shape[1]
    count = halves.shape[0]

    def kernel(h_ref, qkv_ref, dense_ref, *out_refs):
        for n in range(count):
            for t in range(3):
                out_refs[n][:, t * HD : (t + 1) * HD] = qkv_ref[t, :, aligned(h_ref[n], HD)]
            out_refs[n][:, 3 * HD :] = dense_ref[:, aligned(h_ref[n], HD)]

    def spec(columns):
        return pl.BlockSpec((rows // 2, columns), lambda r, h: (r, 0))

    return kernel_call(
        kernel,
        halves,
        (qkv_weight, dense_weight),
        [pl.BlockSpec((3, rows // 2, 2 * HD), lambda r, h: (0, r, 0)), spec(2 * HD)],
        [jax.ShapeDtypeStruct((rows, 4 * HD), BF16)] * count,
        [spec(4 * HD)] * count,
        (2,),
        "pack_attention",
    )


class Rounds:
    def __init__(self):
        self.last = ()

    def __call__(self, *arrays):
        got = lax.optimization_barrier((*arrays, *self.last))[: len(arrays)]
        return got if len(arrays) > 1 else got[0]

    def done(self, *arrays):
        self.last = arrays
        return arrays if len(arrays) > 1 else arrays[0]

    def close(self, *arrays):
        self.last = (*self.last, *arrays)


def per_device(
    tokens,
    lengths,
    block_order,
    ln_gain,
    ln_bias,
    qkv_weight,
    qkv_bias,
    dense_weight,
    dense_bias,
    fc1_weight,
    fc1_bias,
    fc2_weight,
    fc2_bias,
    cotangent,
):
    me = lax.axis_index("fsdp")
    core = me % 2
    tp_index = lax.axis_index("tp").astype(jnp.int32)
    tp_size = lax.axis_size("tp")
    ctx_index = lax.axis_index("ctx")
    ctx_size = lax.axis_size("ctx")
    pairs = ctx_size == 2
    side = ctx_index % 2 if pairs else 0 * ctx_index
    shard = ln_gain.shape[0]
    row_count = tokens.shape[1]
    block_rows = row_count // 2
    score_scale = 1.0 / math.sqrt(HD)
    order = jnp.stack([me, me ^ 1, me ^ (2 + side), me ^ (3 - side)]).astype(jnp.int32)
    near_bits, far_bits = ((2, 3), (3, 2)) if pairs else ((2, 2), (3, 3))
    inputs_low, upstream_low = tokens[0], cotangent[0]
    then = Rounds()

    halves = jnp.stack([core, 1 - core, core ^ side, core ^ 1 ^ side]).astype(jnp.int32)

    def relayed(name):
        return RELAY[name] and pairs

    def four(weight, name):
        return [half_of(weight, halves[n], 1) for n in range(3 if relayed(name) else 4)]

    def far_of(name, near, packs):
        return ctx_pair(near) if relayed(name) else fsdp_permute(then(packs[3]), far_bits)

    def joined(pieces):
        return jnp.concatenate(pieces, axis=0)

    seq_count, slots = lengths.shape[1], block_order.shape[1]
    vectors = jnp.concatenate(
        [
            v.astype(F32)
            for v in (ln_gain, ln_bias, dense_bias, fc2_bias, lengths[0], block_order[0])
        ]
    )
    then.done(vectors)
    vectors = [
        vectors,
        swap(vectors, 1),
        fsdp_permute(vectors, near_bits),
        fsdp_permute(vectors, far_bits),
    ]
    inputs_other = swap(inputs_low, 1)
    fc1_packs = four(then(fc1_weight), "fc1")
    then.done(*fc1_packs)
    fc1_near = fsdp_permute(fc1_packs[2], near_bits)
    packs = pack_attention(
        qkv_weight.transpose(1, 0, 2), then(dense_weight), halves[: 3 if relayed("attention") else 4]
    )
    then.done(*packs)
    then.close(inputs_other, *vectors[1:])

    def over_features(n):
        return jnp.concatenate([v[n * shard : (n + 1) * shard] for v in vectors])[None, :]

    norm_gain, norm_bias = over_features(0), over_features(1)
    out_bias = over_features(2) + over_features(3)
    their_layout = vectors[1][4 * shard :].astype(jnp.int32)

    upstream_other = swap(then(upstream_low), 1)
    fc1_core, attention_core = swap(then(fc1_packs[1]), 1), swap(then(packs[1]), 1)
    normed = then.done(frame_rows(inputs_low, then(inputs_other), order, (norm_gain, norm_bias)))
    fc2_packs = four(then(fc2_weight), "fc2")
    then.done(*fc2_packs)
    layouts = [
        (then(lengths[0]), block_order[0]),
        (their_layout[:seq_count], their_layout[seq_count:]),
    ]
    local_slots = ctx_index * 2 + jnp.arange(2, dtype=jnp.int32)
    if pairs:
        key_slots = jnp.concatenate([local_slots, (1 - ctx_index) * 2 + jnp.arange(2)])
    else:
        key_slots = jnp.arange(slots, dtype=jnp.int32)
    allowed, valid, positions, row_places, key_places = [], [], [], [], []
    for lengths_row, order_row in layouts:
        local_packed = packed_rows(order_row, local_slots, block_rows)
        key_packed = packed_rows(order_row, key_slots, block_rows)
        segment, position = place_rows(local_packed, lengths_row)
        key_segment = place_rows(key_packed, lengths_row)[0]
        allowed.append(
            (segment[:, None] == key_segment[None, :])
            & (key_packed[None, :] <= local_packed[:, None])
        )
        valid.append((segment < seq_count).astype(F32)[:, None])
        positions.append(position)
        row_places.append(jnp.stack([local_packed - position, local_packed], axis=1))
        key_places.append(key_packed[None, :])
    cosine_table, sine_table = rotation_tables(jnp.concatenate(positions))
    valid = jnp.concatenate(valid)
    upstream_sum = jnp.sum(upstream_low.astype(F32), axis=0, keepdims=True)
    row_places, key_places = jnp.stack(row_places), jnp.stack(key_places)
    upstream_near, upstream_far = [
        jnp.concatenate(
            [lax.dynamic_slice_in_dim(upstream_sum, order[k] * shard, shard, axis=1) for k in blocks],
            axis=1,
        )
        for blocks in ((0, 1), (2 + side, 3 - side))
    ]
    then.done(cosine_table, sine_table, valid, upstream_near, upstream_far, row_places, key_places, *fc2_packs)
    then.close(upstream_other, fc1_core, attention_core, fc1_near)

    attention_near = fsdp_permute(then(packs[2]), near_bits)
    fc1_far = far_of("fc1", then(fc1_near), fc1_packs)
    fc2_core = swap(then(fc2_packs[1]), 1)
    upstream = then.done(frame_rows(upstream_low, then(upstream_other), order))
    fc1_pieces = [fc1_packs[0], fc1_core, fc1_near, fc1_far]
    then.close(attention_near, fc1_far, fc2_core)

    def grad_block(k, *products, kind=BF16):
        parts = []
        for left, right in products:
            rows = lax.dynamic_slice_in_dim(left, k * shard, shard, axis=1)
            parts.append(dot(rows, right, ((0,), (0,))).astype(kind))
        return jnp.concatenate(parts, axis=1)

    def grad_blocks(*products):
        far = grad_block(2 + side, *products)
        rest = [grad_block(k, *products) for k in (3 - side, 1)]
        return (far, *rest, grad_block(0, *products, kind=F32))

    def add_mine(own, far):
        return then.done((own + then(far).astype(F32)).astype(BF16))

    def add_theirs(near, farther):
        return then.done((near.astype(F32) + then(farther).astype(F32)).astype(BF16))

    def placed(mine, theirs, attention=False):
        parts = then(*mine, *theirs)
        return then.done(*place_grad(parts, core, attention))

    fc2_near = fsdp_permute(then(fc2_packs[2]), near_bits)
    attention_far = far_of("attention", then(attention_near), packs)
    attention = [packs[0], attention_core, attention_near, attention_far]
    pre_act = dot(then(normed), joined(fc1_pieces), ((1,), (0,)))
    pre_act = pre_act + half_of(fc1_bias, core, 0).astype(F32)[None, :]
    normal_cdf = 0.5 * (1.0 + lax.erf(pre_act * (1.0 / math.sqrt(2.0))))
    density = jnp.exp(-0.5 * pre_act * pre_act) * (1.0 / math.sqrt(2.0 * math.pi))
    hidden = (pre_act * normal_cdf).astype(BF16)
    slope = normal_cdf + pre_act * density
    hidden, slope = then.done(hidden, slope)
    fc2_blocks = then.done(*grad_blocks((then(upstream), hidden)))
    then.close(fc2_near, attention_far)

    def row_block_of(index):
        place, bit = 0 * index, 1
        while bit < tp_size:
            place = place * 2 + (index // bit) % 2
            bit *= 2
        return place

    def flips_to_places(flips):
        return jnp.stack([row_block_of(tp_index ^ f) for f in flips]).astype(jnp.int32)

    fc2_far = far_of("fc2", then(fc2_near), fc2_packs)
    fc2_pieces = [fc2_packs[0], fc2_core, fc2_near, fc2_far]
    fc2_grad_near = swap(then(fc2_blocks[2]), 1)
    qkv_bias_own = half_of(qkv_bias, core, 1).astype(F32).reshape(1, 3 * HD)
    queries, both_local = then.done(
        *project(then(normed), attention, qkv_bias_own, cosine_table, sine_table)
    )
    both_local = both_local.reshape(2, row_count, 2 * HD)
    if pairs:
        both_other = ctx_pair(both_local)
    else:
        both_other = lax.all_gather(both_local, "ctx", axis=1, tiled=True)
    attended_grad = then.done(attended_grads(then(upstream), attention, valid))
    then.close(fc2_far, fc2_grad_near)

    fc2_grad_far = swap(then(fc2_blocks[0]), 2)
    hidden_grad = dot(then(upstream), joined(fc2_pieces), ((1,), (0,)))
    pre_grad = then.done((hidden_grad * slope).astype(BF16))
    both_other = then(both_other)
    attended, probs_all = [], []
    if pairs:
        both = (both_local, both_other)
        key_parts = key_places[:, :, :row_count], key_places[:, :, row_count:]
        attended = then.done(attend(queries, both, row_places, key_parts, valid))
    else:
        for s in range(2):
            rows = slice(s * row_count, (s + 1) * row_count)
            keys, values = both_other[s, :, :HD], both_other[s, :, HD:]
            scores = dot(queries[rows], keys, ((1,), (1,))) * score_scale
            scores = jnp.where(allowed[s], scores, MASK_FLOOR)
            exp_scores = jnp.exp(scores - jnp.max(scores, axis=1, keepdims=True))
            probs = exp_scores / jnp.sum(exp_scores, axis=1, keepdims=True)
            probs_all.append(probs)
            attended.append(dot(probs.astype(BF16), values, ((1,), (0,))))
        attended = then.done((jnp.concatenate(attended) * valid).astype(BF16))
    hidden_size = hidden.shape[1]
    second = (hidden, fc2_pieces, 0, hidden_size)
    theirs = then.done(share_rows((attended, attention, 3, HD), second, row_count))
    then.close(fc2_grad_far)

    def attention_grads(s, into=()):
        if pairs:
            return then.done(
                *attend_back(s, queries, both, row_places, key_parts, then(attended_grad), into)
            )
        rows = slice(s * row_count, (s + 1) * row_count)
        keys, values = both_other[s, :, :HD], both_other[s, :, HD:]
        probs, head_grad = probs_all[s], then(attended_grad[rows])
        prob_grad = dot(head_grad, values, ((1,), (1,)))
        row_delta = jnp.sum(probs * prob_grad, axis=1, keepdims=True)
        score_grad = (probs * (prob_grad - row_delta)).astype(BF16)
        query_piece = dot(score_grad, keys, ((1,), (0,))) * score_scale
        key_piece = dot(score_grad, queries[rows], ((0,), (0,))) * score_scale
        value_piece = dot(probs.astype(BF16), head_grad, ((0,), (0,)))
        return then.done(query_piece, jnp.concatenate([key_piece, value_piece], axis=1))

    low = tp_index % 2

    def halve_on(kept, got, bit, row_block):
        while bit < tp_size:
            digit = (tp_index // bit) % 2
            given, kept = then.done(*halve_rows(digit, kept, got))
            got, row_block, bit = tp_pair(given, bit), row_block * 2 + digit, bit * 2
        return kept, got, row_block

    def double_up(part):
        pieces, flips, bit = [part], [0], tp_size // 2
        while bit > 1:
            pieces += [tp_pair(p, bit) for p in pieces]
            flips += [f ^ bit for f in flips]
            bit //= 2
        return pieces, flips + [f ^ 1 for f in flips]

    def fc1_block(k, kind=BF16):
        return weight_grad(k, shard, [(then(normed), pre_grad)], kind)

    fc2_grad_farther = swap(then(fc2_blocks[1]), 3)
    theirs = swap(then(theirs), 1)
    fc2_mine = ctx_terms(add_mine(fc2_blocks[3], fc2_grad_far))
    grads_first = attention_grads(0)
    first = (then(attended), attention, 3, HD)
    given, kept = then.done(*share_rows(first, second, row_count, theirs, low))
    fc1_far_block = then.done(grad_block(2 + side, (then(normed), pre_grad)))
    then.close(fc2_grad_farther)

    fc1_grad_far = swap(then(fc1_far_block), 2)
    out_got = tp_pair(then(given), 1)
    if pairs:
        query_grad, both_grad, both_given = attention_grads(1, grads_first)
        both_got = ctx_pair(both_given)
    else:
        grads_second = attention_grads(1)
        both_grad = jnp.stack([grads_first[1], grads_second[1]])
        query_grad = jnp.concatenate([grads_first[0], grads_second[0]])
        both_got = jnp.zeros((2, row_count, 2 * HD), BF16)
        both_grad = lax.psum_scatter(both_grad, "ctx", scatter_dimension=1, tiled=True)
        query_grad, both_grad = then.done(query_grad, both_grad)
    fc1_near_block = then.done(grad_block(1, (then(normed), pre_grad)))
    fc1_grad_near = swap(fc1_near_block, 1)
    fc1_farther_block = then.done(grad_block(3 - side, (then(normed), pre_grad)))
    fc1_own_block = then.done(fc1_block(0, F32))
    then.close(fc1_grad_far, out_got, fc2_mine[1], fc1_grad_near)

    fc1_grad_farther = swap(then(fc1_farther_block), 3)
    out_kept, out_got, out_block = halve_on(then(kept), out_got, 2, low)
    fc2_theirs = ctx_terms(add_theirs(fc2_grad_near, fc2_grad_farther))
    proj_grad = then.done(
        turn_back(then(query_grad), both_grad, both_got, cosine_table, sine_table)
    )
    second = (pre_grad, fc1_pieces, 0, hidden_size)
    theirs = then.done(share_rows((proj_grad, attention, 0, 3 * HD), second, row_count))

    def attention_block(k, kind=BF16):
        return weight_grad(k, shard, [(then(normed), proj_grad), (upstream, attended)], kind)

    far_block = then.done(attention_block(2 + side))
    then.close(fc1_grad_farther, out_got, fc2_theirs[1])

    attention_grad_far = swap(then(far_block), 2)
    theirs = swap(then(theirs), 1)
    out_part = then.done(
        finish_output(order, out_block, then(out_kept), out_got, inputs_low, out_bias)
    )
    out_pieces, flips = double_up(out_part)
    out_late = [tp_pair(out_part, 1)]
    fc1_mine = ctx_terms(add_mine(fc1_own_block, fc1_grad_far))
    first = (then(proj_grad), attention, 0, 3 * HD)
    given, kept = then.done(*share_rows(first, second, row_count, theirs, low))
    farther_block = then.done(attention_block(3 - side))
    then.close(attention_grad_far, out_late[0], *out_pieces[1:], fc1_mine[1])

    attention_grad_farther = swap(then(farther_block), 3)
    got = tp_pair(then(given), 1)
    fc1_theirs = ctx_terms(add_theirs(fc1_grad_near, fc1_grad_farther))
    norm_near, norm_far = then.done(*norm_grads(order, low, side, then(inputs_low), given, kept))
    sums, sums_given = then.done(
        *pack_sums(
            (norm_near, norm_far), (upstream_near, upstream_far), then(pre_grad), proj_grad
        )
    )
    sums_got = swap(sums_given, 2)
    near_block = then.done(attention_block(1))
    own_block = then.done(attention_block(0, kind=F32))
    attention_mine = add_mine(own_block, attention_grad_far)
    then.close(attention_grad_farther, got, fc1_theirs[1], sums_got)

    attention_mine = ctx_terms(then(attention_mine))
    kept, got, row_block = halve_on(then(kept), got, 2, low)
    out_late += [tp_pair(p, 1) for p in then(out_pieces[0], *out_pieces[1:])[1:]]
    sums = then(sums) + sums_got
    norm_sums, other_sums = sums[:2], sums[2:]
    norm_sums = norm_sums + tp_pair(norm_sums, 1)
    attention_grad_near = swap(then(near_block), 1)
    fc2_out = placed(fc2_mine, fc2_theirs)
    then.close(got, norm_sums, attention_mine[1], attention_grad_near, *out_late[1:])

    input_part = then.done(
        finish_input_grad(order, row_block, then(kept), got, inputs_low, upstream_low, norm_gain)
    )
    pieces, _ = double_up(input_part)
    late = [tp_pair(input_part, 1)]
    bit = 2
    while bit < tp_size:
        norm_sums = norm_sums + tp_pair(then(norm_sums), bit)
        bit *= 2
    attention_theirs = ctx_terms(add_theirs(attention_grad_near, attention_grad_farther))
    fc1_out = placed(fc1_mine, fc1_theirs)
    output = then.done(gather_rows(then(*out_pieces, *out_late), flips_to_places(flips), BF16))
    then.close(*pieces[1:], late[0], norm_sums, attention_theirs[1])

    late += [tp_pair(p, 1) for p in then(*pieces, output)[1 : len(pieces)]]
    sums = sum(ctx_terms(jnp.concatenate([then(norm_sums), other_sums])))
    qkv_out, dense_out = placed(attention_mine, attention_theirs, True)
    then.close(*late[1:], sums)

    sums = then(sums)
    other_core = swap(sums, 1)
    vector_sums = sums[:3, :shard] + other_core[:3, shard : 2 * shard]

    def column_sums(packed):
        return packed[3, :hidden_size], packed[4, : 3 * HD].reshape(3, HD)

    input_grad = gather_rows(then(*pieces, *late), flips_to_places(flips), F32)

    def in_order(mine, other, axis):
        return jnp.where(
            core == 0,
            jnp.concatenate([mine, other], axis=axis),
            jnp.concatenate([other, mine], axis=axis),
        )

    fc1_bias_grad, qkv_bias_grad = [
        in_order(mine, other, axis)
        for axis, mine, other in zip((0, 1), column_sums(sums), column_sums(other_core))
    ]
    return (
        output[None],
        input_grad[None],
        vector_sums[0],
        vector_sums[1],
        qkv_out.transpose(1, 0, 2),
        qkv_bias_grad,
        dense_out,
        vector_sums[2],
        fc1_out,
        fc1_bias_grad,
        fc2_out,
        vector_sums[2],
    )


def solution(mesh):
    placed = (
        P("fsdp", "ctx", None),
        P("fsdp", None),
        P("fsdp", None),
        P("fsdp"),
        P("fsdp"),
        P("fsdp", None, "tp"),
        P(None, "tp"),
        P("fsdp", "tp"),
        P("fsdp"),
        P("fsdp", "tp"),
        P("tp"),
        P("fsdp", "tp"),
        P("fsdp"),
        P("fsdp", "ctx", None),
    )
    return jax.shard_map(
        per_device,
        mesh=mesh,
        in_specs=placed,
        out_specs=(
            P("fsdp", "ctx", None),
            P("fsdp", "ctx", None),
            P("fsdp"),
            P("fsdp"),
            P("fsdp", None, "tp"),
            P(None, "tp"),
            P("fsdp", "tp"),
            P("fsdp"),
            P("fsdp", "tp"),
            P("tp"),
            P("fsdp", "tp"),
            P("fsdp"),
        ),
        check_vma=False,
    )
```

```python
import math

import jax
import jax.numpy as jnp
from jax import lax
from jax.experimental import pallas as pl
from jax.experimental.pallas import tpu as pltpu
from jax.sharding import PartitionSpec as P

HD = 256
ROT = 64


NORM_EPSILON = 1e-05
MASK_FLOOR = -1000000000.0
F32 = jnp.float32
BF16 = jnp.bfloat16
LANES = 128
RELAY = {"attention": True, "fc1": True, "fc2": False}


def rotation_tables(position):
    half = ROT // 2
    frequency = jnp.exp(jnp.arange(half, dtype=F32) * (-2.0 * math.log(10000.0) / ROT))
    angles = position.astype(F32)[:, None] * frequency[None, :]
    cosine, sine = jnp.cos(angles), jnp.sin(angles)
    rest = (position.shape[0], LANES - ROT)
    return (
        jnp.concatenate([cosine, cosine, jnp.ones(rest, F32)], axis=1),
        jnp.concatenate([-sine, sine, jnp.zeros(rest, F32)], axis=1),
    )


def packed_rows(order_row, slots, block_rows):
    selector = slots[:, None] == jnp.arange(order_row.shape[0], dtype=jnp.int32)[None, :]
    source_block = jnp.sum(jnp.where(selector, order_row[None, :], 0), axis=1, dtype=jnp.int32)
    within = jnp.arange(block_rows, dtype=jnp.int32)
    return (source_block[:, None] * block_rows + within[None, :]).reshape(-1)


def place_rows(packed_at, lengths_row):
    seq_ends = jnp.cumsum(lengths_row, dtype=jnp.int32)
    passed = packed_at[:, None] >= seq_ends[None, :]
    segment = jnp.sum(passed.astype(jnp.int32), axis=1, dtype=jnp.int32)
    before = jnp.sum(jnp.where(passed, lengths_row[None, :], 0), axis=1, dtype=jnp.int32)
    return (segment, packed_at - before)


def dot(a, b, contract):
    return lax.dot_general(a, b, (contract, ((), ())), preferred_element_type=F32)


def fsdp_permute(x, bits):
    size, lanes = lax.axis_size("fsdp"), lax.axis_size("ctx")
    perm = [
        (f * lanes + x, (f ^ bits[x % 2]) * lanes + x) for f in range(size) for x in range(lanes)
    ]
    return lax.ppermute(x, ("fsdp", "ctx"), perm)


def swap(x, bit):
    return fsdp_permute(x, (bit, bit))


def ctx_pair(x):
    return lax.ppermute(x, "ctx", [(0, 1), (1, 0)])


def ctx_terms(x):
    if lax.axis_size("ctx") == 2:
        return x, ctx_pair(x)
    return lax.psum(x.astype(F32), "ctx"), jnp.zeros_like(x)


def tp_pair(x, bit):
    return lax.ppermute(x, "tp", [(i, i ^ bit) for i in range(lax.axis_size("tp"))])


def half_of(x, which, axis):
    size = x.shape[axis] // 2
    return lax.dynamic_slice_in_dim(x, which * size, size, axis=axis)


def kernel_call(body, scalars, arrays, in_specs, out_shape, out_specs, grid, name, scratch=(), aliases=None):
    return pl.pallas_call(
        body,
        out_shape=out_shape,
        grid_spec=pltpu.PrefetchScalarGridSpec(
            num_scalar_prefetch=1,
            grid=grid,
            in_specs=in_specs,
            out_specs=out_specs,
            scratch_shapes=scratch,
        ),
        input_output_aliases=aliases or {},
        cost_estimate=pl.CostEstimate(flops=0, transcendentals=0, bytes_accessed=0),
        name=name,
    )(scalars, *arrays)


def aligned(index, size):
    return pl.ds(pl.multiple_of(index * size, size), size)


def frame_rows(own, other, order, norm=None):
    rows, columns = own.shape
    width, step = columns // 4, rows // 2

    def kernel(order_ref, own_ref, other_ref, *refs):
        gain_ref, bias_ref, out_ref, wide_ref = refs if norm else (None, None, refs[0], None)
        for s, ref in enumerate((own_ref, other_ref)):
            if norm:
                x = ref[...].astype(F32)
                x = x - jnp.mean(x, axis=1, keepdims=True)
                variance = jnp.mean(x * x, axis=1, keepdims=True)
                wide_ref[...] = x * lax.rsqrt(variance + NORM_EPSILON)
            for k in range(4):
                to = slice(k * width, (k + 1) * width)
                at = aligned(order_ref[k], width)
                if norm:
                    out_ref[s, :, to] = (
                        wide_ref[:, at] * gain_ref[:, to] + bias_ref[:, to]
                    ).astype(BF16)
                else:
                    out_ref[s, :, to] = ref[:, at]

    row_spec = pl.BlockSpec((step, columns), lambda r, o: (r, 0))
    vector_spec = pl.BlockSpec((1, columns), lambda r, o: (0, 0))
    out = kernel_call(
        kernel,
        order,
        (own, other, *(norm or ())),
        [row_spec, row_spec] + ([vector_spec, vector_spec] if norm else []),
        jax.ShapeDtypeStruct((2, rows, columns), BF16),
        pl.BlockSpec((2, step, columns), lambda r, o: (0, r, 0)),
        (2,),
        "norm_rows" if norm else "frame_rows",
        scratch=[pltpu.VMEM((step, columns), F32)] if norm else (),
    )
    return out.reshape(2 * rows, columns)


def place_grad(parts, core, attention):
    rows, columns = parts[0].shape
    step = rows // 2

    def kernel(core_ref, a_ref, ax_ref, b_ref, bx_ref, *out_refs):
        for h, (u_ref, ux_ref) in enumerate(((a_ref, ax_ref), (b_ref, bx_ref))):
            total = u_ref[...].astype(F32) + ux_ref[...].astype(F32)
            place = core_ref[0] ^ h
            if attention:
                for t in range(3):
                    out_refs[0][t, :, aligned(place, HD)] = total[:, t * HD : (t + 1) * HD]
                out_refs[1][:, aligned(place, HD)] = total[:, 3 * HD :]
            else:
                out_refs[0][:, aligned(place, columns)] = total

    shapes = [(rows, 2 * columns)]
    specs = [pl.BlockSpec((step, 2 * columns), lambda r, c: (r, 0))]
    if attention:
        shapes = [(3, rows, 2 * HD), (rows, 2 * HD)]
        specs = [
            pl.BlockSpec((3, step, 2 * HD), lambda r, c: (0, r, 0)),
            pl.BlockSpec((step, 2 * HD), lambda r, c: (r, 0)),
        ]
    return kernel_call(
        kernel,
        core[None],
        parts,
        [pl.BlockSpec((step, columns), lambda r, c: (r, 0))] * 4,
        [jax.ShapeDtypeStruct(shape, F32) for shape in shapes],
        specs,
        (2,),
        "place_grad",
    )


def weight_grad(block, shard, products, kind):
    step = shard // 2
    widths = [right.shape[1] for _, right in products]

    def kernel(_, *refs):
        at = 0
        for n, width in enumerate(widths):
            left_ref, right_ref = refs[2 * n : 2 * n + 2]
            total = dot(left_ref[...], right_ref[...], ((0,), (0,)))
            refs[-1][:, at : at + width] = total.astype(kind)
            at += width

    specs = []
    for left, right in products:
        specs.append(pl.BlockSpec((left.shape[0], step), lambda n, k: (0, 2 * k[0] + n)))
        specs.append(pl.BlockSpec(right.shape, lambda n, k: (0, 0)))
    return kernel_call(
        kernel,
        jnp.asarray(block, jnp.int32)[None],
        [a for product in products for a in product],
        specs,
        jax.ShapeDtypeStruct((shard, sum(widths)), kind),
        pl.BlockSpec((step, sum(widths)), lambda n, k: (n, 0)),
        (2,),
        "weight_grad",
    )


def share_rows(first, second, rows, theirs=None, low=None):
    width = first[1][0].shape[0]
    own = theirs is not None
    at = 0 if own else 1
    half = rows // 2

    def kernel(low_ref, f_ref, s_ref, *refs):
        f_refs, s_refs, refs = refs[:4], refs[4:8], refs[8:]
        for n in range(2):

            @pl.when(pl.program_id(0) == n)
            def _(n=n):
                for m in range(2):
                    k = 2 * n + m
                    total = dot(f_ref[...], f_refs[k][...], ((1,), (1,)))
                    total = total + dot(s_ref[...], s_refs[k][...], ((1,), (1,)))
                    if not own:
                        refs[0][:, (1 - m) * width : (2 - m) * width] = total.astype(BF16)
                        continue
                    theirs_ref, given_ref, kept_ref, all_ref = refs
                    to = slice(m * width, (m + 1) * width)
                    all_ref[...] = (total + theirs_ref[:, to].astype(F32)).astype(BF16)
                    given_ref[:, to] = all_ref[aligned(1 - low_ref[0], half), :]
                    kept_ref[:, to] = all_ref[aligned(low_ref[0], half), :]

    arrays, in_specs = [], []
    for acts, _, _, size in (first, second):
        arrays.append(acts)
        in_specs.append(pl.BlockSpec((rows, size), lambda n, b: (at, 0)))
    for _, pieces, block, size in (first, second):
        arrays += pieces
        in_specs += [pl.BlockSpec((width, size), lambda n, b, block=block: (0, block))] * 4
    out_shape = jax.ShapeDtypeStruct((rows, 4 * width), BF16)
    out_spec = pl.BlockSpec((rows, 2 * width), lambda n, b: (0, n))
    scratch = ()
    if own:
        arrays.append(theirs)
        in_specs.append(out_spec)
        out_shape = [jax.ShapeDtypeStruct((half, 4 * width), BF16)] * 2
        out_spec = [pl.BlockSpec((half, 2 * width), lambda n, b: (0, n))] * 2
        scratch = [pltpu.VMEM((rows, width), BF16)]
    return kernel_call(
        kernel,
        low[None] if own else jnp.zeros((1,), jnp.int32),
        arrays,
        in_specs,
        out_shape,
        out_spec,
        (2,),
        "share_rows",
        scratch=scratch,
    )


def finish_output(order, row_block, kept, got, inputs, out_bias):
    rows, columns = kept.shape
    width, steps = columns // 4, 1
    step = rows // steps

    def kernel(s_ref, kept_ref, got_ref, x_ref, bias_ref, out_ref):
        for k in range(4):
            cols, at = slice(k * width, (k + 1) * width), aligned(s_ref[k], width)
            total = kept_ref[:, cols] + got_ref[:, cols].astype(F32)
            out_ref[:, at] = (x_ref[:, at].astype(F32) + total + bias_ref[:, cols]).astype(BF16)

    spec = pl.BlockSpec((step, columns), lambda i, s: (i, 0))
    return kernel_call(
        kernel,
        jnp.concatenate([order, row_block[None]]),
        (kept, got, inputs, out_bias),
        [
            spec,
            spec,
            pl.BlockSpec((step, columns), lambda i, s: (s[4] * steps + i, 0)),
            pl.BlockSpec((1, columns), lambda i, s: (0, 0)),
        ],
        jax.ShapeDtypeStruct((rows, columns), BF16),
        spec,
        (steps,),
        "finish_output",
    )


def finish_input_grad(order, row_block, kept, got, inputs, upstream, norm_gain):
    rows, columns = kept.shape
    width, steps = columns // 4, 1
    step = rows // steps

    def kernel(s_ref, kept_ref, got_ref, x_ref, dy_ref, gain_ref, out_ref, std_ref):
        x = x_ref[...].astype(F32)
        x = x - jnp.mean(x, axis=1, keepdims=True)
        inverse = lax.rsqrt(jnp.mean(x * x, axis=1, keepdims=True) + NORM_EPSILON)
        std_ref[...] = x * inverse
        mean_scaled = jnp.zeros((step, 1), F32)
        mean_product = jnp.zeros((step, 1), F32)

        def parts(k):
            cols, at = slice(k * width, (k + 1) * width), aligned(s_ref[k], width)
            total = kept_ref[:, cols] + got_ref[:, cols].astype(F32)
            return at, total * gain_ref[:, cols], std_ref[:, at]

        for k in range(4):
            _, scaled, standard = parts(k)
            mean_scaled += jnp.sum(scaled, axis=1, keepdims=True) / columns
            mean_product += jnp.sum(scaled * standard, axis=1, keepdims=True) / columns
        for k in range(4):
            at, scaled, standard = parts(k)
            change = inverse * (scaled - mean_scaled - standard * mean_product)
            out_ref[:, at] = (dy_ref[:, at].astype(F32) + change).astype(BF16)

    spec = pl.BlockSpec((step, columns), lambda i, s: (i, 0))
    rows_spec = pl.BlockSpec((step, columns), lambda i, s: (s[4] * steps + i, 0))
    return kernel_call(
        kernel,
        jnp.concatenate([order, row_block[None]]),
        (kept, got, inputs, upstream, norm_gain),
        [spec, spec, rows_spec, rows_spec, pl.BlockSpec((1, columns), lambda i, s: (0, 0))],
        jax.ShapeDtypeStruct((rows, columns), BF16),
        spec,
        (steps,),
        "finish_input_grad",
        scratch=[pltpu.VMEM((step, columns), F32)],
    )


def norm_grads(order, low, side, inputs, given, kept):
    rows, columns = inputs.shape
    width, step = columns // 4, rows // 2

    def kernel(order_ref, x_ref, given_ref, kept_ref, near_ref, far_ref, std_ref):
        x = x_ref[...].astype(F32)
        x = x - jnp.mean(x, axis=1, keepdims=True)
        std_ref[...] = x * lax.rsqrt(jnp.mean(x * x, axis=1, keepdims=True) + NORM_EPSILON)

        def add(share_ref, first):
            for k in range(4):
                cols = slice(k * width, (k + 1) * width)
                part = share_ref[:, cols].astype(F32)
                product = part * std_ref[:, aligned(order_ref[k], width)]
                sums = jnp.sum(product, axis=0, keepdims=True), jnp.sum(part, axis=0, keepdims=True)
                out_ref, at = near_ref, cols
                if k > 1:
                    out_ref, at = far_ref, aligned((k - 2) ^ order_ref[5], width)
                for n in range(2):
                    before = 0.0 if first else out_ref[n : n + 1, at]
                    out_ref[n : n + 1, at] = before + sums[n]

        @pl.when(pl.program_id(0) == 0)
        def _():
            add(given_ref, True)

        @pl.when(pl.program_id(0) == 1)
        def _():
            add(kept_ref, False)

    half_spec = pl.BlockSpec((step, columns), lambda r, o: (0, 0))
    return kernel_call(
        kernel,
        jnp.concatenate([order, low[None], side[None].astype(jnp.int32)]),
        (inputs, given, kept),
        [
            pl.BlockSpec((step, columns), lambda r, o: (r * o[4] + (1 - r) * (1 - o[4]), 0)),
            half_spec,
            half_spec,
        ],
        [jax.ShapeDtypeStruct((2, columns // 2), F32)] * 2,
        [pl.BlockSpec((2, columns // 2), lambda r, o: (0, 0))] * 2,
        (2,),
        "norm_grads",
        scratch=[pltpu.VMEM((step, columns), F32)],
    )


def halve_rows(digit, kept, got):
    rows, columns = kept.shape

    def kernel(_, a_ref, b_ref, c_ref, d_ref, given_ref, kept_ref):
        given_ref[...] = (a_ref[...].astype(F32) + b_ref[...].astype(F32)).astype(BF16)
        kept_ref[...] = c_ref[...].astype(F32) + d_ref[...].astype(F32)

    block = rows // 2, columns // 2
    leaves = pl.BlockSpec(block, lambda n, d: (1 - d[0], n))
    stays = pl.BlockSpec(block, lambda n, d: (d[0], n))
    out_spec = pl.BlockSpec(block, lambda n, d: (0, n))
    return kernel_call(
        kernel,
        digit[None],
        (kept, got, kept, got),
        [leaves, leaves, stays, stays],
        [jax.ShapeDtypeStruct((rows // 2, columns), kind) for kind in (BF16, F32)],
        [out_spec, out_spec],
        (2,),
        "halve_rows",
    )


def pack_sums(norm_sums, upstream_sums, pre_grad, proj_grad):
    wide = max(norm_sums[0].shape[1], pre_grad.shape[1], proj_grad.shape[1])
    step = pre_grad.shape[0] // 8

    def kernel(_, *refs):
        norm_refs, up_refs, grad_refs, out_refs = refs[:2], refs[2:4], refs[4:6], refs[6:]
        for out_ref in out_refs:
            out_ref[...] = jnp.zeros_like(out_ref)
        for norm_ref, up_ref, out_ref in zip(norm_refs, up_refs, out_refs):
            out_ref[0:2, : norm_ref.shape[1]] = norm_ref[...]
            out_ref[2:3, : up_ref.shape[1]] = up_ref[...]
        for n, ref in enumerate(grad_refs):
            total = jnp.zeros((1, ref.shape[1]), F32)
            for c in range(8):
                part = ref[c * step : (c + 1) * step, :].astype(F32)
                total = total + jnp.sum(part, axis=0, keepdims=True)
            for out_ref in out_refs:
                out_ref[3 + n : 4 + n, : ref.shape[1]] = total

    arrays = (*norm_sums, *upstream_sums, pre_grad, proj_grad)
    return kernel_call(
        kernel,
        jnp.zeros((1,), jnp.int32),
        arrays,
        [pl.BlockSpec(a.shape, lambda n, z: (0, 0)) for a in arrays],
        [jax.ShapeDtypeStruct((8, wide), F32)] * 2,
        [pl.BlockSpec((8, wide), lambda n, z: (0, 0))] * 2,
        (1,),
        "pack_sums",
    )


def gather_rows(pieces, places, dtype):
    size, (rows, columns) = len(pieces), pieces[0].shape

    def kernel(place_ref, *refs):
        for n in range(size):
            refs[-1][aligned(place_ref[n], rows), :] = refs[n][...].astype(dtype)

    return kernel_call(
        kernel,
        places,
        pieces,
        [pl.BlockSpec((rows, columns // 2), lambda c, p: (0, c))] * size,
        jax.ShapeDtypeStruct((rows * size, columns), dtype),
        pl.BlockSpec((rows * size, columns // 2), lambda c, p: (0, c)),
        (2,),
        "gather_rows",
    )


def turned(x, cosine, sine):
    lane = lax.broadcasted_iota(jnp.int32, x.shape, 1)
    half = ROT // 2
    partner = jnp.where(
        lane < half, pltpu.roll(x, x.shape[1] - half, axis=1), pltpu.roll(x, half, axis=1)
    )
    return x * cosine + partner * sine


def project(normed, pieces, bias, cosine, sine):
    rows = normed.shape[0] // 2
    width = pieces[0].shape[0]

    def kernel(_, x_ref, *refs):
        piece_refs, (bias_ref, cos_ref, sin_ref, q_ref, kv_ref) = refs[:4], refs[4:]
        total = dot(x_ref[:, :width], piece_refs[0][...], ((1,), (0,)))
        for k in range(1, 4):
            cols = slice(k * width, (k + 1) * width)
            total = total + dot(x_ref[:, cols], piece_refs[k][...], ((1,), (0,)))
        total = total + bias_ref[...]
        cosine, sine = cos_ref[...], sin_ref[...]
        for n, ref in enumerate((q_ref, kv_ref)):
            head = total[:, n * HD : (n + 1) * HD]
            ref[:, :LANES] = turned(head[:, :LANES], cosine, sine).astype(BF16)
            ref[:, LANES:HD] = head[:, LANES:].astype(BF16)
        kv_ref[:, HD:] = total[:, 2 * HD :].astype(BF16)

    def by_row(columns):
        return pl.BlockSpec((rows, columns), lambda s, z: (s, 0))

    return kernel_call(
        kernel,
        jnp.zeros((1,), jnp.int32),
        (normed, *pieces, bias, cosine, sine),
        [by_row(normed.shape[1])]
        + [pl.BlockSpec((width, 3 * HD), lambda s, z: (0, 0))] * 4
        + [pl.BlockSpec((1, 3 * HD), lambda s, z: (0, 0)), by_row(LANES), by_row(LANES)],
        [
            jax.ShapeDtypeStruct((2 * rows, HD), BF16),
            jax.ShapeDtypeStruct((2 * rows, 2 * HD), BF16),
        ],
        [by_row(HD), by_row(2 * HD)],
        (2,),
        "project",
    )


def turn_back(query_grad, kept, got, cosine, sine):
    rows = kept.shape[1]

    def kernel(_, q_ref, kept_ref, got_ref, cos_ref, sin_ref, out_ref):
        both = kept_ref[...] + got_ref[...].astype(F32)
        cosine, sine = cos_ref[...], -sin_ref[...]
        for n, head in enumerate((q_ref[...], both[:, :HD])):
            at = n * HD
            out_ref[:, at : at + LANES] = turned(head[:, :LANES], cosine, sine).astype(BF16)
            out_ref[:, at + LANES : at + HD] = head[:, LANES:].astype(BF16)
        out_ref[:, 2 * HD :] = both[:, HD:].astype(BF16)

    def by_row(columns):
        return pl.BlockSpec((rows, columns), lambda s, z: (s, 0))

    both_spec = pl.BlockSpec((None, rows, 2 * HD), lambda s, z: (s, 0, 0))
    return kernel_call(
        kernel,
        jnp.zeros((1,), jnp.int32),
        (query_grad, kept, got, cosine, sine),
        [by_row(HD), both_spec, both_spec, by_row(LANES), by_row(LANES)],
        jax.ShapeDtypeStruct((2 * rows, 3 * HD), BF16),
        by_row(3 * HD),
        (2,),
        "turn_back",
    )


def attended_grads(upstream, pieces, valid):
    rows = upstream.shape[0] // 2
    width = pieces[0].shape[0]

    def kernel(_, dy_ref, *refs):
        piece_refs, (valid_ref, out_ref) = refs[:4], refs[4:]
        total = dot(dy_ref[:, :width], piece_refs[0][...], ((1,), (0,)))
        for k in range(1, 4):
            cols = slice(k * width, (k + 1) * width)
            total = total + dot(dy_ref[:, cols], piece_refs[k][...], ((1,), (0,)))
        out_ref[...] = total.astype(BF16) * valid_ref[...].astype(BF16)

    def by_row(columns):
        return pl.BlockSpec((rows, columns), lambda s, z: (s, 0))

    return kernel_call(
        kernel,
        jnp.zeros((1,), jnp.int32),
        (upstream, *pieces, valid),
        [by_row(upstream.shape[1])]
        + [pl.BlockSpec((width, HD), lambda s, z: (0, 3))] * 4
        + [by_row(1)],
        jax.ShapeDtypeStruct((2 * rows, HD), BF16),
        by_row(HD),
        (2,),
        "attended_grads",
    )


def chances(query, keys, first, last, key_place):
    scores = []
    for part, place in zip(keys, key_place):
        score = dot(query, part, ((1,), (1,))) * (1.0 / math.sqrt(HD))
        scores.append(jnp.where((place >= first) & (place <= last), score, MASK_FLOOR))
    top = jnp.max(scores[0], axis=1, keepdims=True)
    for score in scores[1:]:
        top = jnp.maximum(top, jnp.max(score, axis=1, keepdims=True))
    exps = [jnp.exp(score - top) for score in scores]
    total = sum(jnp.sum(e, axis=1, keepdims=True) for e in exps)
    return [e / total for e in exps]


def attention_specs(rows, parts):
    return (
        [pl.BlockSpec((rows, HD), lambda n, s: (n + s[0], 0))]
        + [pl.BlockSpec((None, rows, 2 * HD), lambda n, s: (n + s[0], 0, 0))] * parts
        + [pl.BlockSpec((None, rows, 2), lambda n, s: (n + s[0], 0, 0))]
        + [pl.BlockSpec((None, 1, rows), lambda n, s: (n + s[0], 0, 0))] * parts
    )


def attend(queries, both, row_places, key_places, valid):
    rows = queries.shape[0] // 2
    parts = len(both)

    def kernel(_, q_ref, *refs):
        both_refs, place_ref, key_refs = refs[:parts], refs[parts], refs[parts + 1 : 2 * parts + 1]
        valid_ref, out_ref = refs[2 * parts + 1 :]
        step = rows // 2
        for c in range(2):
            at = slice(c * step, (c + 1) * step)
            probs = chances(
                q_ref[at, :],
                [ref[:, :HD] for ref in both_refs],
                place_ref[at, 0:1],
                place_ref[at, 1:2],
                [ref[...] for ref in key_refs],
            )
            total = 0.0
            for p, ref in zip(probs, both_refs):
                total = total + dot(p.astype(BF16), ref[:, HD:], ((1,), (0,)))
            out_ref[at, :] = (total * valid_ref[at, :]).astype(BF16)

    return kernel_call(
        kernel,
        jnp.zeros((1,), jnp.int32),
        (queries, *both, row_places, *key_places, valid),
        attention_specs(rows, parts) + [pl.BlockSpec((rows, 1), lambda n, s: (n, 0))],
        jax.ShapeDtypeStruct(queries.shape, BF16),
        pl.BlockSpec((rows, HD), lambda n, s: (n, 0)),
        (2,),
        "attend",
    )


def attend_back(s, queries, both, row_places, key_places, attended_grad, into=()):
    rows = queries.shape[0] // 2
    scale = 1.0 / math.sqrt(HD)

    def kernel(_, q_ref, own_ref, far_ref, place_ref, own_key_ref, far_key_ref, up_ref, *outs):
        query_ref, kept_ref, given_ref = outs[-3:]
        step = rows // 2
        sums = [[0.0, 0.0], [0.0, 0.0]]
        for c in range(2):
            at = slice(c * step, (c + 1) * step)
            query, up = q_ref[at, :], up_ref[at, :]
            probs = chances(
                query,
                [own_ref[:, :HD], far_ref[:, :HD]],
                place_ref[at, 0:1],
                place_ref[at, 1:2],
                [own_key_ref[...], far_key_ref[...]],
            )
            grads = [dot(up, ref[:, HD:], ((1,), (1,))) for ref in (own_ref, far_ref)]
            delta = sum(jnp.sum(p * g, axis=1, keepdims=True) for p, g in zip(probs, grads))
            total = 0.0
            for n, ref in enumerate((own_ref, far_ref)):
                score_grad = (probs[n] * (grads[n] - delta)).astype(BF16)
                total = total + dot(score_grad, ref[:, :HD], ((1,), (0,)))
                sums[n][0] = sums[n][0] + dot(score_grad, query, ((0,), (0,)))
                sums[n][1] = sums[n][1] + dot(probs[n].astype(BF16), up, ((0,), (0,)))
            query_ref[at, :] = total * scale
        for n, ref in enumerate((kept_ref, given_ref)):
            ref[:, :HD] = (sums[n][0] * scale).astype(ref.dtype)
            ref[:, HD:] = sums[n][1].astype(ref.dtype)

    both_spec = pl.BlockSpec((None, rows, 2 * HD), lambda n, s: (n + s[0], 0, 0))
    row_spec = pl.BlockSpec((rows, HD), lambda n, s: (n + s[0], 0))
    arrays = (queries, *both, row_places, *key_places, attended_grad)
    return kernel_call(
        kernel,
        jnp.full((1,), s, jnp.int32),
        (*arrays, *into),
        attention_specs(rows, 2) + [row_spec] + [pl.BlockSpec(memory_space=pl.ANY)] * len(into),
        [
            jax.ShapeDtypeStruct(queries.shape, F32),
            jax.ShapeDtypeStruct(both[0].shape, F32),
            jax.ShapeDtypeStruct(both[0].shape, BF16),
        ],
        [row_spec, both_spec, both_spec],
        (1,),
        "attend_back",
        aliases={1 + len(arrays) + n: n for n in range(len(into))},
    )


def pack_attention(qkv_weight, dense_weight, halves):
    rows = qkv_weight.shape[1]
    count = halves.shape[0]

    def kernel(h_ref, qkv_ref, dense_ref, *out_refs):
        for n in range(count):
            for t in range(3):
                out_refs[n][:, t * HD : (t + 1) * HD] = qkv_ref[t, :, aligned(h_ref[n], HD)]
            out_refs[n][:, 3 * HD :] = dense_ref[:, aligned(h_ref[n], HD)]

    def spec(columns):
        return pl.BlockSpec((rows // 2, columns), lambda r, h: (r, 0))

    return kernel_call(
        kernel,
        halves,
        (qkv_weight, dense_weight),
        [pl.BlockSpec((3, rows // 2, 2 * HD), lambda r, h: (0, r, 0)), spec(2 * HD)],
        [jax.ShapeDtypeStruct((rows, 4 * HD), BF16)] * count,
        [spec(4 * HD)] * count,
        (2,),
        "pack_attention",
    )


class Rounds:
    def __init__(self):
        self.last = ()

    def __call__(self, *arrays):
        got = lax.optimization_barrier((*arrays, *self.last))[: len(arrays)]
        return got if len(arrays) > 1 else got[0]

    def done(self, *arrays):
        self.last = arrays
        return arrays if len(arrays) > 1 else arrays[0]

    def close(self, *arrays):
        self.last = (*self.last, *arrays)


def per_device(
    tokens,
    lengths,
    block_order,
    ln_gain,
    ln_bias,
    qkv_weight,
    qkv_bias,
    dense_weight,
    dense_bias,
    fc1_weight,
    fc1_bias,
    fc2_weight,
    fc2_bias,
    cotangent,
):
    me = lax.axis_index("fsdp")
    core = me % 2
    tp_index = lax.axis_index("tp").astype(jnp.int32)
    tp_size = lax.axis_size("tp")
    ctx_index = lax.axis_index("ctx")
    ctx_size = lax.axis_size("ctx")
    pairs = ctx_size == 2
    side = ctx_index % 2 if pairs else 0 * ctx_index
    shard = ln_gain.shape[0]
    row_count = tokens.shape[1]
    block_rows = row_count // 2
    score_scale = 1.0 / math.sqrt(HD)
    order = jnp.stack([me, me ^ 1, me ^ (2 + side), me ^ (3 - side)]).astype(jnp.int32)
    near_bits, far_bits = ((2, 3), (3, 2)) if pairs else ((2, 2), (3, 3))
    inputs_low, upstream_low = tokens[0], cotangent[0]
    then = Rounds()

    halves = jnp.stack([core, 1 - core, core ^ side, core ^ 1 ^ side]).astype(jnp.int32)

    def relayed(name):
        return RELAY[name] and pairs

    def four(weight, name):
        return [half_of(weight, halves[n], 1) for n in range(3 if relayed(name) else 4)]

    def far_of(name, near, packs):
        return ctx_pair(near) if relayed(name) else fsdp_permute(then(packs[3]), far_bits)

    def joined(pieces):
        return jnp.concatenate(pieces, axis=0)

    seq_count, slots = lengths.shape[1], block_order.shape[1]
    fc1_packs = then.done(*four(fc1_weight, "fc1"))
    fc1_near = fsdp_permute(fc1_packs[2], near_bits)
    own_vectors = jnp.concatenate(
        [
            v.astype(F32)
            for v in (then(ln_gain), ln_bias, dense_bias, fc2_bias, lengths[0], block_order[0])
        ]
    )
    inputs_other = swap(inputs_low, 1)
    vectors = [
        own_vectors,
        swap(own_vectors, 1),
        fsdp_permute(own_vectors, near_bits),
        fsdp_permute(own_vectors, far_bits),
    ]
    packs = pack_attention(
        qkv_weight.transpose(1, 0, 2), then(dense_weight), halves[: 3 if relayed("attention") else 4]
    )
    then.done(*packs)
    fc2_packs = four(then(fc2_weight), "fc2")
    then.done(*fc2_packs)
    upstream_sum = jnp.sum(then(upstream_low).astype(F32), axis=0, keepdims=True)
    then.close(inputs_other, *vectors[1:], fc1_near)

    def over_features(n):
        return jnp.concatenate([v[n * shard : (n + 1) * shard] for v in vectors])[None, :]

    norm_gain, norm_bias = over_features(0), over_features(1)
    out_bias = over_features(2) + over_features(3)
    their_layout = vectors[1][4 * shard :].astype(jnp.int32)

    upstream_other = swap(then(upstream_low), 1)
    fc1_core, attention_core = swap(then(fc1_packs[1]), 1), swap(then(packs[1]), 1)
    attention_near = fsdp_permute(then(packs[2]), near_bits)
    fc1_far = far_of("fc1", then(fc1_near), fc1_packs)
    normed = then.done(frame_rows(inputs_low, then(inputs_other), order, (norm_gain, norm_bias)))
    layouts = [
        (then(lengths[0]), block_order[0]),
        (their_layout[:seq_count], their_layout[seq_count:]),
    ]
    local_slots = ctx_index * 2 + jnp.arange(2, dtype=jnp.int32)
    if pairs:
        key_slots = jnp.concatenate([local_slots, (1 - ctx_index) * 2 + jnp.arange(2)])
    else:
        key_slots = jnp.arange(slots, dtype=jnp.int32)
    allowed, valid, positions, row_places, key_places = [], [], [], [], []
    for lengths_row, order_row in layouts:
        local_packed = packed_rows(order_row, local_slots, block_rows)
        key_packed = packed_rows(order_row, key_slots, block_rows)
        segment, position = place_rows(local_packed, lengths_row)
        key_segment = place_rows(key_packed, lengths_row)[0]
        allowed.append(
            (segment[:, None] == key_segment[None, :])
            & (key_packed[None, :] <= local_packed[:, None])
        )
        valid.append((segment < seq_count).astype(F32)[:, None])
        positions.append(position)
        row_places.append(jnp.stack([local_packed - position, local_packed], axis=1))
        key_places.append(key_packed[None, :])
    cosine_table, sine_table = rotation_tables(jnp.concatenate(positions))
    valid = jnp.concatenate(valid)
    row_places, key_places = jnp.stack(row_places), jnp.stack(key_places)
    upstream_near, upstream_far = [
        jnp.concatenate(
            [lax.dynamic_slice_in_dim(upstream_sum, order[k] * shard, shard, axis=1) for k in blocks],
            axis=1,
        )
        for blocks in ((0, 1), (2 + side, 3 - side))
    ]
    then.done(cosine_table, sine_table, valid, upstream_near, upstream_far, row_places, key_places)
    then.close(upstream_other, fc1_core, attention_core, attention_near, fc1_far)
    fc1_pieces = [fc1_packs[0], fc1_core, fc1_near, fc1_far]

    def grad_block(k, *products, kind=BF16):
        parts = []
        for left, right in products:
            rows = lax.dynamic_slice_in_dim(left, k * shard, shard, axis=1)
            parts.append(dot(rows, right, ((0,), (0,))).astype(kind))
        return jnp.concatenate(parts, axis=1)

    def grad_blocks(*products):
        far = grad_block(2 + side, *products)
        rest = [grad_block(k, *products) for k in (3 - side, 1)]
        return (far, *rest, grad_block(0, *products, kind=F32))

    def add_mine(own, far):
        return then.done((own + then(far).astype(F32)).astype(BF16))

    def add_theirs(near, farther):
        return then.done((near.astype(F32) + then(farther).astype(F32)).astype(BF16))

    def placed(mine, theirs, attention=False):
        parts = then(*mine, *theirs)
        return then.done(*place_grad(parts, core, attention))

    fc2_near = fsdp_permute(then(fc2_packs[2]), near_bits)
    fc2_core = swap(then(fc2_packs[1]), 1)
    attention_far = far_of("attention", then(attention_near), packs)
    attention = [packs[0], attention_core, attention_near, attention_far]
    pre_act = dot(then(normed), joined(fc1_pieces), ((1,), (0,)))
    pre_act = pre_act + half_of(fc1_bias, core, 0).astype(F32)[None, :]
    normal_cdf = 0.5 * (1.0 + lax.erf(pre_act * (1.0 / math.sqrt(2.0))))
    density = jnp.exp(-0.5 * pre_act * pre_act) * (1.0 / math.sqrt(2.0 * math.pi))
    hidden = (pre_act * normal_cdf).astype(BF16)
    slope = normal_cdf + pre_act * density
    hidden, slope = then.done(hidden, slope)
    upstream = then.done(frame_rows(upstream_low, then(upstream_other), order))
    fc2_blocks = then.done(*grad_blocks((then(upstream), hidden)))
    then.close(fc2_near, attention_far, fc2_core)

    def row_block_of(index):
        place, bit = 0 * index, 1
        while bit < tp_size:
            place = place * 2 + (index // bit) % 2
            bit *= 2
        return place

    def flips_to_places(flips):
        return jnp.stack([row_block_of(tp_index ^ f) for f in flips]).astype(jnp.int32)

    fc2_far = far_of("fc2", then(fc2_near), fc2_packs)
    fc2_pieces = [fc2_packs[0], fc2_core, fc2_near, fc2_far]
    fc2_grad_near = swap(then(fc2_blocks[2]), 1)
    qkv_bias_own = half_of(qkv_bias, core, 1).astype(F32).reshape(1, 3 * HD)
    queries, both_local = then.done(
        *project(then(normed), attention, qkv_bias_own, cosine_table, sine_table)
    )
    both_local = both_local.reshape(2, row_count, 2 * HD)
    if pairs:
        both_other = ctx_pair(both_local)
    else:
        both_other = lax.all_gather(both_local, "ctx", axis=1, tiled=True)
    attended_grad = then.done(attended_grads(then(upstream), attention, valid))
    then.close(fc2_far, fc2_grad_near)

    fc2_grad_far = swap(then(fc2_blocks[0]), 2)
    hidden_grad = dot(then(upstream), joined(fc2_pieces), ((1,), (0,)))
    pre_grad = then.done((hidden_grad * slope).astype(BF16))
    both_other = then(both_other)
    attended, probs_all = [], []
    if pairs:
        both = (both_local, both_other)
        key_parts = key_places[:, :, :row_count], key_places[:, :, row_count:]
        attended = then.done(attend(queries, both, row_places, key_parts, valid))
    else:
        for s in range(2):
            rows = slice(s * row_count, (s + 1) * row_count)
            keys, values = both_other[s, :, :HD], both_other[s, :, HD:]
            scores = dot(queries[rows], keys, ((1,), (1,))) * score_scale
            scores = jnp.where(allowed[s], scores, MASK_FLOOR)
            exp_scores = jnp.exp(scores - jnp.max(scores, axis=1, keepdims=True))
            probs = exp_scores / jnp.sum(exp_scores, axis=1, keepdims=True)
            probs_all.append(probs)
            attended.append(dot(probs.astype(BF16), values, ((1,), (0,))))
        attended = then.done((jnp.concatenate(attended) * valid).astype(BF16))
    hidden_size = hidden.shape[1]
    second = (hidden, fc2_pieces, 0, hidden_size)
    theirs = then.done(share_rows((attended, attention, 3, HD), second, row_count))
    then.close(fc2_grad_far)

    def attention_grads(s, into=()):
        if pairs:
            return then.done(
                *attend_back(s, queries, both, row_places, key_parts, then(attended_grad), into)
            )
        rows = slice(s * row_count, (s + 1) * row_count)
        keys, values = both_other[s, :, :HD], both_other[s, :, HD:]
        probs, head_grad = probs_all[s], then(attended_grad[rows])
        prob_grad = dot(head_grad, values, ((1,), (1,)))
        row_delta = jnp.sum(probs * prob_grad, axis=1, keepdims=True)
        score_grad = (probs * (prob_grad - row_delta)).astype(BF16)
        query_piece = dot(score_grad, keys, ((1,), (0,))) * score_scale
        key_piece = dot(score_grad, queries[rows], ((0,), (0,))) * score_scale
        value_piece = dot(probs.astype(BF16), head_grad, ((0,), (0,)))
        return then.done(query_piece, jnp.concatenate([key_piece, value_piece], axis=1))

    low = tp_index % 2

    def halve_on(kept, got, bit, row_block):
        while bit < tp_size:
            digit = (tp_index // bit) % 2
            given, kept = then.done(*halve_rows(digit, kept, got))
            got, row_block, bit = tp_pair(given, bit), row_block * 2 + digit, bit * 2
        return kept, got, row_block

    def double_up(part):
        pieces, flips, bit = [part], [0], tp_size // 2
        while bit > 1:
            pieces += [tp_pair(p, bit) for p in pieces]
            flips += [f ^ bit for f in flips]
            bit //= 2
        return pieces, flips + [f ^ 1 for f in flips]

    def fc1_block(k, kind=BF16):
        return weight_grad(k, shard, [(then(normed), pre_grad)], kind)

    fc2_grad_farther = swap(then(fc2_blocks[1]), 3)
    theirs = swap(then(theirs), 1)
    fc2_mine = ctx_terms(add_mine(fc2_blocks[3], fc2_grad_far))
    grads_first = attention_grads(0)
    first = (then(attended), attention, 3, HD)
    given, kept = then.done(*share_rows(first, second, row_count, theirs, low))
    fc1_far_block = then.done(grad_block(2 + side, (then(normed), pre_grad)))
    then.close(fc2_grad_farther)

    fc1_grad_far = swap(then(fc1_far_block), 2)
    out_got = tp_pair(then(given), 1)
    if pairs:
        query_grad, both_grad, both_given = attention_grads(1, grads_first)
        both_got = ctx_pair(both_given)
    else:
        grads_second = attention_grads(1)
        both_grad = jnp.stack([grads_first[1], grads_second[1]])
        query_grad = jnp.concatenate([grads_first[0], grads_second[0]])
        both_got = jnp.zeros((2, row_count, 2 * HD), BF16)
        both_grad = lax.psum_scatter(both_grad, "ctx", scatter_dimension=1, tiled=True)
        query_grad, both_grad = then.done(query_grad, both_grad)
    fc1_near_block = then.done(grad_block(1, (then(normed), pre_grad)))
    fc1_grad_near = swap(fc1_near_block, 1)
    fc1_farther_block = then.done(grad_block(3 - side, (then(normed), pre_grad)))
    fc1_own_block = then.done(fc1_block(0, F32))
    fc2_theirs = add_theirs(fc2_grad_near, fc2_grad_farther)
    then.close(fc1_grad_far, out_got, fc2_mine[1])

    fc1_grad_farther = swap(then(fc1_farther_block), 3)
    out_kept, out_got, out_block = halve_on(then(kept), out_got, 2, low)
    fc2_theirs = ctx_terms(then(fc2_theirs))
    proj_grad = then.done(
        turn_back(then(query_grad), both_grad, both_got, cosine_table, sine_table)
    )
    second = (pre_grad, fc1_pieces, 0, hidden_size)
    theirs = then.done(share_rows((proj_grad, attention, 0, 3 * HD), second, row_count))

    def attention_block(k, kind=BF16):
        return weight_grad(k, shard, [(then(normed), proj_grad), (upstream, attended)], kind)

    far_block = then.done(attention_block(2 + side))
    fc1_mine = add_mine(fc1_own_block, fc1_grad_far)
    then.close(fc1_grad_farther, out_got, fc2_theirs[1], fc1_grad_near)

    attention_grad_far = swap(then(far_block), 2)
    theirs = swap(then(theirs), 1)
    fc1_mine = ctx_terms(then(fc1_mine))
    out_part = then.done(
        finish_output(order, out_block, then(out_kept), out_got, inputs_low, out_bias)
    )
    out_pieces, flips = double_up(out_part)
    out_late = [tp_pair(out_part, 1)]
    first = (then(proj_grad), attention, 0, 3 * HD)
    given, kept = then.done(*share_rows(first, second, row_count, theirs, low))
    farther_block = then.done(attention_block(3 - side))
    fc1_theirs = add_theirs(fc1_grad_near, fc1_grad_farther)
    then.close(attention_grad_far, out_late[0], *out_pieces[1:], fc1_mine[1])

    attention_grad_farther = swap(then(farther_block), 3)
    got = tp_pair(then(given), 1)
    fc1_theirs = ctx_terms(then(fc1_theirs))
    norm_near, norm_far = then.done(*norm_grads(order, low, side, then(inputs_low), given, kept))
    sums, sums_given = then.done(
        *pack_sums(
            (norm_near, norm_far), (upstream_near, upstream_far), then(pre_grad), proj_grad
        )
    )
    sums_got = swap(sums_given, 2)
    near_block = then.done(attention_block(1))
    attention_grad_near = swap(near_block, 1)
    own_block = then.done(attention_block(0, kind=F32))
    attention_mine = add_mine(own_block, attention_grad_far)
    then.close(attention_grad_farther, got, fc1_theirs[1], sums_got)

    attention_mine = ctx_terms(then(attention_mine))
    kept, got, row_block = halve_on(then(kept), got, 2, low)
    out_late += [tp_pair(p, 1) for p in then(out_pieces[0], *out_pieces[1:])[1:]]
    sums = then(sums) + sums_got
    norm_sums, other_sums = sums[:2], sums[2:]
    norm_sums = norm_sums + tp_pair(norm_sums, 1)
    attention_theirs = add_theirs(attention_grad_near, attention_grad_farther)
    fc2_out = placed(fc2_mine, fc2_theirs)
    then.close(got, norm_sums, attention_mine[1], *out_late[1:])

    attention_theirs = ctx_terms(then(attention_theirs))
    input_part = then.done(
        finish_input_grad(order, row_block, then(kept), got, inputs_low, upstream_low, norm_gain)
    )
    pieces, _ = double_up(input_part)
    late = [tp_pair(input_part, 1)]
    bit = 2
    while bit < tp_size:
        norm_sums = norm_sums + tp_pair(then(norm_sums), bit)
        bit *= 2
    fc1_out = placed(fc1_mine, fc1_theirs)
    output = then.done(gather_rows(then(*out_pieces, *out_late), flips_to_places(flips), BF16))
    then.close(*pieces[1:], late[0], norm_sums, attention_theirs[1])

    late += [tp_pair(p, 1) for p in then(*pieces, output)[1 : len(pieces)]]
    sums = sum(ctx_terms(jnp.concatenate([then(norm_sums), other_sums])))
    qkv_out, dense_out = placed(attention_mine, attention_theirs, True)
    then.close(*late[1:])

    other_core = swap(sums, 1)
    vector_sums = sums[:3, :shard] + other_core[:3, shard : 2 * shard]

    def column_sums(packed):
        return packed[3, :hidden_size], packed[4, : 3 * HD].reshape(3, HD)

    input_grad = gather_rows(then(*pieces, *late), flips_to_places(flips), F32)

    def in_order(mine, other, axis):
        return jnp.where(
            core == 0,
            jnp.concatenate([mine, other], axis=axis),
            jnp.concatenate([other, mine], axis=axis),
        )

    fc1_bias_grad, qkv_bias_grad = [
        in_order(mine, other, axis)
        for axis, mine, other in zip((0, 1), column_sums(sums), column_sums(other_core))
    ]
    return (
        output[None],
        input_grad[None],
        vector_sums[0],
        vector_sums[1],
        qkv_out.transpose(1, 0, 2),
        qkv_bias_grad,
        dense_out,
        vector_sums[2],
        fc1_out,
        fc1_bias_grad,
        fc2_out,
        vector_sums[2],
    )


def solution(mesh):
    placed = (
        P("fsdp", "ctx", None),
        P("fsdp", None),
        P("fsdp", None),
        P("fsdp"),
        P("fsdp"),
        P("fsdp", None, "tp"),
        P(None, "tp"),
        P("fsdp", "tp"),
        P("fsdp"),
        P("fsdp", "tp"),
        P("tp"),
        P("fsdp", "tp"),
        P("fsdp"),
        P("fsdp", "ctx", None),
    )
    return jax.shard_map(
        per_device,
        mesh=mesh,
        in_specs=placed,
        out_specs=(
            P("fsdp", "ctx", None),
            P("fsdp", "ctx", None),
            P("fsdp"),
            P("fsdp"),
            P("fsdp", None, "tp"),
            P(None, "tp"),
            P("fsdp", "tp"),
            P("fsdp"),
            P("fsdp", "tp"),
            P("tp"),
            P("fsdp", "tp"),
            P("fsdp"),
        ),
        check_vma=False,
    )
```

```python
import math

import jax
import jax.numpy as jnp
from jax import lax
from jax.experimental import pallas as pl
from jax.experimental.pallas import tpu as pltpu
from jax.sharding import PartitionSpec as P

HD = 256
ROT = 64


NORM_EPSILON = 1e-05
MASK_FLOOR = -1000000000.0
F32 = jnp.float32
BF16 = jnp.bfloat16
LANES = 128
RELAY = {"attention": True, "fc1": True, "fc2": False}


def rotation_tables(position):
    half = ROT // 2
    frequency = jnp.exp(jnp.arange(half, dtype=F32) * (-2.0 * math.log(10000.0) / ROT))
    angles = position.astype(F32)[:, None] * frequency[None, :]
    cosine, sine = jnp.cos(angles), jnp.sin(angles)
    rest = (position.shape[0], LANES - ROT)
    return (
        jnp.concatenate([cosine, cosine, jnp.ones(rest, F32)], axis=1),
        jnp.concatenate([-sine, sine, jnp.zeros(rest, F32)], axis=1),
    )


def packed_rows(order_row, slots, block_rows):
    selector = slots[:, None] == jnp.arange(order_row.shape[0], dtype=jnp.int32)[None, :]
    source_block = jnp.sum(jnp.where(selector, order_row[None, :], 0), axis=1, dtype=jnp.int32)
    within = jnp.arange(block_rows, dtype=jnp.int32)
    return (source_block[:, None] * block_rows + within[None, :]).reshape(-1)


def place_rows(packed_at, lengths_row):
    seq_ends = jnp.cumsum(lengths_row, dtype=jnp.int32)
    passed = packed_at[:, None] >= seq_ends[None, :]
    segment = jnp.sum(passed.astype(jnp.int32), axis=1, dtype=jnp.int32)
    before = jnp.sum(jnp.where(passed, lengths_row[None, :], 0), axis=1, dtype=jnp.int32)
    return (segment, packed_at - before)


def dot(a, b, contract):
    return lax.dot_general(a, b, (contract, ((), ())), preferred_element_type=F32)


def fsdp_permute(x, bits):
    size, lanes = lax.axis_size("fsdp"), lax.axis_size("ctx")
    perm = [
        (f * lanes + x, (f ^ bits[x % 2]) * lanes + x) for f in range(size) for x in range(lanes)
    ]
    return lax.ppermute(x, ("fsdp", "ctx"), perm)


def swap(x, bit):
    return fsdp_permute(x, (bit, bit))


def ctx_pair(x):
    return lax.ppermute(x, "ctx", [(0, 1), (1, 0)])


def ctx_terms(x):
    if lax.axis_size("ctx") == 2:
        return x, ctx_pair(x)
    return lax.psum(x.astype(F32), "ctx"), jnp.zeros_like(x)


def tp_pair(x, bit):
    return lax.ppermute(x, "tp", [(i, i ^ bit) for i in range(lax.axis_size("tp"))])


def half_of(x, which, axis):
    size = x.shape[axis] // 2
    return lax.dynamic_slice_in_dim(x, which * size, size, axis=axis)


def kernel_call(body, scalars, arrays, in_specs, out_shape, out_specs, grid, name, scratch=(), aliases=None):
    return pl.pallas_call(
        body,
        out_shape=out_shape,
        grid_spec=pltpu.PrefetchScalarGridSpec(
            num_scalar_prefetch=1,
            grid=grid,
            in_specs=in_specs,
            out_specs=out_specs,
            scratch_shapes=scratch,
        ),
        input_output_aliases=aliases or {},
        cost_estimate=pl.CostEstimate(flops=0, transcendentals=0, bytes_accessed=0),
        name=name,
    )(scalars, *arrays)


def aligned(index, size):
    return pl.ds(pl.multiple_of(index * size, size), size)


def frame_rows(own, other, order, norm=None):
    rows, columns = own.shape
    width, step = columns // 4, rows // 2

    def kernel(order_ref, own_ref, other_ref, *refs):
        gain_ref, bias_ref, out_ref, wide_ref = refs if norm else (None, None, refs[0], None)
        for s, ref in enumerate((own_ref, other_ref)):
            if norm:
                x = ref[...].astype(F32)
                x = x - jnp.mean(x, axis=1, keepdims=True)
                variance = jnp.mean(x * x, axis=1, keepdims=True)
                wide_ref[...] = x * lax.rsqrt(variance + NORM_EPSILON)
            for k in range(4):
                to = slice(k * width, (k + 1) * width)
                at = aligned(order_ref[k], width)
                if norm:
                    out_ref[s, :, to] = (
                        wide_ref[:, at] * gain_ref[:, to] + bias_ref[:, to]
                    ).astype(BF16)
                else:
                    out_ref[s, :, to] = ref[:, at]

    row_spec = pl.BlockSpec((step, columns), lambda r, o: (r, 0))
    vector_spec = pl.BlockSpec((1, columns), lambda r, o: (0, 0))
    out = kernel_call(
        kernel,
        order,
        (own, other, *(norm or ())),
        [row_spec, row_spec] + ([vector_spec, vector_spec] if norm else []),
        jax.ShapeDtypeStruct((2, rows, columns), BF16),
        pl.BlockSpec((2, step, columns), lambda r, o: (0, r, 0)),
        (2,),
        "norm_rows" if norm else "frame_rows",
        scratch=[pltpu.VMEM((step, columns), F32)] if norm else (),
    )
    return out.reshape(2 * rows, columns)


def place_grad(parts, core, attention):
    rows, columns = parts[0].shape
    step = rows // 2

    def kernel(core_ref, a_ref, ax_ref, b_ref, bx_ref, *out_refs):
        for h, (u_ref, ux_ref) in enumerate(((a_ref, ax_ref), (b_ref, bx_ref))):
            total = u_ref[...].astype(F32) + ux_ref[...].astype(F32)
            place = core_ref[0] ^ h
            if attention:
                for t in range(3):
                    out_refs[0][t, :, aligned(place, HD)] = total[:, t * HD : (t + 1) * HD]
                out_refs[1][:, aligned(place, HD)] = total[:, 3 * HD :]
            else:
                out_refs[0][:, aligned(place, columns)] = total

    shapes = [(rows, 2 * columns)]
    specs = [pl.BlockSpec((step, 2 * columns), lambda r, c: (r, 0))]
    if attention:
        shapes = [(3, rows, 2 * HD), (rows, 2 * HD)]
        specs = [
            pl.BlockSpec((3, step, 2 * HD), lambda r, c: (0, r, 0)),
            pl.BlockSpec((step, 2 * HD), lambda r, c: (r, 0)),
        ]
    return kernel_call(
        kernel,
        core[None],
        parts,
        [pl.BlockSpec((step, columns), lambda r, c: (r, 0))] * 4,
        [jax.ShapeDtypeStruct(shape, F32) for shape in shapes],
        specs,
        (2,),
        "place_grad",
    )


def weight_grad(block, shard, products, kind):
    step = shard // 2
    widths = [right.shape[1] for _, right in products]

    def kernel(_, *refs):
        at = 0
        for n, width in enumerate(widths):
            left_ref, right_ref = refs[2 * n : 2 * n + 2]
            total = dot(left_ref[...], right_ref[...], ((0,), (0,)))
            refs[-1][:, at : at + width] = total.astype(kind)
            at += width

    specs = []
    for left, right in products:
        specs.append(pl.BlockSpec((left.shape[0], step), lambda n, k: (0, 2 * k[0] + n)))
        specs.append(pl.BlockSpec(right.shape, lambda n, k: (0, 0)))
    return kernel_call(
        kernel,
        jnp.asarray(block, jnp.int32)[None],
        [a for product in products for a in product],
        specs,
        jax.ShapeDtypeStruct((shard, sum(widths)), kind),
        pl.BlockSpec((step, sum(widths)), lambda n, k: (n, 0)),
        (2,),
        "weight_grad",
    )


def share_rows(first, second, rows, theirs=None, low=None):
    width = first[1][0].shape[0]
    own = theirs is not None
    at = 0 if own else 1
    half = rows // 2

    def kernel(low_ref, f_ref, s_ref, *refs):
        f_refs, s_refs, refs = refs[:4], refs[4:8], refs[8:]
        for n in range(2):

            @pl.when(pl.program_id(0) == n)
            def _(n=n):
                for m in range(2):
                    k = 2 * n + m
                    total = dot(f_ref[...], f_refs[k][...], ((1,), (1,)))
                    total = total + dot(s_ref[...], s_refs[k][...], ((1,), (1,)))
                    if not own:
                        refs[0][:, (1 - m) * width : (2 - m) * width] = total.astype(BF16)
                        continue
                    theirs_ref, given_ref, kept_ref, all_ref = refs
                    to = slice(m * width, (m + 1) * width)
                    all_ref[...] = (total + theirs_ref[:, to].astype(F32)).astype(BF16)
                    given_ref[:, to] = all_ref[aligned(1 - low_ref[0], half), :]
                    kept_ref[:, to] = all_ref[aligned(low_ref[0], half), :]

    arrays, in_specs = [], []
    for acts, _, _, size in (first, second):
        arrays.append(acts)
        in_specs.append(pl.BlockSpec((rows, size), lambda n, b: (at, 0)))
    for _, pieces, block, size in (first, second):
        arrays += pieces
        in_specs += [pl.BlockSpec((width, size), lambda n, b, block=block: (0, block))] * 4
    out_shape = jax.ShapeDtypeStruct((rows, 4 * width), BF16)
    out_spec = pl.BlockSpec((rows, 2 * width), lambda n, b: (0, n))
    scratch = ()
    if own:
        arrays.append(theirs)
        in_specs.append(out_spec)
        out_shape = [jax.ShapeDtypeStruct((half, 4 * width), BF16)] * 2
        out_spec = [pl.BlockSpec((half, 2 * width), lambda n, b: (0, n))] * 2
        scratch = [pltpu.VMEM((rows, width), BF16)]
    return kernel_call(
        kernel,
        low[None] if own else jnp.zeros((1,), jnp.int32),
        arrays,
        in_specs,
        out_shape,
        out_spec,
        (2,),
        "share_rows",
        scratch=scratch,
    )


def finish_output(order, row_block, kept, got, inputs, out_bias):
    rows, columns = kept.shape
    width, steps = columns // 4, 1
    step = rows // steps

    def kernel(s_ref, kept_ref, got_ref, x_ref, bias_ref, out_ref):
        for k in range(4):
            cols, at = slice(k * width, (k + 1) * width), aligned(s_ref[k], width)
            total = kept_ref[:, cols] + got_ref[:, cols].astype(F32)
            out_ref[:, at] = (x_ref[:, at].astype(F32) + total + bias_ref[:, cols]).astype(BF16)

    spec = pl.BlockSpec((step, columns), lambda i, s: (i, 0))
    return kernel_call(
        kernel,
        jnp.concatenate([order, row_block[None]]),
        (kept, got, inputs, out_bias),
        [
            spec,
            spec,
            pl.BlockSpec((step, columns), lambda i, s: (s[4] * steps + i, 0)),
            pl.BlockSpec((1, columns), lambda i, s: (0, 0)),
        ],
        jax.ShapeDtypeStruct((rows, columns), BF16),
        spec,
        (steps,),
        "finish_output",
    )


def finish_input_grad(order, row_block, kept, got, inputs, upstream, norm_gain):
    rows, columns = kept.shape
    width, steps = columns // 4, 1
    step = rows // steps

    def kernel(s_ref, kept_ref, got_ref, x_ref, dy_ref, gain_ref, out_ref, std_ref):
        x = x_ref[...].astype(F32)
        x = x - jnp.mean(x, axis=1, keepdims=True)
        inverse = lax.rsqrt(jnp.mean(x * x, axis=1, keepdims=True) + NORM_EPSILON)
        std_ref[...] = x * inverse
        mean_scaled = jnp.zeros((step, 1), F32)
        mean_product = jnp.zeros((step, 1), F32)

        def parts(k):
            cols, at = slice(k * width, (k + 1) * width), aligned(s_ref[k], width)
            total = kept_ref[:, cols] + got_ref[:, cols].astype(F32)
            return at, total * gain_ref[:, cols], std_ref[:, at]

        for k in range(4):
            _, scaled, standard = parts(k)
            mean_scaled += jnp.sum(scaled, axis=1, keepdims=True) / columns
            mean_product += jnp.sum(scaled * standard, axis=1, keepdims=True) / columns
        for k in range(4):
            at, scaled, standard = parts(k)
            change = inverse * (scaled - mean_scaled - standard * mean_product)
            out_ref[:, at] = (dy_ref[:, at].astype(F32) + change).astype(BF16)

    spec = pl.BlockSpec((step, columns), lambda i, s: (i, 0))
    rows_spec = pl.BlockSpec((step, columns), lambda i, s: (s[4] * steps + i, 0))
    return kernel_call(
        kernel,
        jnp.concatenate([order, row_block[None]]),
        (kept, got, inputs, upstream, norm_gain),
        [spec, spec, rows_spec, rows_spec, pl.BlockSpec((1, columns), lambda i, s: (0, 0))],
        jax.ShapeDtypeStruct((rows, columns), BF16),
        spec,
        (steps,),
        "finish_input_grad",
        scratch=[pltpu.VMEM((step, columns), F32)],
    )


def norm_grads(order, low, side, inputs, given, kept):
    rows, columns = inputs.shape
    width, step = columns // 4, rows // 2

    def kernel(order_ref, x_ref, given_ref, kept_ref, near_ref, far_ref, std_ref):
        x = x_ref[...].astype(F32)
        x = x - jnp.mean(x, axis=1, keepdims=True)
        std_ref[...] = x * lax.rsqrt(jnp.mean(x * x, axis=1, keepdims=True) + NORM_EPSILON)

        def add(share_ref, first):
            for k in range(4):
                cols = slice(k * width, (k + 1) * width)
                part = share_ref[:, cols].astype(F32)
                product = part * std_ref[:, aligned(order_ref[k], width)]
                sums = jnp.sum(product, axis=0, keepdims=True), jnp.sum(part, axis=0, keepdims=True)
                out_ref, at = near_ref, cols
                if k > 1:
                    out_ref, at = far_ref, aligned((k - 2) ^ order_ref[5], width)
                for n in range(2):
                    before = 0.0 if first else out_ref[n : n + 1, at]
                    out_ref[n : n + 1, at] = before + sums[n]

        @pl.when(pl.program_id(0) == 0)
        def _():
            add(given_ref, True)

        @pl.when(pl.program_id(0) == 1)
        def _():
            add(kept_ref, False)

    half_spec = pl.BlockSpec((step, columns), lambda r, o: (0, 0))
    return kernel_call(
        kernel,
        jnp.concatenate([order, low[None], side[None].astype(jnp.int32)]),
        (inputs, given, kept),
        [
            pl.BlockSpec((step, columns), lambda r, o: (r * o[4] + (1 - r) * (1 - o[4]), 0)),
            half_spec,
            half_spec,
        ],
        [jax.ShapeDtypeStruct((2, columns // 2), F32)] * 2,
        [pl.BlockSpec((2, columns // 2), lambda r, o: (0, 0))] * 2,
        (2,),
        "norm_grads",
        scratch=[pltpu.VMEM((step, columns), F32)],
    )


def halve_rows(digit, kept, got):
    rows, columns = kept.shape

    def kernel(_, a_ref, b_ref, c_ref, d_ref, given_ref, kept_ref):
        given_ref[...] = (a_ref[...].astype(F32) + b_ref[...].astype(F32)).astype(BF16)
        kept_ref[...] = c_ref[...].astype(F32) + d_ref[...].astype(F32)

    block = rows // 2, columns // 2
    leaves = pl.BlockSpec(block, lambda n, d: (1 - d[0], n))
    stays = pl.BlockSpec(block, lambda n, d: (d[0], n))
    out_spec = pl.BlockSpec(block, lambda n, d: (0, n))
    return kernel_call(
        kernel,
        digit[None],
        (kept, got, kept, got),
        [leaves, leaves, stays, stays],
        [jax.ShapeDtypeStruct((rows // 2, columns), kind) for kind in (BF16, F32)],
        [out_spec, out_spec],
        (2,),
        "halve_rows",
    )


def pack_sums(norm_sums, upstream_sums, pre_grad, proj_grad):
    wide = max(norm_sums[0].shape[1], pre_grad.shape[1], proj_grad.shape[1])
    step = pre_grad.shape[0] // 8

    def kernel(_, *refs):
        norm_refs, up_refs, grad_refs, out_refs = refs[:2], refs[2:4], refs[4:6], refs[6:]
        for out_ref in out_refs:
            out_ref[...] = jnp.zeros_like(out_ref)
        for norm_ref, up_ref, out_ref in zip(norm_refs, up_refs, out_refs):
            out_ref[0:2, : norm_ref.shape[1]] = norm_ref[...]
            out_ref[2:3, : up_ref.shape[1]] = up_ref[...]
        for n, ref in enumerate(grad_refs):
            total = jnp.zeros((1, ref.shape[1]), F32)
            for c in range(8):
                part = ref[c * step : (c + 1) * step, :].astype(F32)
                total = total + jnp.sum(part, axis=0, keepdims=True)
            for out_ref in out_refs:
                out_ref[3 + n : 4 + n, : ref.shape[1]] = total

    arrays = (*norm_sums, *upstream_sums, pre_grad, proj_grad)
    return kernel_call(
        kernel,
        jnp.zeros((1,), jnp.int32),
        arrays,
        [pl.BlockSpec(a.shape, lambda n, z: (0, 0)) for a in arrays],
        [jax.ShapeDtypeStruct((8, wide), F32)] * 2,
        [pl.BlockSpec((8, wide), lambda n, z: (0, 0))] * 2,
        (1,),
        "pack_sums",
    )


def gather_rows(pieces, places, count, dtype, into=()):
    rows, columns = pieces[0].shape

    def kernel(_, *refs):
        for n in range(len(pieces)):

            @pl.when(pl.program_id(0) == n)
            def _(n=n):
                refs[-1][...] = refs[n][...].astype(dtype)

    return kernel_call(
        kernel,
        places,
        (*pieces, *into),
        [pl.BlockSpec((rows, columns), lambda n, p: (0, 0))] * len(pieces)
        + [pl.BlockSpec(memory_space=pl.ANY)] * len(into),
        jax.ShapeDtypeStruct((rows * count, columns), dtype),
        pl.BlockSpec((rows, columns), lambda n, p: (p[n], 0)),
        (len(pieces),),
        "gather_rows",
        aliases={1 + len(pieces): 0} if into else None,
    )


def turned(x, cosine, sine):
    lane = lax.broadcasted_iota(jnp.int32, x.shape, 1)
    half = ROT // 2
    partner = jnp.where(
        lane < half, pltpu.roll(x, x.shape[1] - half, axis=1), pltpu.roll(x, half, axis=1)
    )
    return x * cosine + partner * sine


def project(normed, pieces, bias, cosine, sine):
    rows = normed.shape[0] // 2
    width = pieces[0].shape[0]

    def kernel(_, x_ref, *refs):
        piece_refs, (bias_ref, cos_ref, sin_ref, q_ref, kv_ref) = refs[:4], refs[4:]
        total = dot(x_ref[:, :width], piece_refs[0][...], ((1,), (0,)))
        for k in range(1, 4):
            cols = slice(k * width, (k + 1) * width)
            total = total + dot(x_ref[:, cols], piece_refs[k][...], ((1,), (0,)))
        total = total + bias_ref[...]
        cosine, sine = cos_ref[...], sin_ref[...]
        for n, ref in enumerate((q_ref, kv_ref)):
            head = total[:, n * HD : (n + 1) * HD]
            ref[:, :LANES] = turned(head[:, :LANES], cosine, sine).astype(BF16)
            ref[:, LANES:HD] = head[:, LANES:].astype(BF16)
        kv_ref[:, HD:] = total[:, 2 * HD :].astype(BF16)

    def by_row(columns):
        return pl.BlockSpec((rows, columns), lambda s, z: (s, 0))

    return kernel_call(
        kernel,
        jnp.zeros((1,), jnp.int32),
        (normed, *pieces, bias, cosine, sine),
        [by_row(normed.shape[1])]
        + [pl.BlockSpec((width, 3 * HD), lambda s, z: (0, 0))] * 4
        + [pl.BlockSpec((1, 3 * HD), lambda s, z: (0, 0)), by_row(LANES), by_row(LANES)],
        [
            jax.ShapeDtypeStruct((2 * rows, HD), BF16),
            jax.ShapeDtypeStruct((2 * rows, 2 * HD), BF16),
        ],
        [by_row(HD), by_row(2 * HD)],
        (2,),
        "project",
    )


def turn_back(query_grad, kept, got, cosine, sine):
    rows = kept.shape[1]

    def kernel(_, q_ref, kept_ref, got_ref, cos_ref, sin_ref, out_ref):
        both = kept_ref[...] + got_ref[...].astype(F32)
        cosine, sine = cos_ref[...], -sin_ref[...]
        for n, head in enumerate((q_ref[...], both[:, :HD])):
            at = n * HD
            out_ref[:, at : at + LANES] = turned(head[:, :LANES], cosine, sine).astype(BF16)
            out_ref[:, at + LANES : at + HD] = head[:, LANES:].astype(BF16)
        out_ref[:, 2 * HD :] = both[:, HD:].astype(BF16)

    def by_row(columns):
        return pl.BlockSpec((rows, columns), lambda s, z: (s, 0))

    both_spec = pl.BlockSpec((None, rows, 2 * HD), lambda s, z: (s, 0, 0))
    return kernel_call(
        kernel,
        jnp.zeros((1,), jnp.int32),
        (query_grad, kept, got, cosine, sine),
        [by_row(HD), both_spec, both_spec, by_row(LANES), by_row(LANES)],
        jax.ShapeDtypeStruct((2 * rows, 3 * HD), BF16),
        by_row(3 * HD),
        (2,),
        "turn_back",
    )


def attended_grads(upstream, pieces, valid):
    rows = upstream.shape[0] // 2
    width = pieces[0].shape[0]

    def kernel(_, dy_ref, *refs):
        piece_refs, (valid_ref, out_ref) = refs[:4], refs[4:]
        total = dot(dy_ref[:, :width], piece_refs[0][...], ((1,), (0,)))
        for k in range(1, 4):
            cols = slice(k * width, (k + 1) * width)
            total = total + dot(dy_ref[:, cols], piece_refs[k][...], ((1,), (0,)))
        out_ref[...] = total.astype(BF16) * valid_ref[...].astype(BF16)

    def by_row(columns):
        return pl.BlockSpec((rows, columns), lambda s, z: (s, 0))

    return kernel_call(
        kernel,
        jnp.zeros((1,), jnp.int32),
        (upstream, *pieces, valid),
        [by_row(upstream.shape[1])]
        + [pl.BlockSpec((width, HD), lambda s, z: (0, 3))] * 4
        + [by_row(1)],
        jax.ShapeDtypeStruct((2 * rows, HD), BF16),
        by_row(HD),
        (2,),
        "attended_grads",
    )


def chances(query, keys, first, last, key_place):
    scores = []
    for part, place in zip(keys, key_place):
        score = dot(query, part, ((1,), (1,))) * (1.0 / math.sqrt(HD))
        scores.append(jnp.where((place >= first) & (place <= last), score, MASK_FLOOR))
    top = jnp.max(scores[0], axis=1, keepdims=True)
    for score in scores[1:]:
        top = jnp.maximum(top, jnp.max(score, axis=1, keepdims=True))
    exps = [jnp.exp(score - top) for score in scores]
    total = sum(jnp.sum(e, axis=1, keepdims=True) for e in exps)
    return [e / total for e in exps]


def attention_specs(rows, parts):
    return (
        [pl.BlockSpec((rows, HD), lambda n, s: (n + s[0], 0))]
        + [pl.BlockSpec((None, rows, 2 * HD), lambda n, s: (n + s[0], 0, 0))] * parts
        + [pl.BlockSpec((None, rows, 2), lambda n, s: (n + s[0], 0, 0))]
        + [pl.BlockSpec((None, 1, rows), lambda n, s: (n + s[0], 0, 0))] * parts
    )


def attend(queries, both, row_places, key_places, valid):
    rows = queries.shape[0] // 2
    parts = len(both)

    def kernel(_, q_ref, *refs):
        both_refs, place_ref, key_refs = refs[:parts], refs[parts], refs[parts + 1 : 2 * parts + 1]
        valid_ref, out_ref = refs[2 * parts + 1 :]
        step = rows // 2
        for c in range(2):
            at = slice(c * step, (c + 1) * step)
            probs = chances(
                q_ref[at, :],
                [ref[:, :HD] for ref in both_refs],
                place_ref[at, 0:1],
                place_ref[at, 1:2],
                [ref[...] for ref in key_refs],
            )
            total = 0.0
            for p, ref in zip(probs, both_refs):
                total = total + dot(p.astype(BF16), ref[:, HD:], ((1,), (0,)))
            out_ref[at, :] = (total * valid_ref[at, :]).astype(BF16)

    return kernel_call(
        kernel,
        jnp.zeros((1,), jnp.int32),
        (queries, *both, row_places, *key_places, valid),
        attention_specs(rows, parts) + [pl.BlockSpec((rows, 1), lambda n, s: (n, 0))],
        jax.ShapeDtypeStruct(queries.shape, BF16),
        pl.BlockSpec((rows, HD), lambda n, s: (n, 0)),
        (2,),
        "attend",
    )


def attend_back(s, queries, both, row_places, key_places, attended_grad, into=()):
    rows = queries.shape[0] // 2
    scale = 1.0 / math.sqrt(HD)

    def kernel(_, q_ref, own_ref, far_ref, place_ref, own_key_ref, far_key_ref, up_ref, *outs):
        query_ref, kept_ref, given_ref = outs[-3:]
        step = rows // 2
        sums = [[0.0, 0.0], [0.0, 0.0]]
        for c in range(2):
            at = slice(c * step, (c + 1) * step)
            query, up = q_ref[at, :], up_ref[at, :]
            probs = chances(
                query,
                [own_ref[:, :HD], far_ref[:, :HD]],
                place_ref[at, 0:1],
                place_ref[at, 1:2],
                [own_key_ref[...], far_key_ref[...]],
            )
            grads = [dot(up, ref[:, HD:], ((1,), (1,))) for ref in (own_ref, far_ref)]
            delta = sum(jnp.sum(p * g, axis=1, keepdims=True) for p, g in zip(probs, grads))
            total = 0.0
            for n, ref in enumerate((own_ref, far_ref)):
                score_grad = (probs[n] * (grads[n] - delta)).astype(BF16)
                total = total + dot(score_grad, ref[:, :HD], ((1,), (0,)))
                sums[n][0] = sums[n][0] + dot(score_grad, query, ((0,), (0,)))
                sums[n][1] = sums[n][1] + dot(probs[n].astype(BF16), up, ((0,), (0,)))
            query_ref[at, :] = total * scale
        for n, ref in enumerate((kept_ref, given_ref)):
            ref[:, :HD] = (sums[n][0] * scale).astype(ref.dtype)
            ref[:, HD:] = sums[n][1].astype(ref.dtype)

    both_spec = pl.BlockSpec((None, rows, 2 * HD), lambda n, s: (n + s[0], 0, 0))
    row_spec = pl.BlockSpec((rows, HD), lambda n, s: (n + s[0], 0))
    arrays = (queries, *both, row_places, *key_places, attended_grad)
    return kernel_call(
        kernel,
        jnp.full((1,), s, jnp.int32),
        (*arrays, *into),
        attention_specs(rows, 2) + [row_spec] + [pl.BlockSpec(memory_space=pl.ANY)] * len(into),
        [
            jax.ShapeDtypeStruct(queries.shape, F32),
            jax.ShapeDtypeStruct(both[0].shape, F32),
            jax.ShapeDtypeStruct(both[0].shape, BF16),
        ],
        [row_spec, both_spec, both_spec],
        (1,),
        "attend_back",
        aliases={1 + len(arrays) + n: n for n in range(len(into))},
    )


def pack_attention(qkv_weight, dense_weight, halves):
    rows = qkv_weight.shape[1]
    count = halves.shape[0]

    def kernel(h_ref, qkv_ref, dense_ref, *out_refs):
        for n in range(count):
            for t in range(3):
                out_refs[n][:, t * HD : (t + 1) * HD] = qkv_ref[t, :, aligned(h_ref[n], HD)]
            out_refs[n][:, 3 * HD :] = dense_ref[:, aligned(h_ref[n], HD)]

    def spec(columns):
        return pl.BlockSpec((rows // 2, columns), lambda r, h: (r, 0))

    return kernel_call(
        kernel,
        halves,
        (qkv_weight, dense_weight),
        [pl.BlockSpec((3, rows // 2, 2 * HD), lambda r, h: (0, r, 0)), spec(2 * HD)],
        [jax.ShapeDtypeStruct((rows, 4 * HD), BF16)] * count,
        [spec(4 * HD)] * count,
        (2,),
        "pack_attention",
    )


class Rounds:
    def __init__(self):
        self.last = ()

    def __call__(self, *arrays):
        got = lax.optimization_barrier((*arrays, *self.last))[: len(arrays)]
        return got if len(arrays) > 1 else got[0]

    def done(self, *arrays):
        self.last = arrays
        return arrays if len(arrays) > 1 else arrays[0]

    def close(self, *arrays):
        self.last = (*self.last, *arrays)


def per_device(
    tokens,
    lengths,
    block_order,
    ln_gain,
    ln_bias,
    qkv_weight,
    qkv_bias,
    dense_weight,
    dense_bias,
    fc1_weight,
    fc1_bias,
    fc2_weight,
    fc2_bias,
    cotangent,
):
    me = lax.axis_index("fsdp")
    core = me % 2
    tp_index = lax.axis_index("tp").astype(jnp.int32)
    tp_size = lax.axis_size("tp")
    ctx_index = lax.axis_index("ctx")
    ctx_size = lax.axis_size("ctx")
    pairs = ctx_size == 2
    side = ctx_index % 2 if pairs else 0 * ctx_index
    shard = ln_gain.shape[0]
    row_count = tokens.shape[1]
    block_rows = row_count // 2
    score_scale = 1.0 / math.sqrt(HD)
    order = jnp.stack([me, me ^ 1, me ^ (2 + side), me ^ (3 - side)]).astype(jnp.int32)
    near_bits, far_bits = ((2, 3), (3, 2)) if pairs else ((2, 2), (3, 3))
    inputs_low, upstream_low = tokens[0], cotangent[0]
    then = Rounds()

    halves = jnp.stack([core, 1 - core, core ^ side, core ^ 1 ^ side]).astype(jnp.int32)

    def relayed(name):
        return RELAY[name] and pairs

    def four(weight, name):
        return [half_of(weight, halves[n], 1) for n in range(3 if relayed(name) else 4)]

    def far_of(name, near, packs):
        return ctx_pair(near) if relayed(name) else fsdp_permute(then(packs[3]), far_bits)

    def joined(pieces):
        return jnp.concatenate(pieces, axis=0)

    seq_count, slots = lengths.shape[1], block_order.shape[1]
    fc1_pack = then.done(half_of(fc1_weight, halves[2], 1))
    fc1_near = fsdp_permute(fc1_pack, near_bits)
    own_vectors = jnp.concatenate(
        [
            v.astype(F32)
            for v in (then(ln_gain), ln_bias, dense_bias, fc2_bias, lengths[0], block_order[0])
        ]
    )
    inputs_other = swap(inputs_low, 1)
    vectors = [
        own_vectors,
        swap(own_vectors, 1),
        fsdp_permute(own_vectors, near_bits),
        fsdp_permute(own_vectors, far_bits),
    ]
    fc1_packs = four(then(fc1_weight, own_vectors)[0], "fc1")
    fc1_packs[2] = fc1_pack
    then.done(*fc1_packs)
    packs = pack_attention(
        qkv_weight.transpose(1, 0, 2), then(dense_weight), halves[: 3 if relayed("attention") else 4]
    )
    then.done(*packs)
    fc2_packs = four(then(fc2_weight), "fc2")
    then.done(*fc2_packs)
    upstream_sum = jnp.sum(then(upstream_low).astype(F32), axis=0, keepdims=True)
    then.close(inputs_other, *vectors[1:], fc1_near)

    def over_features(n):
        return jnp.concatenate([v[n * shard : (n + 1) * shard] for v in vectors])[None, :]

    norm_gain, norm_bias = over_features(0), over_features(1)
    out_bias = over_features(2) + over_features(3)
    their_layout = vectors[1][4 * shard :].astype(jnp.int32)

    upstream_other = swap(then(upstream_low), 1)
    fc1_core, attention_core = swap(then(fc1_packs[1]), 1), swap(then(packs[1]), 1)
    attention_near = fsdp_permute(then(packs[2]), near_bits)
    fc1_far = far_of("fc1", then(fc1_near), fc1_packs)
    normed = then.done(frame_rows(inputs_low, then(inputs_other), order, (norm_gain, norm_bias)))
    layouts = [
        (then(lengths[0]), block_order[0]),
        (their_layout[:seq_count], their_layout[seq_count:]),
    ]
    local_slots = ctx_index * 2 + jnp.arange(2, dtype=jnp.int32)
    if pairs:
        key_slots = jnp.concatenate([local_slots, (1 - ctx_index) * 2 + jnp.arange(2)])
    else:
        key_slots = jnp.arange(slots, dtype=jnp.int32)
    allowed, valid, positions, row_places, key_places = [], [], [], [], []
    for lengths_row, order_row in layouts:
        local_packed = packed_rows(order_row, local_slots, block_rows)
        key_packed = packed_rows(order_row, key_slots, block_rows)
        segment, position = place_rows(local_packed, lengths_row)
        key_segment = place_rows(key_packed, lengths_row)[0]
        allowed.append(
            (segment[:, None] == key_segment[None, :])
            & (key_packed[None, :] <= local_packed[:, None])
        )
        valid.append((segment < seq_count).astype(F32)[:, None])
        positions.append(position)
        row_places.append(jnp.stack([local_packed - position, local_packed], axis=1))
        key_places.append(key_packed[None, :])
    cosine_table, sine_table = rotation_tables(jnp.concatenate(positions))
    valid = jnp.concatenate(valid)
    row_places, key_places = jnp.stack(row_places), jnp.stack(key_places)
    upstream_near, upstream_far = [
        jnp.concatenate(
            [lax.dynamic_slice_in_dim(upstream_sum, order[k] * shard, shard, axis=1) for k in blocks],
            axis=1,
        )
        for blocks in ((0, 1), (2 + side, 3 - side))
    ]
    then.done(cosine_table, sine_table, valid, upstream_near, upstream_far, row_places, key_places)
    then.close(upstream_other, fc1_core, attention_core, attention_near, fc1_far, out_bias)
    fc1_pieces = [fc1_packs[0], fc1_core, fc1_near, fc1_far]

    def grad_block(k, *products, kind=BF16):
        parts = []
        for left, right in products:
            rows = lax.dynamic_slice_in_dim(left, k * shard, shard, axis=1)
            parts.append(dot(rows, right, ((0,), (0,))).astype(kind))
        return jnp.concatenate(parts, axis=1)

    def grad_blocks(*products):
        far = grad_block(2 + side, *products)
        rest = [grad_block(k, *products) for k in (3 - side, 1)]
        return (far, *rest, grad_block(0, *products, kind=F32))

    def add_mine(own, far):
        return then.done((own + then(far).astype(F32)).astype(BF16))

    def add_theirs(near, farther):
        return then.done((near.astype(F32) + then(farther).astype(F32)).astype(BF16))

    def placed(mine, theirs, attention=False):
        parts = then(*mine, *theirs)
        return then.done(*place_grad(parts, core, attention))

    fc2_near = fsdp_permute(then(fc2_packs[2]), near_bits)
    fc2_core = swap(then(fc2_packs[1]), 1)
    attention_far = far_of("attention", then(attention_near), packs)
    attention = [packs[0], attention_core, attention_near, attention_far]
    pre_act = dot(then(normed), joined(fc1_pieces), ((1,), (0,)))
    pre_act = pre_act + half_of(fc1_bias, core, 0).astype(F32)[None, :]
    normal_cdf = 0.5 * (1.0 + lax.erf(pre_act * (1.0 / math.sqrt(2.0))))
    density = jnp.exp(-0.5 * pre_act * pre_act) * (1.0 / math.sqrt(2.0 * math.pi))
    hidden = (pre_act * normal_cdf).astype(BF16)
    slope = normal_cdf + pre_act * density
    hidden, slope = then.done(hidden, slope)
    upstream = then.done(frame_rows(upstream_low, then(upstream_other), order))
    fc2_blocks = then.done(*grad_blocks((then(upstream), hidden)))
    then.close(fc2_near, attention_far, fc2_core)

    def row_block_of(index):
        place, bit = 0 * index, 1
        while bit < tp_size:
            place = place * 2 + (index // bit) % 2
            bit *= 2
        return place

    def flips_to_places(flips):
        return jnp.stack([row_block_of(tp_index ^ f) for f in flips]).astype(jnp.int32)

    fc2_far = far_of("fc2", then(fc2_near), fc2_packs)
    fc2_pieces = [fc2_packs[0], fc2_core, fc2_near, fc2_far]
    fc2_grad_near = swap(then(fc2_blocks[2]), 1)
    qkv_bias_own = half_of(qkv_bias, core, 1).astype(F32).reshape(1, 3 * HD)
    queries, both_local = then.done(
        *project(then(normed), attention, qkv_bias_own, cosine_table, sine_table)
    )
    both_local = both_local.reshape(2, row_count, 2 * HD)
    if pairs:
        both_other = ctx_pair(both_local)
    else:
        both_other = lax.all_gather(both_local, "ctx", axis=1, tiled=True)
    attended_grad = then.done(attended_grads(then(upstream), attention, valid))
    then.close(fc2_far, fc2_grad_near)

    fc2_grad_far = swap(then(fc2_blocks[0]), 2)
    hidden_grad = dot(then(upstream), joined(fc2_pieces), ((1,), (0,)))
    pre_grad = then.done((hidden_grad * slope).astype(BF16))
    both_other = then(both_other)
    attended, probs_all = [], []
    if pairs:
        both = (both_local, both_other)
        key_parts = key_places[:, :, :row_count], key_places[:, :, row_count:]
        attended = then.done(attend(queries, both, row_places, key_parts, valid))
    else:
        for s in range(2):
            rows = slice(s * row_count, (s + 1) * row_count)
            keys, values = both_other[s, :, :HD], both_other[s, :, HD:]
            scores = dot(queries[rows], keys, ((1,), (1,))) * score_scale
            scores = jnp.where(allowed[s], scores, MASK_FLOOR)
            exp_scores = jnp.exp(scores - jnp.max(scores, axis=1, keepdims=True))
            probs = exp_scores / jnp.sum(exp_scores, axis=1, keepdims=True)
            probs_all.append(probs)
            attended.append(dot(probs.astype(BF16), values, ((1,), (0,))))
        attended = then.done((jnp.concatenate(attended) * valid).astype(BF16))
    hidden_size = hidden.shape[1]
    second = (hidden, fc2_pieces, 0, hidden_size)
    theirs = then.done(share_rows((attended, attention, 3, HD), second, row_count))
    then.close(fc2_grad_far)

    def attention_grads(s, into=()):
        if pairs:
            return then.done(
                *attend_back(s, queries, both, row_places, key_parts, then(attended_grad), into)
            )
        rows = slice(s * row_count, (s + 1) * row_count)
        keys, values = both_other[s, :, :HD], both_other[s, :, HD:]
        probs, head_grad = probs_all[s], then(attended_grad[rows])
        prob_grad = dot(head_grad, values, ((1,), (1,)))
        row_delta = jnp.sum(probs * prob_grad, axis=1, keepdims=True)
        score_grad = (probs * (prob_grad - row_delta)).astype(BF16)
        query_piece = dot(score_grad, keys, ((1,), (0,))) * score_scale
        key_piece = dot(score_grad, queries[rows], ((0,), (0,))) * score_scale
        value_piece = dot(probs.astype(BF16), head_grad, ((0,), (0,)))
        return then.done(query_piece, jnp.concatenate([key_piece, value_piece], axis=1))

    low = tp_index % 2

    def halve_on(kept, got, bit, row_block):
        while bit < tp_size:
            digit = (tp_index // bit) % 2
            given, kept = then.done(*halve_rows(digit, kept, got))
            got, row_block, bit = tp_pair(given, bit), row_block * 2 + digit, bit * 2
        return kept, got, row_block

    def double_up(part):
        pieces, flips, bit = [part], [0], tp_size // 2
        while bit > 1:
            pieces += [tp_pair(p, bit) for p in pieces]
            flips += [f ^ bit for f in flips]
            bit //= 2
        return pieces, flips + [f ^ 1 for f in flips]

    def fc1_block(k, kind=BF16):
        return weight_grad(k, shard, [(then(normed), pre_grad)], kind)

    fc2_grad_farther = swap(then(fc2_blocks[1]), 3)
    theirs = swap(then(theirs), 1)
    fc2_mine = ctx_terms(add_mine(fc2_blocks[3], fc2_grad_far))
    grads_first = attention_grads(0)
    first = (then(attended), attention, 3, HD)
    given, kept = then.done(*share_rows(first, second, row_count, theirs, low))
    fc1_far_block = then.done(grad_block(2 + side, (then(normed), pre_grad)))
    then.close(fc2_grad_farther)

    fc1_grad_far = swap(then(fc1_far_block), 2)
    out_got = tp_pair(then(given), 1)
    if pairs:
        query_grad, both_grad, both_given = attention_grads(1, grads_first)
        both_got = ctx_pair(both_given)
    else:
        grads_second = attention_grads(1)
        both_grad = jnp.stack([grads_first[1], grads_second[1]])
        query_grad = jnp.concatenate([grads_first[0], grads_second[0]])
        both_got = jnp.zeros((2, row_count, 2 * HD), BF16)
        both_grad = lax.psum_scatter(both_grad, "ctx", scatter_dimension=1, tiled=True)
        query_grad, both_grad = then.done(query_grad, both_grad)
    fc1_farther_block = then.done(grad_block(3 - side, (then(normed), pre_grad)))
    fc1_near_block = then.done(grad_block(1, (then(normed), pre_grad)))
    fc1_grad_near = swap(fc1_near_block, 1)
    fc1_own_block = then.done(fc1_block(0, F32))
    fc2_theirs = add_theirs(fc2_grad_near, fc2_grad_farther)
    then.close(fc1_grad_far, out_got, fc2_mine[1])

    fc1_grad_farther = swap(then(fc1_farther_block), 3)
    out_kept, out_got, out_block = halve_on(then(kept), out_got, 2, low)
    fc2_theirs = ctx_terms(then(fc2_theirs))
    proj_grad = then.done(
        turn_back(then(query_grad), both_grad, both_got, cosine_table, sine_table)
    )
    second = (pre_grad, fc1_pieces, 0, hidden_size)
    theirs = then.done(share_rows((proj_grad, attention, 0, 3 * HD), second, row_count))

    def attention_block(k, kind=BF16):
        return weight_grad(k, shard, [(then(normed), proj_grad), (upstream, attended)], kind)

    far_block = then.done(attention_block(2 + side))
    fc1_mine = add_mine(fc1_own_block, fc1_grad_far)
    then.close(fc1_grad_farther, out_got, fc2_theirs[1], fc1_grad_near)

    attention_grad_far = swap(then(far_block), 2)
    theirs = swap(then(theirs), 1)
    fc1_mine = ctx_terms(then(fc1_mine))
    out_part = then.done(
        finish_output(order, out_block, then(out_kept), out_got, inputs_low, out_bias)
    )
    out_pieces, flips = double_up(out_part)
    out_late = [tp_pair(out_part, 1)]
    first = (then(proj_grad), attention, 0, 3 * HD)
    given, kept = then.done(*share_rows(first, second, row_count, theirs, low))
    farther_block = then.done(attention_block(3 - side))
    fc1_theirs = add_theirs(fc1_grad_near, fc1_grad_farther)
    then.close(attention_grad_far, out_late[0], *out_pieces[1:], fc1_mine[1])

    attention_grad_farther = swap(then(farther_block), 3)
    got = tp_pair(then(given), 1)
    fc1_theirs = ctx_terms(then(fc1_theirs))
    norm_near, norm_far = then.done(*norm_grads(order, low, side, then(inputs_low), given, kept))
    sums, sums_given = then.done(
        *pack_sums(
            (norm_near, norm_far), (upstream_near, upstream_far), then(pre_grad), proj_grad
        )
    )
    sums_got = swap(sums_given, 2)
    near_block = then.done(attention_block(1))
    attention_grad_near = swap(near_block, 1)
    own_block = then.done(attention_block(0, kind=F32))
    attention_mine = add_mine(own_block, attention_grad_far)
    then.close(attention_grad_farther, got, fc1_theirs[1], sums_got)

    attention_mine = ctx_terms(then(attention_mine))
    kept, got, row_block = halve_on(then(kept), got, 2, low)
    out_late += [tp_pair(p, 1) for p in then(out_pieces[0], *out_pieces[1:])[1:]]
    sums = then(sums) + sums_got
    norm_sums, other_sums = sums[:2], sums[2:]
    norm_sums = norm_sums + tp_pair(norm_sums, 1)
    attention_theirs = add_theirs(attention_grad_near, attention_grad_farther)
    fc2_out = placed(fc2_mine, fc2_theirs)
    then.close(got, norm_sums, attention_mine[1], *out_late[1:])

    attention_theirs = ctx_terms(then(attention_theirs))
    input_part = then.done(
        finish_input_grad(order, row_block, then(kept), got, inputs_low, upstream_low, norm_gain)
    )
    pieces, _ = double_up(input_part)
    late = [tp_pair(input_part, 1)]
    bit = 2
    while bit < tp_size:
        norm_sums = norm_sums + tp_pair(then(norm_sums), bit)
        bit *= 2
    fc1_out = placed(fc1_mine, fc1_theirs)
    output = then.done(gather_rows(then(*out_pieces, *out_late), flips_to_places(flips), tp_size, BF16))
    then.close(*pieces[1:], late[0], norm_sums, attention_theirs[1])

    late += [tp_pair(p, 1) for p in then(*pieces, output)[1 : len(pieces)]]
    sums = sum(ctx_terms(jnp.concatenate([then(norm_sums), other_sums])))
    early = len(pieces) + 1
    places = flips_to_places(flips)
    input_grad = then.done(
        gather_rows(then(*pieces, late[0]), places[:early], tp_size, F32)
    )
    qkv_out, dense_out = placed(attention_mine, attention_theirs, True)
    then.close(*late[1:])

    other_core = swap(sums, 1)
    vector_sums = sums[:3, :shard] + other_core[:3, shard : 2 * shard]

    def column_sums(packed):
        return packed[3, :hidden_size], packed[4, : 3 * HD].reshape(3, HD)

    rest = then(*late)[1:]
    input_grad = gather_rows(rest, places[early:], tp_size, F32, (input_grad,))

    def in_order(mine, other, axis):
        return jnp.where(
            core == 0,
            jnp.concatenate([mine, other], axis=axis),
            jnp.concatenate([other, mine], axis=axis),
        )

    fc1_bias_grad, qkv_bias_grad = [
        in_order(mine, other, axis)
        for axis, mine, other in zip((0, 1), column_sums(sums), column_sums(other_core))
    ]
    return (
        output[None],
        input_grad[None],
        vector_sums[0],
        vector_sums[1],
        qkv_out.transpose(1, 0, 2),
        qkv_bias_grad,
        dense_out,
        vector_sums[2],
        fc1_out,
        fc1_bias_grad,
        fc2_out,
        vector_sums[2],
    )


def solution(mesh):
    placed = (
        P("fsdp", "ctx", None),
        P("fsdp", None),
        P("fsdp", None),
        P("fsdp"),
        P("fsdp"),
        P("fsdp", None, "tp"),
        P(None, "tp"),
        P("fsdp", "tp"),
        P("fsdp"),
        P("fsdp", "tp"),
        P("tp"),
        P("fsdp", "tp"),
        P("fsdp"),
        P("fsdp", "ctx", None),
    )
    return jax.shard_map(
        per_device,
        mesh=mesh,
        in_specs=placed,
        out_specs=(
            P("fsdp", "ctx", None),
            P("fsdp", "ctx", None),
            P("fsdp"),
            P("fsdp"),
            P("fsdp", None, "tp"),
            P(None, "tp"),
            P("fsdp", "tp"),
            P("fsdp"),
            P("fsdp", "tp"),
            P("tp"),
            P("fsdp", "tp"),
            P("fsdp"),
        ),
        check_vma=False,
    )
```

```python
import math

import jax
import jax.numpy as jnp
from jax import lax
from jax.experimental import pallas as pl
from jax.experimental.pallas import tpu as pltpu
from jax.sharding import PartitionSpec as P

HD = 256
ROT = 64


NORM_EPSILON = 1e-05
MASK_FLOOR = -1000000000.0
F32 = jnp.float32
BF16 = jnp.bfloat16
LANES = 128
RELAY = {"attention": True, "fc1": True, "fc2": False}


def rotation_tables(position):
    half = ROT // 2
    frequency = jnp.exp(jnp.arange(half, dtype=F32) * (-2.0 * math.log(10000.0) / ROT))
    angles = position.astype(F32)[:, None] * frequency[None, :]
    cosine, sine = jnp.cos(angles), jnp.sin(angles)
    rest = (position.shape[0], LANES - ROT)
    return (
        jnp.concatenate([cosine, cosine, jnp.ones(rest, F32)], axis=1),
        jnp.concatenate([-sine, sine, jnp.zeros(rest, F32)], axis=1),
    )


def packed_rows(order_row, slots, block_rows):
    selector = slots[:, None] == jnp.arange(order_row.shape[0], dtype=jnp.int32)[None, :]
    source_block = jnp.sum(jnp.where(selector, order_row[None, :], 0), axis=1, dtype=jnp.int32)
    within = jnp.arange(block_rows, dtype=jnp.int32)
    return (source_block[:, None] * block_rows + within[None, :]).reshape(-1)


def place_rows(packed_at, lengths_row):
    seq_ends = jnp.cumsum(lengths_row, dtype=jnp.int32)
    passed = packed_at[:, None] >= seq_ends[None, :]
    segment = jnp.sum(passed.astype(jnp.int32), axis=1, dtype=jnp.int32)
    before = jnp.sum(jnp.where(passed, lengths_row[None, :], 0), axis=1, dtype=jnp.int32)
    return (segment, packed_at - before)


def dot(a, b, contract):
    return lax.dot_general(a, b, (contract, ((), ())), preferred_element_type=F32)


def fsdp_permute(x, bits):
    size, lanes = lax.axis_size("fsdp"), lax.axis_size("ctx")
    perm = [
        (f * lanes + x, (f ^ bits[x % 2]) * lanes + x) for f in range(size) for x in range(lanes)
    ]
    return lax.ppermute(x, ("fsdp", "ctx"), perm)


def swap(x, bit):
    return fsdp_permute(x, (bit, bit))


def ctx_pair(x):
    return lax.ppermute(x, "ctx", [(0, 1), (1, 0)])


def ctx_terms(x):
    if lax.axis_size("ctx") == 2:
        return x, ctx_pair(x)
    return lax.psum(x.astype(F32), "ctx"), jnp.zeros_like(x)


def tp_pair(x, bit):
    return lax.ppermute(x, "tp", [(i, i ^ bit) for i in range(lax.axis_size("tp"))])


def half_of(x, which, axis):
    size = x.shape[axis] // 2
    return lax.dynamic_slice_in_dim(x, which * size, size, axis=axis)


def kernel_call(body, scalars, arrays, in_specs, out_shape, out_specs, grid, name, scratch=(), aliases=None):
    return pl.pallas_call(
        body,
        out_shape=out_shape,
        grid_spec=pltpu.PrefetchScalarGridSpec(
            num_scalar_prefetch=1,
            grid=grid,
            in_specs=in_specs,
            out_specs=out_specs,
            scratch_shapes=scratch,
        ),
        input_output_aliases=aliases or {},
        cost_estimate=pl.CostEstimate(flops=0, transcendentals=0, bytes_accessed=0),
        name=name,
    )(scalars, *arrays)


def aligned(index, size):
    return pl.ds(pl.multiple_of(index * size, size), size)


def frame_rows(own, other, order, norm=None):
    rows, columns = own.shape
    width, step = columns // 4, rows // 2

    def kernel(order_ref, own_ref, other_ref, *refs):
        gain_ref, bias_ref, out_ref, wide_ref = refs if norm else (None, None, refs[0], None)
        for s, ref in enumerate((own_ref, other_ref)):
            if norm:
                x = ref[...].astype(F32)
                x = x - jnp.mean(x, axis=1, keepdims=True)
                variance = jnp.mean(x * x, axis=1, keepdims=True)
                wide_ref[...] = x * lax.rsqrt(variance + NORM_EPSILON)
            for k in range(4):
                to = slice(k * width, (k + 1) * width)
                at = aligned(order_ref[k], width)
                if norm:
                    out_ref[s, :, to] = (
                        wide_ref[:, at] * gain_ref[:, to] + bias_ref[:, to]
                    ).astype(BF16)
                else:
                    out_ref[s, :, to] = ref[:, at]

    row_spec = pl.BlockSpec((step, columns), lambda r, o: (r, 0))
    vector_spec = pl.BlockSpec((1, columns), lambda r, o: (0, 0))
    out = kernel_call(
        kernel,
        order,
        (own, other, *(norm or ())),
        [row_spec, row_spec] + ([vector_spec, vector_spec] if norm else []),
        jax.ShapeDtypeStruct((2, rows, columns), BF16),
        pl.BlockSpec((2, step, columns), lambda r, o: (0, r, 0)),
        (2,),
        "norm_rows" if norm else "frame_rows",
        scratch=[pltpu.VMEM((step, columns), F32)] if norm else (),
    )
    return out.reshape(2 * rows, columns)


def place_grad(parts, core, attention):
    rows, columns = parts[0].shape
    step = rows // 2

    def kernel(core_ref, a_ref, ax_ref, b_ref, bx_ref, *out_refs):
        for h, (u_ref, ux_ref) in enumerate(((a_ref, ax_ref), (b_ref, bx_ref))):
            total = u_ref[...].astype(F32) + ux_ref[...].astype(F32)
            place = core_ref[0] ^ h
            if attention:
                for t in range(3):
                    out_refs[0][t, :, aligned(place, HD)] = total[:, t * HD : (t + 1) * HD]
                out_refs[1][:, aligned(place, HD)] = total[:, 3 * HD :]
            else:
                out_refs[0][:, aligned(place, columns)] = total

    shapes = [(rows, 2 * columns)]
    specs = [pl.BlockSpec((step, 2 * columns), lambda r, c: (r, 0))]
    if attention:
        shapes = [(3, rows, 2 * HD), (rows, 2 * HD)]
        specs = [
            pl.BlockSpec((3, step, 2 * HD), lambda r, c: (0, r, 0)),
            pl.BlockSpec((step, 2 * HD), lambda r, c: (r, 0)),
        ]
    return kernel_call(
        kernel,
        core[None],
        parts,
        [pl.BlockSpec((step, columns), lambda r, c: (r, 0))] * 4,
        [jax.ShapeDtypeStruct(shape, F32) for shape in shapes],
        specs,
        (2,),
        "place_grad",
    )


def weight_grad(block, shard, products, kind):
    step = shard // 2
    widths = [right.shape[1] for _, right in products]

    def kernel(_, *refs):
        at = 0
        for n, width in enumerate(widths):
            left_ref, right_ref = refs[2 * n : 2 * n + 2]
            total = dot(left_ref[...], right_ref[...], ((0,), (0,)))
            refs[-1][:, at : at + width] = total.astype(kind)
            at += width

    specs = []
    for left, right in products:
        specs.append(pl.BlockSpec((left.shape[0], step), lambda n, k: (0, 2 * k[0] + n)))
        specs.append(pl.BlockSpec(right.shape, lambda n, k: (0, 0)))
    return kernel_call(
        kernel,
        jnp.asarray(block, jnp.int32)[None],
        [a for product in products for a in product],
        specs,
        jax.ShapeDtypeStruct((shard, sum(widths)), kind),
        pl.BlockSpec((step, sum(widths)), lambda n, k: (n, 0)),
        (2,),
        "weight_grad",
    )


def share_rows(first, second, rows, theirs=None, low=None):
    width = first[1][0].shape[0]
    own = theirs is not None
    at = 0 if own else 1
    half = rows // 2

    def kernel(low_ref, f_ref, s_ref, *refs):
        f_refs, s_refs, refs = refs[:4], refs[4:8], refs[8:]
        for n in range(2):

            @pl.when(pl.program_id(0) == n)
            def _(n=n):
                for m in range(2):
                    k = 2 * n + m
                    total = dot(f_ref[...], f_refs[k][...], ((1,), (1,)))
                    total = total + dot(s_ref[...], s_refs[k][...], ((1,), (1,)))
                    if not own:
                        refs[0][:, (1 - m) * width : (2 - m) * width] = total.astype(BF16)
                        continue
                    theirs_ref, given_ref, kept_ref, all_ref = refs
                    to = slice(m * width, (m + 1) * width)
                    all_ref[...] = (total + theirs_ref[:, to].astype(F32)).astype(BF16)
                    given_ref[:, to] = all_ref[aligned(1 - low_ref[0], half), :]
                    kept_ref[:, to] = all_ref[aligned(low_ref[0], half), :]

    arrays, in_specs = [], []
    for acts, _, _, size in (first, second):
        arrays.append(acts)
        in_specs.append(pl.BlockSpec((rows, size), lambda n, b: (at, 0)))
    for _, pieces, block, size in (first, second):
        arrays += pieces
        in_specs += [pl.BlockSpec((width, size), lambda n, b, block=block: (0, block))] * 4
    out_shape = jax.ShapeDtypeStruct((rows, 4 * width), BF16)
    out_spec = pl.BlockSpec((rows, 2 * width), lambda n, b: (0, n))
    scratch = ()
    if own:
        arrays.append(theirs)
        in_specs.append(out_spec)
        out_shape = [jax.ShapeDtypeStruct((half, 4 * width), BF16)] * 2
        out_spec = [pl.BlockSpec((half, 2 * width), lambda n, b: (0, n))] * 2
        scratch = [pltpu.VMEM((rows, width), BF16)]
    return kernel_call(
        kernel,
        low[None] if own else jnp.zeros((1,), jnp.int32),
        arrays,
        in_specs,
        out_shape,
        out_spec,
        (2,),
        "share_rows",
        scratch=scratch,
    )


def finish_output(order, row_block, kept, got, inputs, out_bias):
    rows, columns = kept.shape
    width, steps = columns // 4, 1
    step = rows // steps

    def kernel(s_ref, kept_ref, got_ref, x_ref, bias_ref, out_ref):
        for k in range(4):
            cols, at = slice(k * width, (k + 1) * width), aligned(s_ref[k], width)
            total = kept_ref[:, cols] + got_ref[:, cols].astype(F32)
            out_ref[:, at] = (x_ref[:, at].astype(F32) + total + bias_ref[:, cols]).astype(BF16)

    spec = pl.BlockSpec((step, columns), lambda i, s: (i, 0))
    return kernel_call(
        kernel,
        jnp.concatenate([order, row_block[None]]),
        (kept, got, inputs, out_bias),
        [
            spec,
            spec,
            pl.BlockSpec((step, columns), lambda i, s: (s[4] * steps + i, 0)),
            pl.BlockSpec((1, columns), lambda i, s: (0, 0)),
        ],
        jax.ShapeDtypeStruct((rows, columns), BF16),
        spec,
        (steps,),
        "finish_output",
    )


def finish_input_grad(order, row_block, kept, got, inputs, upstream, norm_gain):
    rows, columns = kept.shape
    width, steps = columns // 4, 1
    step = rows // steps

    def kernel(s_ref, kept_ref, got_ref, x_ref, dy_ref, gain_ref, out_ref, std_ref):
        x = x_ref[...].astype(F32)
        x = x - jnp.mean(x, axis=1, keepdims=True)
        inverse = lax.rsqrt(jnp.mean(x * x, axis=1, keepdims=True) + NORM_EPSILON)
        std_ref[...] = x * inverse
        mean_scaled = jnp.zeros((step, 1), F32)
        mean_product = jnp.zeros((step, 1), F32)

        def parts(k):
            cols, at = slice(k * width, (k + 1) * width), aligned(s_ref[k], width)
            total = kept_ref[:, cols] + got_ref[:, cols].astype(F32)
            return at, total * gain_ref[:, cols], std_ref[:, at]

        for k in range(4):
            _, scaled, standard = parts(k)
            mean_scaled += jnp.sum(scaled, axis=1, keepdims=True) / columns
            mean_product += jnp.sum(scaled * standard, axis=1, keepdims=True) / columns
        for k in range(4):
            at, scaled, standard = parts(k)
            change = inverse * (scaled - mean_scaled - standard * mean_product)
            out_ref[:, at] = (dy_ref[:, at].astype(F32) + change).astype(BF16)

    spec = pl.BlockSpec((step, columns), lambda i, s: (i, 0))
    rows_spec = pl.BlockSpec((step, columns), lambda i, s: (s[4] * steps + i, 0))
    return kernel_call(
        kernel,
        jnp.concatenate([order, row_block[None]]),
        (kept, got, inputs, upstream, norm_gain),
        [spec, spec, rows_spec, rows_spec, pl.BlockSpec((1, columns), lambda i, s: (0, 0))],
        jax.ShapeDtypeStruct((rows, columns), BF16),
        spec,
        (steps,),
        "finish_input_grad",
        scratch=[pltpu.VMEM((step, columns), F32)],
    )


def norm_grads(order, low, side, inputs, given, kept):
    rows, columns = inputs.shape
    width, step = columns // 4, rows // 2

    def kernel(order_ref, x_ref, given_ref, kept_ref, near_ref, far_ref, std_ref):
        x = x_ref[...].astype(F32)
        x = x - jnp.mean(x, axis=1, keepdims=True)
        std_ref[...] = x * lax.rsqrt(jnp.mean(x * x, axis=1, keepdims=True) + NORM_EPSILON)

        def add(share_ref, first):
            for k in range(4):
                cols = slice(k * width, (k + 1) * width)
                part = share_ref[:, cols].astype(F32)
                product = part * std_ref[:, aligned(order_ref[k], width)]
                sums = jnp.sum(product, axis=0, keepdims=True), jnp.sum(part, axis=0, keepdims=True)
                out_ref, at = near_ref, cols
                if k > 1:
                    out_ref, at = far_ref, aligned((k - 2) ^ order_ref[5], width)
                for n in range(2):
                    before = 0.0 if first else out_ref[n : n + 1, at]
                    out_ref[n : n + 1, at] = before + sums[n]

        @pl.when(pl.program_id(0) == 0)
        def _():
            add(given_ref, True)

        @pl.when(pl.program_id(0) == 1)
        def _():
            add(kept_ref, False)

    half_spec = pl.BlockSpec((step, columns), lambda r, o: (0, 0))
    return kernel_call(
        kernel,
        jnp.concatenate([order, low[None], side[None].astype(jnp.int32)]),
        (inputs, given, kept),
        [
            pl.BlockSpec((step, columns), lambda r, o: (r * o[4] + (1 - r) * (1 - o[4]), 0)),
            half_spec,
            half_spec,
        ],
        [jax.ShapeDtypeStruct((2, columns // 2), F32)] * 2,
        [pl.BlockSpec((2, columns // 2), lambda r, o: (0, 0))] * 2,
        (2,),
        "norm_grads",
        scratch=[pltpu.VMEM((step, columns), F32)],
    )


def halve_rows(digit, kept, got):
    rows, columns = kept.shape

    def kernel(_, a_ref, b_ref, c_ref, d_ref, given_ref, kept_ref):
        given_ref[...] = (a_ref[...].astype(F32) + b_ref[...].astype(F32)).astype(BF16)
        kept_ref[...] = c_ref[...].astype(F32) + d_ref[...].astype(F32)

    block = rows // 2, columns // 2
    leaves = pl.BlockSpec(block, lambda n, d: (1 - d[0], n))
    stays = pl.BlockSpec(block, lambda n, d: (d[0], n))
    out_spec = pl.BlockSpec(block, lambda n, d: (0, n))
    return kernel_call(
        kernel,
        digit[None],
        (kept, got, kept, got),
        [leaves, leaves, stays, stays],
        [jax.ShapeDtypeStruct((rows // 2, columns), kind) for kind in (BF16, F32)],
        [out_spec, out_spec],
        (2,),
        "halve_rows",
    )


def pack_sums(norm_sums, upstream_sums, pre_grad, proj_grad):
    wide = max(norm_sums[0].shape[1], pre_grad.shape[1], proj_grad.shape[1])
    step = pre_grad.shape[0] // 8

    def kernel(_, *refs):
        norm_refs, up_refs, grad_refs, out_refs = refs[:2], refs[2:4], refs[4:6], refs[6:]
        for out_ref in out_refs:
            out_ref[...] = jnp.zeros_like(out_ref)
        for norm_ref, up_ref, out_ref in zip(norm_refs, up_refs, out_refs):
            out_ref[0:2, : norm_ref.shape[1]] = norm_ref[...]
            out_ref[2:3, : up_ref.shape[1]] = up_ref[...]
        for n, ref in enumerate(grad_refs):
            total = jnp.zeros((1, ref.shape[1]), F32)
            for c in range(8):
                part = ref[c * step : (c + 1) * step, :].astype(F32)
                total = total + jnp.sum(part, axis=0, keepdims=True)
            for out_ref in out_refs:
                out_ref[3 + n : 4 + n, : ref.shape[1]] = total

    arrays = (*norm_sums, *upstream_sums, pre_grad, proj_grad)
    return kernel_call(
        kernel,
        jnp.zeros((1,), jnp.int32),
        arrays,
        [pl.BlockSpec(a.shape, lambda n, z: (0, 0)) for a in arrays],
        [jax.ShapeDtypeStruct((8, wide), F32)] * 2,
        [pl.BlockSpec((8, wide), lambda n, z: (0, 0))] * 2,
        (1,),
        "pack_sums",
    )


def gather_rows(pieces, places, count, dtype, into=()):
    rows, columns = pieces[0].shape

    def kernel(_, *refs):
        for n in range(len(pieces)):

            @pl.when(pl.program_id(0) == n)
            def _(n=n):
                refs[-1][...] = refs[n][...].astype(dtype)

    return kernel_call(
        kernel,
        places,
        (*pieces, *into),
        [pl.BlockSpec((rows, columns), lambda n, p: (0, 0))] * len(pieces)
        + [pl.BlockSpec(memory_space=pl.ANY)] * len(into),
        jax.ShapeDtypeStruct((rows * count, columns), dtype),
        pl.BlockSpec((rows, columns), lambda n, p: (p[n], 0)),
        (len(pieces),),
        "gather_rows",
        aliases={1 + len(pieces): 0} if into else None,
    )


def turned(x, cosine, sine):
    lane = lax.broadcasted_iota(jnp.int32, x.shape, 1)
    half = ROT // 2
    partner = jnp.where(
        lane < half, pltpu.roll(x, x.shape[1] - half, axis=1), pltpu.roll(x, half, axis=1)
    )
    return x * cosine + partner * sine


def project(normed, pieces, bias, cosine, sine):
    rows = normed.shape[0] // 2
    width = pieces[0].shape[0]

    def kernel(_, x_ref, *refs):
        piece_refs, (bias_ref, cos_ref, sin_ref, q_ref, kv_ref) = refs[:4], refs[4:]
        total = dot(x_ref[:, :width], piece_refs[0][...], ((1,), (0,)))
        for k in range(1, 4):
            cols = slice(k * width, (k + 1) * width)
            total = total + dot(x_ref[:, cols], piece_refs[k][...], ((1,), (0,)))
        total = total + bias_ref[...]
        cosine, sine = cos_ref[...], sin_ref[...]
        for n, ref in enumerate((q_ref, kv_ref)):
            head = total[:, n * HD : (n + 1) * HD]
            ref[:, :LANES] = turned(head[:, :LANES], cosine, sine).astype(BF16)
            ref[:, LANES:HD] = head[:, LANES:].astype(BF16)
        kv_ref[:, HD:] = total[:, 2 * HD :].astype(BF16)

    def by_row(columns):
        return pl.BlockSpec((rows, columns), lambda s, z: (s, 0))

    return kernel_call(
        kernel,
        jnp.zeros((1,), jnp.int32),
        (normed, *pieces, bias, cosine, sine),
        [by_row(normed.shape[1])]
        + [pl.BlockSpec((width, 3 * HD), lambda s, z: (0, 0))] * 4
        + [pl.BlockSpec((1, 3 * HD), lambda s, z: (0, 0)), by_row(LANES), by_row(LANES)],
        [
            jax.ShapeDtypeStruct((2 * rows, HD), BF16),
            jax.ShapeDtypeStruct((2 * rows, 2 * HD), BF16),
        ],
        [by_row(HD), by_row(2 * HD)],
        (2,),
        "project",
    )


def turn_back(query_grad, kept, got, cosine, sine):
    rows = kept.shape[1]

    def kernel(_, q_ref, kept_ref, got_ref, cos_ref, sin_ref, out_ref):
        both = kept_ref[...] + got_ref[...].astype(F32)
        cosine, sine = cos_ref[...], -sin_ref[...]
        for n, head in enumerate((q_ref[...], both[:, :HD])):
            at = n * HD
            out_ref[:, at : at + LANES] = turned(head[:, :LANES], cosine, sine).astype(BF16)
            out_ref[:, at + LANES : at + HD] = head[:, LANES:].astype(BF16)
        out_ref[:, 2 * HD :] = both[:, HD:].astype(BF16)

    def by_row(columns):
        return pl.BlockSpec((rows, columns), lambda s, z: (s, 0))

    both_spec = pl.BlockSpec((None, rows, 2 * HD), lambda s, z: (s, 0, 0))
    return kernel_call(
        kernel,
        jnp.zeros((1,), jnp.int32),
        (query_grad, kept, got, cosine, sine),
        [by_row(HD), both_spec, both_spec, by_row(LANES), by_row(LANES)],
        jax.ShapeDtypeStruct((2 * rows, 3 * HD), BF16),
        by_row(3 * HD),
        (2,),
        "turn_back",
    )


def attended_grads(upstream, pieces, valid):
    rows = upstream.shape[0] // 2
    width = pieces[0].shape[0]

    def kernel(_, dy_ref, *refs):
        piece_refs, (valid_ref, out_ref) = refs[:4], refs[4:]
        total = dot(dy_ref[:, :width], piece_refs[0][...], ((1,), (0,)))
        for k in range(1, 4):
            cols = slice(k * width, (k + 1) * width)
            total = total + dot(dy_ref[:, cols], piece_refs[k][...], ((1,), (0,)))
        out_ref[...] = total.astype(BF16) * valid_ref[...].astype(BF16)

    def by_row(columns):
        return pl.BlockSpec((rows, columns), lambda s, z: (s, 0))

    return kernel_call(
        kernel,
        jnp.zeros((1,), jnp.int32),
        (upstream, *pieces, valid),
        [by_row(upstream.shape[1])]
        + [pl.BlockSpec((width, HD), lambda s, z: (0, 3))] * 4
        + [by_row(1)],
        jax.ShapeDtypeStruct((2 * rows, HD), BF16),
        by_row(HD),
        (2,),
        "attended_grads",
    )


def chances(query, keys, first, last, key_place):
    scores = []
    for part, place in zip(keys, key_place):
        score = dot(query, part, ((1,), (1,))) * (1.0 / math.sqrt(HD))
        scores.append(jnp.where((place >= first) & (place <= last), score, MASK_FLOOR))
    top = jnp.max(scores[0], axis=1, keepdims=True)
    for score in scores[1:]:
        top = jnp.maximum(top, jnp.max(score, axis=1, keepdims=True))
    exps = [jnp.exp(score - top) for score in scores]
    total = sum(jnp.sum(e, axis=1, keepdims=True) for e in exps)
    return [e / total for e in exps]


def attention_specs(rows, parts):
    return (
        [pl.BlockSpec((rows, HD), lambda n, s: (n + s[0], 0))]
        + [pl.BlockSpec((None, rows, 2 * HD), lambda n, s: (n + s[0], 0, 0))] * parts
        + [pl.BlockSpec((None, rows, 2), lambda n, s: (n + s[0], 0, 0))]
        + [pl.BlockSpec((None, 1, rows), lambda n, s: (n + s[0], 0, 0))] * parts
    )


def attend(queries, both, row_places, key_places, valid):
    rows = queries.shape[0] // 2
    parts = len(both)

    def kernel(_, q_ref, *refs):
        both_refs, place_ref, key_refs = refs[:parts], refs[parts], refs[parts + 1 : 2 * parts + 1]
        valid_ref, out_ref = refs[2 * parts + 1 :]
        step = rows // 2
        for c in range(2):
            at = slice(c * step, (c + 1) * step)
            probs = chances(
                q_ref[at, :],
                [ref[:, :HD] for ref in both_refs],
                place_ref[at, 0:1],
                place_ref[at, 1:2],
                [ref[...] for ref in key_refs],
            )
            total = 0.0
            for p, ref in zip(probs, both_refs):
                total = total + dot(p.astype(BF16), ref[:, HD:], ((1,), (0,)))
            out_ref[at, :] = (total * valid_ref[at, :]).astype(BF16)

    return kernel_call(
        kernel,
        jnp.zeros((1,), jnp.int32),
        (queries, *both, row_places, *key_places, valid),
        attention_specs(rows, parts) + [pl.BlockSpec((rows, 1), lambda n, s: (n, 0))],
        jax.ShapeDtypeStruct(queries.shape, BF16),
        pl.BlockSpec((rows, HD), lambda n, s: (n, 0)),
        (2,),
        "attend",
    )


def attend_back(s, queries, both, row_places, key_places, attended_grad, into=()):
    rows = queries.shape[0] // 2
    scale = 1.0 / math.sqrt(HD)

    def kernel(_, q_ref, own_ref, far_ref, place_ref, own_key_ref, far_key_ref, up_ref, *outs):
        query_ref, kept_ref, given_ref = outs[-3:]
        step = rows // 2
        sums = [[0.0, 0.0], [0.0, 0.0]]
        for c in range(2):
            at = slice(c * step, (c + 1) * step)
            query, up = q_ref[at, :], up_ref[at, :]
            probs = chances(
                query,
                [own_ref[:, :HD], far_ref[:, :HD]],
                place_ref[at, 0:1],
                place_ref[at, 1:2],
                [own_key_ref[...], far_key_ref[...]],
            )
            grads = [dot(up, ref[:, HD:], ((1,), (1,))) for ref in (own_ref, far_ref)]
            delta = sum(jnp.sum(p * g, axis=1, keepdims=True) for p, g in zip(probs, grads))
            total = 0.0
            for n, ref in enumerate((own_ref, far_ref)):
                score_grad = (probs[n] * (grads[n] - delta)).astype(BF16)
                total = total + dot(score_grad, ref[:, :HD], ((1,), (0,)))
                sums[n][0] = sums[n][0] + dot(score_grad, query, ((0,), (0,)))
                sums[n][1] = sums[n][1] + dot(probs[n].astype(BF16), up, ((0,), (0,)))
            query_ref[at, :] = total * scale
        for n, ref in enumerate((kept_ref, given_ref)):
            ref[:, :HD] = (sums[n][0] * scale).astype(ref.dtype)
            ref[:, HD:] = sums[n][1].astype(ref.dtype)

    both_spec = pl.BlockSpec((None, rows, 2 * HD), lambda n, s: (n + s[0], 0, 0))
    row_spec = pl.BlockSpec((rows, HD), lambda n, s: (n + s[0], 0))
    arrays = (queries, *both, row_places, *key_places, attended_grad)
    return kernel_call(
        kernel,
        jnp.full((1,), s, jnp.int32),
        (*arrays, *into),
        attention_specs(rows, 2) + [row_spec] + [pl.BlockSpec(memory_space=pl.ANY)] * len(into),
        [
            jax.ShapeDtypeStruct(queries.shape, F32),
            jax.ShapeDtypeStruct(both[0].shape, F32),
            jax.ShapeDtypeStruct(both[0].shape, BF16),
        ],
        [row_spec, both_spec, both_spec],
        (1,),
        "attend_back",
        aliases={1 + len(arrays) + n: n for n in range(len(into))},
    )


def pack_attention(qkv_weight, dense_weight, halves):
    rows = qkv_weight.shape[1]
    count = halves.shape[0]

    def kernel(h_ref, qkv_ref, dense_ref, *out_refs):
        for n in range(count):
            for t in range(3):
                out_refs[n][:, t * HD : (t + 1) * HD] = qkv_ref[t, :, aligned(h_ref[n], HD)]
            out_refs[n][:, 3 * HD :] = dense_ref[:, aligned(h_ref[n], HD)]

    def spec(columns):
        return pl.BlockSpec((rows // 2, columns), lambda r, h: (r, 0))

    return kernel_call(
        kernel,
        halves,
        (qkv_weight, dense_weight),
        [pl.BlockSpec((3, rows // 2, 2 * HD), lambda r, h: (0, r, 0)), spec(2 * HD)],
        [jax.ShapeDtypeStruct((rows, 4 * HD), BF16)] * count,
        [spec(4 * HD)] * count,
        (2,),
        "pack_attention",
    )


class Rounds:
    def __init__(self):
        self.last = ()

    def __call__(self, *arrays):
        got = lax.optimization_barrier((*arrays, *self.last))[: len(arrays)]
        return got if len(arrays) > 1 else got[0]

    def done(self, *arrays):
        self.last = arrays
        return arrays if len(arrays) > 1 else arrays[0]

    def close(self, *arrays):
        self.last = (*self.last, *arrays)


def per_device(
    tokens,
    lengths,
    block_order,
    ln_gain,
    ln_bias,
    qkv_weight,
    qkv_bias,
    dense_weight,
    dense_bias,
    fc1_weight,
    fc1_bias,
    fc2_weight,
    fc2_bias,
    cotangent,
):
    me = lax.axis_index("fsdp")
    core = me % 2
    tp_index = lax.axis_index("tp").astype(jnp.int32)
    tp_size = lax.axis_size("tp")
    ctx_index = lax.axis_index("ctx")
    ctx_size = lax.axis_size("ctx")
    pairs = ctx_size == 2
    side = ctx_index % 2 if pairs else 0 * ctx_index
    shard = ln_gain.shape[0]
    row_count = tokens.shape[1]
    block_rows = row_count // 2
    score_scale = 1.0 / math.sqrt(HD)
    order = jnp.stack([me, me ^ 1, me ^ (2 + side), me ^ (3 - side)]).astype(jnp.int32)
    near_bits, far_bits = ((2, 3), (3, 2)) if pairs else ((2, 2), (3, 3))
    inputs_low, upstream_low = tokens[0], cotangent[0]
    then = Rounds()

    halves = jnp.stack([core, 1 - core, core ^ side, core ^ 1 ^ side]).astype(jnp.int32)

    def relayed(name):
        return RELAY[name] and pairs

    def four(weight, name):
        return [half_of(weight, halves[n], 1) for n in range(3 if relayed(name) else 4)]

    def far_of(name, near, packs):
        return ctx_pair(near) if relayed(name) else fsdp_permute(then(packs[3]), far_bits)

    def joined(pieces):
        return jnp.concatenate(pieces, axis=0)

    seq_count, slots = lengths.shape[1], block_order.shape[1]
    fc1_packs = then.done(*four(fc1_weight, "fc1"))
    fc1_near = fsdp_permute(fc1_packs[2], near_bits)
    own_vectors = jnp.concatenate(
        [
            v.astype(F32)
            for v in (then(ln_gain), ln_bias, dense_bias, fc2_bias, lengths[0], block_order[0])
        ]
    )
    inputs_other = swap(inputs_low, 1)
    vectors = [
        own_vectors,
        swap(own_vectors, 1),
        fsdp_permute(own_vectors, near_bits),
        fsdp_permute(own_vectors, far_bits),
    ]
    packs = pack_attention(
        qkv_weight.transpose(1, 0, 2), then(dense_weight), halves[: 3 if relayed("attention") else 4]
    )
    then.done(*packs)
    fc2_packs = four(then(fc2_weight), "fc2")
    then.done(*fc2_packs)
    upstream_sum = jnp.sum(then(upstream_low).astype(F32), axis=0, keepdims=True)
    then.close(inputs_other, *vectors[1:], fc1_near)

    def over_features(n):
        return jnp.concatenate([v[n * shard : (n + 1) * shard] for v in vectors])[None, :]

    norm_gain, norm_bias = over_features(0), over_features(1)
    out_bias = over_features(2) + over_features(3)
    their_layout = vectors[1][4 * shard :].astype(jnp.int32)

    upstream_other = swap(then(upstream_low), 1)
    fc1_core, attention_core = swap(then(fc1_packs[1]), 1), swap(then(packs[1]), 1)
    attention_near = fsdp_permute(then(packs[2]), near_bits)
    fc1_far = far_of("fc1", then(fc1_near), fc1_packs)
    normed = then.done(frame_rows(inputs_low, then(inputs_other), order, (norm_gain, norm_bias)))
    layouts = [
        (then(lengths[0]), block_order[0]),
        (their_layout[:seq_count], their_layout[seq_count:]),
    ]
    local_slots = ctx_index * 2 + jnp.arange(2, dtype=jnp.int32)
    if pairs:
        key_slots = jnp.concatenate([local_slots, (1 - ctx_index) * 2 + jnp.arange(2)])
    else:
        key_slots = jnp.arange(slots, dtype=jnp.int32)
    allowed, valid, positions, row_places, key_places = [], [], [], [], []
    for lengths_row, order_row in layouts:
        local_packed = packed_rows(order_row, local_slots, block_rows)
        key_packed = packed_rows(order_row, key_slots, block_rows)
        segment, position = place_rows(local_packed, lengths_row)
        key_segment = place_rows(key_packed, lengths_row)[0]
        allowed.append(
            (segment[:, None] == key_segment[None, :])
            & (key_packed[None, :] <= local_packed[:, None])
        )
        valid.append((segment < seq_count).astype(F32)[:, None])
        positions.append(position)
        row_places.append(jnp.stack([local_packed - position, local_packed], axis=1))
        key_places.append(key_packed[None, :])
    cosine_table, sine_table = rotation_tables(jnp.concatenate(positions))
    valid = jnp.concatenate(valid)
    row_places, key_places = jnp.stack(row_places), jnp.stack(key_places)
    upstream_near, upstream_far = [
        jnp.concatenate(
            [lax.dynamic_slice_in_dim(upstream_sum, order[k] * shard, shard, axis=1) for k in blocks],
            axis=1,
        )
        for blocks in ((0, 1), (2 + side, 3 - side))
    ]
    then.done(cosine_table, sine_table, valid, upstream_near, upstream_far, row_places, key_places)
    then.close(upstream_other, fc1_core, attention_core, attention_near, fc1_far, out_bias)
    fc1_pieces = [fc1_packs[0], fc1_core, fc1_near, fc1_far]

    def grad_block(k, *products, kind=BF16):
        parts = []
        for left, right in products:
            rows = lax.dynamic_slice_in_dim(left, k * shard, shard, axis=1)
            parts.append(dot(rows, right, ((0,), (0,))).astype(kind))
        return jnp.concatenate(parts, axis=1)

    def grad_blocks(*products):
        far = grad_block(2 + side, *products)
        rest = [grad_block(k, *products) for k in (3 - side, 1)]
        return (far, *rest, grad_block(0, *products, kind=F32))

    def add_mine(own, far):
        return then.done((own + then(far).astype(F32)).astype(BF16))

    def add_theirs(near, farther):
        return then.done((near.astype(F32) + then(farther).astype(F32)).astype(BF16))

    def placed(mine, theirs, attention=False):
        parts = then(*mine, *theirs)
        return then.done(*place_grad(parts, core, attention))

    fc2_near = fsdp_permute(then(fc2_packs[2]), near_bits)
    fc2_core = swap(then(fc2_packs[1]), 1)
    attention_far = far_of("attention", then(attention_near), packs)
    attention = [packs[0], attention_core, attention_near, attention_far]
    pre_act = dot(then(normed), joined(fc1_pieces), ((1,), (0,)))
    pre_act = pre_act + half_of(fc1_bias, core, 0).astype(F32)[None, :]
    normal_cdf = 0.5 * (1.0 + lax.erf(pre_act * (1.0 / math.sqrt(2.0))))
    density = jnp.exp(-0.5 * pre_act * pre_act) * (1.0 / math.sqrt(2.0 * math.pi))
    hidden = (pre_act * normal_cdf).astype(BF16)
    slope = normal_cdf + pre_act * density
    hidden, slope = then.done(hidden, slope)
    upstream = then.done(frame_rows(upstream_low, then(upstream_other), order))
    fc2_blocks = then.done(*grad_blocks((then(upstream), hidden)))
    then.close(fc2_near, attention_far, fc2_core)

    def row_block_of(index):
        place, bit = 0 * index, 1
        while bit < tp_size:
            place = place * 2 + (index // bit) % 2
            bit *= 2
        return place

    def flips_to_places(flips):
        return jnp.stack([row_block_of(tp_index ^ f) for f in flips]).astype(jnp.int32)

    fc2_far = far_of("fc2", then(fc2_near), fc2_packs)
    fc2_pieces = [fc2_packs[0], fc2_core, fc2_near, fc2_far]
    fc2_grad_near = swap(then(fc2_blocks[2]), 1)
    qkv_bias_own = half_of(qkv_bias, core, 1).astype(F32).reshape(1, 3 * HD)
    queries, both_local = then.done(
        *project(then(normed), attention, qkv_bias_own, cosine_table, sine_table)
    )
    both_local = both_local.reshape(2, row_count, 2 * HD)
    if pairs:
        both_other = ctx_pair(both_local)
    else:
        both_other = lax.all_gather(both_local, "ctx", axis=1, tiled=True)
    attended_grad = then.done(attended_grads(then(upstream), attention, valid))
    then.close(fc2_far, fc2_grad_near)

    fc2_grad_far = swap(then(fc2_blocks[0]), 2)
    hidden_grad = dot(then(upstream), joined(fc2_pieces), ((1,), (0,)))
    pre_grad = then.done((hidden_grad * slope).astype(BF16))
    both_other = then(both_other)
    attended, probs_all = [], []
    if pairs:
        both = (both_local, both_other)
        key_parts = key_places[:, :, :row_count], key_places[:, :, row_count:]
        attended = then.done(attend(queries, both, row_places, key_parts, valid))
    else:
        for s in range(2):
            rows = slice(s * row_count, (s + 1) * row_count)
            keys, values = both_other[s, :, :HD], both_other[s, :, HD:]
            scores = dot(queries[rows], keys, ((1,), (1,))) * score_scale
            scores = jnp.where(allowed[s], scores, MASK_FLOOR)
            exp_scores = jnp.exp(scores - jnp.max(scores, axis=1, keepdims=True))
            probs = exp_scores / jnp.sum(exp_scores, axis=1, keepdims=True)
            probs_all.append(probs)
            attended.append(dot(probs.astype(BF16), values, ((1,), (0,))))
        attended = then.done((jnp.concatenate(attended) * valid).astype(BF16))
    hidden_size = hidden.shape[1]
    second = (hidden, fc2_pieces, 0, hidden_size)
    theirs = then.done(share_rows((attended, attention, 3, HD), second, row_count))
    then.close(fc2_grad_far)

    def attention_grads(s, into=()):
        if pairs:
            return then.done(
                *attend_back(s, queries, both, row_places, key_parts, then(attended_grad), into)
            )
        rows = slice(s * row_count, (s + 1) * row_count)
        keys, values = both_other[s, :, :HD], both_other[s, :, HD:]
        probs, head_grad = probs_all[s], then(attended_grad[rows])
        prob_grad = dot(head_grad, values, ((1,), (1,)))
        row_delta = jnp.sum(probs * prob_grad, axis=1, keepdims=True)
        score_grad = (probs * (prob_grad - row_delta)).astype(BF16)
        query_piece = dot(score_grad, keys, ((1,), (0,))) * score_scale
        key_piece = dot(score_grad, queries[rows], ((0,), (0,))) * score_scale
        value_piece = dot(probs.astype(BF16), head_grad, ((0,), (0,)))
        return then.done(query_piece, jnp.concatenate([key_piece, value_piece], axis=1))

    low = tp_index % 2

    def halve_on(kept, got, bit, row_block):
        while bit < tp_size:
            digit = (tp_index // bit) % 2
            given, kept = then.done(*halve_rows(digit, kept, got))
            got, row_block, bit = tp_pair(given, bit), row_block * 2 + digit, bit * 2
        return kept, got, row_block

    def double_up(part):
        pieces, flips, bit = [part], [0], tp_size // 2
        while bit > 1:
            pieces += [tp_pair(p, bit) for p in pieces]
            flips += [f ^ bit for f in flips]
            bit //= 2
        return pieces, flips + [f ^ 1 for f in flips]

    def fc1_block(k, kind=BF16):
        return weight_grad(k, shard, [(then(normed), pre_grad)], kind)

    fc2_grad_farther = swap(then(fc2_blocks[1]), 3)
    theirs = swap(then(theirs), 1)
    fc2_mine = ctx_terms(add_mine(fc2_blocks[3], fc2_grad_far))
    grads_first = attention_grads(0)
    first = (then(attended), attention, 3, HD)
    given, kept = then.done(*share_rows(first, second, row_count, theirs, low))
    fc1_far_block = then.done(grad_block(2 + side, (then(normed), pre_grad)))
    then.close(fc2_grad_farther)

    fc1_grad_far = swap(then(fc1_far_block), 2)
    out_got = tp_pair(then(given), 1)
    if pairs:
        query_grad, both_grad, both_given = attention_grads(1, grads_first)
        both_got = ctx_pair(both_given)
    else:
        grads_second = attention_grads(1)
        both_grad = jnp.stack([grads_first[1], grads_second[1]])
        query_grad = jnp.concatenate([grads_first[0], grads_second[0]])
        both_got = jnp.zeros((2, row_count, 2 * HD), BF16)
        both_grad = lax.psum_scatter(both_grad, "ctx", scatter_dimension=1, tiled=True)
        query_grad, both_grad = then.done(query_grad, both_grad)
    fc1_farther_block = then.done(grad_block(3 - side, (then(normed), pre_grad)))
    fc1_near_block = then.done(grad_block(1, (then(normed), pre_grad)))
    fc1_grad_near = swap(fc1_near_block, 1)
    fc1_own_block = then.done(fc1_block(0, F32))
    fc2_theirs = add_theirs(fc2_grad_near, fc2_grad_farther)
    then.close(fc1_grad_far, out_got, fc2_mine[1])

    fc1_grad_farther = swap(then(fc1_farther_block), 3)
    out_kept, out_got, out_block = halve_on(then(kept), out_got, 2, low)
    fc2_theirs = ctx_terms(then(fc2_theirs))
    proj_grad = then.done(
        turn_back(then(query_grad), both_grad, both_got, cosine_table, sine_table)
    )
    second = (pre_grad, fc1_pieces, 0, hidden_size)
    theirs = then.done(share_rows((proj_grad, attention, 0, 3 * HD), second, row_count))

    def attention_block(k, kind=BF16):
        return weight_grad(k, shard, [(then(normed), proj_grad), (upstream, attended)], kind)

    far_block = then.done(attention_block(2 + side))
    fc1_mine = add_mine(fc1_own_block, fc1_grad_far)
    then.close(fc1_grad_farther, out_got, fc2_theirs[1], fc1_grad_near)

    attention_grad_far = swap(then(far_block), 2)
    theirs = swap(then(theirs), 1)
    fc1_mine = ctx_terms(then(fc1_mine))
    out_part = then.done(
        finish_output(order, out_block, then(out_kept), out_got, inputs_low, out_bias)
    )
    out_pieces, flips = double_up(out_part)
    out_late = [tp_pair(out_part, 1)]
    first = (then(proj_grad), attention, 0, 3 * HD)
    given, kept = then.done(*share_rows(first, second, row_count, theirs, low))
    farther_block = then.done(attention_block(3 - side))
    fc1_theirs = add_theirs(fc1_grad_near, fc1_grad_farther)
    then.close(attention_grad_far, out_late[0], *out_pieces[1:], fc1_mine[1])

    attention_grad_farther = swap(then(farther_block), 3)
    got = tp_pair(then(given), 1)
    fc1_theirs = ctx_terms(then(fc1_theirs))
    norm_near, norm_far = then.done(*norm_grads(order, low, side, then(inputs_low), given, kept))
    sums, sums_given = then.done(
        *pack_sums(
            (norm_near, norm_far), (upstream_near, upstream_far), then(pre_grad), proj_grad
        )
    )
    sums_got = swap(sums_given, 2)
    near_block = then.done(attention_block(1))
    attention_grad_near = swap(near_block, 1)
    own_block = then.done(attention_block(0, kind=F32))
    attention_mine = add_mine(own_block, attention_grad_far)
    then.close(attention_grad_farther, got, fc1_theirs[1], sums_got)

    attention_mine = ctx_terms(then(attention_mine))
    kept, got, row_block = halve_on(then(kept), got, 2, low)
    out_late += [tp_pair(p, 1) for p in then(out_pieces[0], *out_pieces[1:])[1:]]
    sums = then(sums) + sums_got
    norm_sums, other_sums = sums[:2], sums[2:]
    norm_sums = norm_sums + tp_pair(norm_sums, 1)
    attention_theirs = add_theirs(attention_grad_near, attention_grad_farther)
    fc2_out = placed(fc2_mine, fc2_theirs)
    then.close(got, norm_sums, attention_mine[1], *out_late[1:])

    attention_theirs = ctx_terms(then(attention_theirs))
    input_part = then.done(
        finish_input_grad(order, row_block, then(kept), got, inputs_low, upstream_low, norm_gain)
    )
    pieces, _ = double_up(input_part)
    late = [tp_pair(input_part, 1)]
    bit = 2
    while bit < tp_size:
        norm_sums = norm_sums + tp_pair(then(norm_sums), bit)
        bit *= 2
    fc1_out = placed(fc1_mine, fc1_theirs)
    output = then.done(gather_rows(then(*out_pieces, *out_late), flips_to_places(flips), tp_size, BF16))
    then.close(*pieces[1:], late[0], norm_sums, attention_theirs[1])

    late += [tp_pair(p, 1) for p in then(*pieces, output)[1 : len(pieces)]]
    sums = sum(ctx_terms(jnp.concatenate([then(norm_sums), other_sums])))
    early = len(pieces) + 1
    places = flips_to_places(flips)
    input_grad = then.done(
        gather_rows(then(*pieces, late[0]), places[:early], tp_size, F32)
    )
    qkv_out, dense_out = placed(attention_mine, attention_theirs, True)
    then.close(*late[1:])

    other_core = swap(sums, 1)
    vector_sums = sums[:3, :shard] + other_core[:3, shard : 2 * shard]

    def column_sums(packed):
        return packed[3, :hidden_size], packed[4, : 3 * HD].reshape(3, HD)

    rest = then(*late)[1:]
    input_grad = gather_rows(rest, places[early:], tp_size, F32, (input_grad,))

    def in_order(mine, other, axis):
        return jnp.where(
            core == 0,
            jnp.concatenate([mine, other], axis=axis),
            jnp.concatenate([other, mine], axis=axis),
        )

    fc1_bias_grad, qkv_bias_grad = [
        in_order(mine, other, axis)
        for axis, mine, other in zip((0, 1), column_sums(sums), column_sums(other_core))
    ]
    return (
        output[None],
        input_grad[None],
        vector_sums[0],
        vector_sums[1],
        qkv_out.transpose(1, 0, 2),
        qkv_bias_grad,
        dense_out,
        vector_sums[2],
        fc1_out,
        fc1_bias_grad,
        fc2_out,
        vector_sums[2],
    )


def solution(mesh):
    placed = (
        P("fsdp", "ctx", None),
        P("fsdp", None),
        P("fsdp", None),
        P("fsdp"),
        P("fsdp"),
        P("fsdp", None, "tp"),
        P(None, "tp"),
        P("fsdp", "tp"),
        P("fsdp"),
        P("fsdp", "tp"),
        P("tp"),
        P("fsdp", "tp"),
        P("fsdp"),
        P("fsdp", "ctx", None),
    )
    return jax.shard_map(
        per_device,
        mesh=mesh,
        in_specs=placed,
        out_specs=(
            P("fsdp", "ctx", None),
            P("fsdp", "ctx", None),
            P("fsdp"),
            P("fsdp"),
            P("fsdp", None, "tp"),
            P(None, "tp"),
            P("fsdp", "tp"),
            P("fsdp"),
            P("fsdp", "tp"),
            P("tp"),
            P("fsdp", "tp"),
            P("fsdp"),
        ),
        check_vma=False,
    )
```

```python
import math

import jax
import jax.numpy as jnp
from jax import lax
from jax.experimental import pallas as pl
from jax.experimental.pallas import tpu as pltpu
from jax.sharding import PartitionSpec as P

HD = 256
ROT = 64


NORM_EPSILON = 1e-05
MASK_FLOOR = -1000000000.0
F32 = jnp.float32
BF16 = jnp.bfloat16
LANES = 128
RELAY = {"attention": True, "fc1": True, "fc2": False}


def rotation_tables(position):
    half = ROT // 2
    frequency = jnp.exp(jnp.arange(half, dtype=F32) * (-2.0 * math.log(10000.0) / ROT))
    angles = position.astype(F32)[:, None] * frequency[None, :]
    cosine, sine = jnp.cos(angles), jnp.sin(angles)
    rest = (position.shape[0], LANES - ROT)
    return (
        jnp.concatenate([cosine, cosine, jnp.ones(rest, F32)], axis=1),
        jnp.concatenate([-sine, sine, jnp.zeros(rest, F32)], axis=1),
    )


def packed_rows(order_row, slots, block_rows):
    selector = slots[:, None] == jnp.arange(order_row.shape[0], dtype=jnp.int32)[None, :]
    source_block = jnp.sum(jnp.where(selector, order_row[None, :], 0), axis=1, dtype=jnp.int32)
    within = jnp.arange(block_rows, dtype=jnp.int32)
    return (source_block[:, None] * block_rows + within[None, :]).reshape(-1)


def place_rows(packed_at, lengths_row):
    seq_ends = jnp.cumsum(lengths_row, dtype=jnp.int32)
    passed = packed_at[:, None] >= seq_ends[None, :]
    segment = jnp.sum(passed.astype(jnp.int32), axis=1, dtype=jnp.int32)
    before = jnp.sum(jnp.where(passed, lengths_row[None, :], 0), axis=1, dtype=jnp.int32)
    return (segment, packed_at - before)


def dot(a, b, contract):
    return lax.dot_general(a, b, (contract, ((), ())), preferred_element_type=F32)


def fsdp_permute(x, bits):
    size, lanes = lax.axis_size("fsdp"), lax.axis_size("ctx")
    perm = [
        (f * lanes + x, (f ^ bits[x % 2]) * lanes + x) for f in range(size) for x in range(lanes)
    ]
    return lax.ppermute(x, ("fsdp", "ctx"), perm)


def swap(x, bit):
    return fsdp_permute(x, (bit, bit))


def ctx_pair(x):
    return lax.ppermute(x, "ctx", [(0, 1), (1, 0)])


def ctx_terms(x):
    if lax.axis_size("ctx") == 2:
        return x, ctx_pair(x)
    return lax.psum(x.astype(F32), "ctx"), jnp.zeros_like(x)


def tp_pair(x, bit):
    return lax.ppermute(x, "tp", [(i, i ^ bit) for i in range(lax.axis_size("tp"))])


def half_of(x, which, axis):
    size = x.shape[axis] // 2
    return lax.dynamic_slice_in_dim(x, which * size, size, axis=axis)


def kernel_call(body, scalars, arrays, in_specs, out_shape, out_specs, grid, name, scratch=(), aliases=None):
    return pl.pallas_call(
        body,
        out_shape=out_shape,
        grid_spec=pltpu.PrefetchScalarGridSpec(
            num_scalar_prefetch=1,
            grid=grid,
            in_specs=in_specs,
            out_specs=out_specs,
            scratch_shapes=scratch,
        ),
        input_output_aliases=aliases or {},
        cost_estimate=pl.CostEstimate(flops=0, transcendentals=0, bytes_accessed=0),
        name=name,
    )(scalars, *arrays)


def aligned(index, size):
    return pl.ds(pl.multiple_of(index * size, size), size)


def frame_rows(own, other, order, norm=None):
    rows, columns = own.shape
    width, step = columns // 4, rows // 2

    def kernel(order_ref, own_ref, other_ref, *refs):
        gain_ref, bias_ref, out_ref, wide_ref = refs if norm else (None, None, refs[0], None)
        for s, ref in enumerate((own_ref, other_ref)):
            if norm:
                x = ref[...].astype(F32)
                x = x - jnp.mean(x, axis=1, keepdims=True)
                variance = jnp.mean(x * x, axis=1, keepdims=True)
                wide_ref[...] = x * lax.rsqrt(variance + NORM_EPSILON)
            for k in range(4):
                to = slice(k * width, (k + 1) * width)
                at = aligned(order_ref[k], width)
                if norm:
                    out_ref[s, :, to] = (
                        wide_ref[:, at] * gain_ref[:, to] + bias_ref[:, to]
                    ).astype(BF16)
                else:
                    out_ref[s, :, to] = ref[:, at]

    row_spec = pl.BlockSpec((step, columns), lambda r, o: (r, 0))
    vector_spec = pl.BlockSpec((1, columns), lambda r, o: (0, 0))
    out = kernel_call(
        kernel,
        order,
        (own, other, *(norm or ())),
        [row_spec, row_spec] + ([vector_spec, vector_spec] if norm else []),
        jax.ShapeDtypeStruct((2, rows, columns), BF16),
        pl.BlockSpec((2, step, columns), lambda r, o: (0, r, 0)),
        (2,),
        "norm_rows" if norm else "frame_rows",
        scratch=[pltpu.VMEM((step, columns), F32)] if norm else (),
    )
    return out.reshape(2 * rows, columns)


def place_grad(parts, core, attention):
    rows, columns = parts[0].shape
    step = rows // 2

    def kernel(core_ref, a_ref, ax_ref, b_ref, bx_ref, *out_refs):
        for h, (u_ref, ux_ref) in enumerate(((a_ref, ax_ref), (b_ref, bx_ref))):
            total = u_ref[...].astype(F32) + ux_ref[...].astype(F32)
            place = core_ref[0] ^ h
            if attention:
                for t in range(3):
                    out_refs[0][t, :, aligned(place, HD)] = total[:, t * HD : (t + 1) * HD]
                out_refs[1][:, aligned(place, HD)] = total[:, 3 * HD :]
            else:
                out_refs[0][:, aligned(place, columns)] = total

    shapes = [(rows, 2 * columns)]
    specs = [pl.BlockSpec((step, 2 * columns), lambda r, c: (r, 0))]
    if attention:
        shapes = [(3, rows, 2 * HD), (rows, 2 * HD)]
        specs = [
            pl.BlockSpec((3, step, 2 * HD), lambda r, c: (0, r, 0)),
            pl.BlockSpec((step, 2 * HD), lambda r, c: (r, 0)),
        ]
    return kernel_call(
        kernel,
        core[None],
        parts,
        [pl.BlockSpec((step, columns), lambda r, c: (r, 0))] * 4,
        [jax.ShapeDtypeStruct(shape, F32) for shape in shapes],
        specs,
        (2,),
        "place_grad",
    )


def weight_grad(block, shard, products, kind):
    step = shard // 2
    widths = [right.shape[1] for _, right in products]

    def kernel(_, *refs):
        at = 0
        for n, width in enumerate(widths):
            left_ref, right_ref = refs[2 * n : 2 * n + 2]
            total = dot(left_ref[...], right_ref[...], ((0,), (0,)))
            refs[-1][:, at : at + width] = total.astype(kind)
            at += width

    specs = []
    for left, right in products:
        specs.append(pl.BlockSpec((left.shape[0], step), lambda n, k: (0, 2 * k[0] + n)))
        specs.append(pl.BlockSpec(right.shape, lambda n, k: (0, 0)))
    return kernel_call(
        kernel,
        jnp.asarray(block, jnp.int32)[None],
        [a for product in products for a in product],
        specs,
        jax.ShapeDtypeStruct((shard, sum(widths)), kind),
        pl.BlockSpec((step, sum(widths)), lambda n, k: (n, 0)),
        (2,),
        "weight_grad",
    )


def share_rows(first, second, rows, theirs=None, low=None):
    width = first[1][0].shape[0]
    own = theirs is not None
    at = 0 if own else 1
    half, step = rows // 2, 256

    def kernel(low_ref, f_ref, s_ref, *refs):
        f_refs, s_refs, refs = refs[:4], refs[4:8], refs[8:]
        for n in range(2):

            @pl.when(pl.program_id(0) == n)
            def _(n=n):
                for m in range(2):
                    k = 2 * n + m

                    def columns(j, _, k=k, first=(m if own else 1 - m) * (width // step)):
                        at, to = aligned(j, step), aligned(first + j, step)
                        total = dot(f_ref[...], f_refs[k][at, :], ((1,), (1,)))
                        total = total + dot(s_ref[...], s_refs[k][at, :], ((1,), (1,)))
                        if not own:
                            refs[0][:, to] = total.astype(BF16)
                            return
                        theirs_ref, given_ref, kept_ref, all_ref = refs
                        all_ref[...] = (total + theirs_ref[:, to].astype(F32)).astype(BF16)
                        given_ref[:, to] = all_ref[aligned(1 - low_ref[0], half), :]
                        kept_ref[:, to] = all_ref[aligned(low_ref[0], half), :]

                    lax.fori_loop(0, width // step, columns, None)

    arrays, in_specs = [], []
    for acts, _, _, size in (first, second):
        arrays.append(acts)
        in_specs.append(pl.BlockSpec((rows, size), lambda n, b: (at, 0)))
    for _, pieces, block, size in (first, second):
        arrays += pieces
        in_specs += [pl.BlockSpec((width, size), lambda n, b, block=block: (0, block))] * 4
    out_shape = jax.ShapeDtypeStruct((rows, 4 * width), BF16)
    out_spec = pl.BlockSpec((rows, 2 * width), lambda n, b: (0, n))
    scratch = ()
    if own:
        arrays.append(theirs)
        in_specs.append(out_spec)
        out_shape = [jax.ShapeDtypeStruct((half, 4 * width), BF16)] * 2
        out_spec = [pl.BlockSpec((half, 2 * width), lambda n, b: (0, n))] * 2
        scratch = [pltpu.VMEM((rows, step), BF16)]
    return kernel_call(
        kernel,
        low[None] if own else jnp.zeros((1,), jnp.int32),
        arrays,
        in_specs,
        out_shape,
        out_spec,
        (2,),
        "share_rows",
        scratch=scratch,
    )


def finish_output(order, row_block, kept, got, inputs, out_bias):
    rows, columns = kept.shape
    width, steps = columns // 4, 1
    step = rows // steps

    def kernel(s_ref, kept_ref, got_ref, x_ref, bias_ref, out_ref):
        for k in range(4):
            cols, at = slice(k * width, (k + 1) * width), aligned(s_ref[k], width)
            total = kept_ref[:, cols] + got_ref[:, cols].astype(F32)
            out_ref[:, at] = (x_ref[:, at].astype(F32) + total + bias_ref[:, cols]).astype(BF16)

    spec = pl.BlockSpec((step, columns), lambda i, s: (i, 0))
    return kernel_call(
        kernel,
        jnp.concatenate([order, row_block[None]]),
        (kept, got, inputs, out_bias),
        [
            spec,
            spec,
            pl.BlockSpec((step, columns), lambda i, s: (s[4] * steps + i, 0)),
            pl.BlockSpec((1, columns), lambda i, s: (0, 0)),
        ],
        jax.ShapeDtypeStruct((rows, columns), BF16),
        spec,
        (steps,),
        "finish_output",
    )


def finish_input_grad(order, row_block, kept, got, inputs, upstream, norm_gain):
    rows, columns = kept.shape
    width, steps = columns // 4, 1
    step = rows // steps

    def kernel(s_ref, kept_ref, got_ref, x_ref, dy_ref, gain_ref, out_ref, std_ref):
        x = x_ref[...].astype(F32)
        x = x - jnp.mean(x, axis=1, keepdims=True)
        inverse = lax.rsqrt(jnp.mean(x * x, axis=1, keepdims=True) + NORM_EPSILON)
        std_ref[...] = x * inverse
        mean_scaled = jnp.zeros((step, 1), F32)
        mean_product = jnp.zeros((step, 1), F32)

        def parts(k):
            cols, at = slice(k * width, (k + 1) * width), aligned(s_ref[k], width)
            total = kept_ref[:, cols] + got_ref[:, cols].astype(F32)
            return at, total * gain_ref[:, cols], std_ref[:, at]

        for k in range(4):
            _, scaled, standard = parts(k)
            mean_scaled += jnp.sum(scaled, axis=1, keepdims=True) / columns
            mean_product += jnp.sum(scaled * standard, axis=1, keepdims=True) / columns
        for k in range(4):
            at, scaled, standard = parts(k)
            change = inverse * (scaled - mean_scaled - standard * mean_product)
            out_ref[:, at] = (dy_ref[:, at].astype(F32) + change).astype(BF16)

    spec = pl.BlockSpec((step, columns), lambda i, s: (i, 0))
    rows_spec = pl.BlockSpec((step, columns), lambda i, s: (s[4] * steps + i, 0))
    return kernel_call(
        kernel,
        jnp.concatenate([order, row_block[None]]),
        (kept, got, inputs, upstream, norm_gain),
        [spec, spec, rows_spec, rows_spec, pl.BlockSpec((1, columns), lambda i, s: (0, 0))],
        jax.ShapeDtypeStruct((rows, columns), BF16),
        spec,
        (steps,),
        "finish_input_grad",
        scratch=[pltpu.VMEM((step, columns), F32)],
    )


def norm_grads(order, low, side, inputs, given, kept):
    rows, columns = inputs.shape
    width, step = columns // 4, rows // 2

    def kernel(order_ref, x_ref, given_ref, kept_ref, near_ref, far_ref, std_ref):
        x = x_ref[...].astype(F32)
        x = x - jnp.mean(x, axis=1, keepdims=True)
        std_ref[...] = x * lax.rsqrt(jnp.mean(x * x, axis=1, keepdims=True) + NORM_EPSILON)

        def add(share_ref, first):
            for k in range(4):
                cols = slice(k * width, (k + 1) * width)
                part = share_ref[:, cols].astype(F32)
                product = part * std_ref[:, aligned(order_ref[k], width)]
                sums = jnp.sum(product, axis=0, keepdims=True), jnp.sum(part, axis=0, keepdims=True)
                out_ref, at = near_ref, cols
                if k > 1:
                    out_ref, at = far_ref, aligned((k - 2) ^ order_ref[5], width)
                for n in range(2):
                    before = 0.0 if first else out_ref[n : n + 1, at]
                    out_ref[n : n + 1, at] = before + sums[n]

        @pl.when(pl.program_id(0) == 0)
        def _():
            add(given_ref, True)

        @pl.when(pl.program_id(0) == 1)
        def _():
            add(kept_ref, False)

    half_spec = pl.BlockSpec((step, columns), lambda r, o: (0, 0))
    return kernel_call(
        kernel,
        jnp.concatenate([order, low[None], side[None].astype(jnp.int32)]),
        (inputs, given, kept),
        [
            pl.BlockSpec((step, columns), lambda r, o: (r * o[4] + (1 - r) * (1 - o[4]), 0)),
            half_spec,
            half_spec,
        ],
        [jax.ShapeDtypeStruct((2, columns // 2), F32)] * 2,
        [pl.BlockSpec((2, columns // 2), lambda r, o: (0, 0))] * 2,
        (2,),
        "norm_grads",
        scratch=[pltpu.VMEM((step, columns), F32)],
    )


def halve_rows(digit, kept, got):
    rows, columns = kept.shape

    def kernel(_, a_ref, b_ref, c_ref, d_ref, given_ref, kept_ref):
        given_ref[...] = (a_ref[...].astype(F32) + b_ref[...].astype(F32)).astype(BF16)
        kept_ref[...] = c_ref[...].astype(F32) + d_ref[...].astype(F32)

    block = rows // 2, columns // 2
    leaves = pl.BlockSpec(block, lambda n, d: (1 - d[0], n))
    stays = pl.BlockSpec(block, lambda n, d: (d[0], n))
    out_spec = pl.BlockSpec(block, lambda n, d: (0, n))
    return kernel_call(
        kernel,
        digit[None],
        (kept, got, kept, got),
        [leaves, leaves, stays, stays],
        [jax.ShapeDtypeStruct((rows // 2, columns), kind) for kind in (BF16, F32)],
        [out_spec, out_spec],
        (2,),
        "halve_rows",
    )


def pack_sums(norm_sums, upstream_sums, pre_grad, proj_grad):
    wide = max(norm_sums[0].shape[1], pre_grad.shape[1], proj_grad.shape[1])
    step = pre_grad.shape[0] // 8

    def kernel(_, *refs):
        norm_refs, up_refs, grad_refs, out_refs = refs[:2], refs[2:4], refs[4:6], refs[6:]
        for out_ref in out_refs:
            out_ref[...] = jnp.zeros_like(out_ref)
        for norm_ref, up_ref, out_ref in zip(norm_refs, up_refs, out_refs):
            out_ref[0:2, : norm_ref.shape[1]] = norm_ref[...]
            out_ref[2:3, : up_ref.shape[1]] = up_ref[...]
        for n, ref in enumerate(grad_refs):
            total = jnp.zeros((1, ref.shape[1]), F32)
            for c in range(8):
                part = ref[c * step : (c + 1) * step, :].astype(F32)
                total = total + jnp.sum(part, axis=0, keepdims=True)
            for out_ref in out_refs:
                out_ref[3 + n : 4 + n, : ref.shape[1]] = total

    arrays = (*norm_sums, *upstream_sums, pre_grad, proj_grad)
    return kernel_call(
        kernel,
        jnp.zeros((1,), jnp.int32),
        arrays,
        [pl.BlockSpec(a.shape, lambda n, z: (0, 0)) for a in arrays],
        [jax.ShapeDtypeStruct((8, wide), F32)] * 2,
        [pl.BlockSpec((8, wide), lambda n, z: (0, 0))] * 2,
        (1,),
        "pack_sums",
    )


def gather_rows(pieces, places, count, dtype, into=()):
    rows, columns = pieces[0].shape

    def kernel(_, *refs):
        for n in range(len(pieces)):

            @pl.when(pl.program_id(0) == n)
            def _(n=n):
                refs[-1][...] = refs[n][...].astype(dtype)

    return kernel_call(
        kernel,
        places,
        (*pieces, *into),
        [pl.BlockSpec((rows, columns), lambda n, p: (0, 0))] * len(pieces)
        + [pl.BlockSpec(memory_space=pl.ANY)] * len(into),
        jax.ShapeDtypeStruct((rows * count, columns), dtype),
        pl.BlockSpec((rows, columns), lambda n, p: (p[n], 0)),
        (len(pieces),),
        "gather_rows",
        aliases={1 + len(pieces): 0} if into else None,
    )


def turned(x, cosine, sine):
    lane = lax.broadcasted_iota(jnp.int32, x.shape, 1)
    half = ROT // 2
    partner = jnp.where(
        lane < half, pltpu.roll(x, x.shape[1] - half, axis=1), pltpu.roll(x, half, axis=1)
    )
    return x * cosine + partner * sine


def project(normed, pieces, bias, cosine, sine):
    rows = normed.shape[0] // 2
    width = pieces[0].shape[0]

    def kernel(_, x_ref, *refs):
        piece_refs, (bias_ref, cos_ref, sin_ref, q_ref, kv_ref) = refs[:4], refs[4:]
        total = dot(x_ref[:, :width], piece_refs[0][...], ((1,), (0,)))
        for k in range(1, 4):
            cols = slice(k * width, (k + 1) * width)
            total = total + dot(x_ref[:, cols], piece_refs[k][...], ((1,), (0,)))
        total = total + bias_ref[...]
        cosine, sine = cos_ref[...], sin_ref[...]
        for n, ref in enumerate((q_ref, kv_ref)):
            head = total[:, n * HD : (n + 1) * HD]
            ref[:, :LANES] = turned(head[:, :LANES], cosine, sine).astype(BF16)
            ref[:, LANES:HD] = head[:, LANES:].astype(BF16)
        kv_ref[:, HD:] = total[:, 2 * HD :].astype(BF16)

    def by_row(columns):
        return pl.BlockSpec((rows, columns), lambda s, z: (s, 0))

    return kernel_call(
        kernel,
        jnp.zeros((1,), jnp.int32),
        (normed, *pieces, bias, cosine, sine),
        [by_row(normed.shape[1])]
        + [pl.BlockSpec((width, 3 * HD), lambda s, z: (0, 0))] * 4
        + [pl.BlockSpec((1, 3 * HD), lambda s, z: (0, 0)), by_row(LANES), by_row(LANES)],
        [
            jax.ShapeDtypeStruct((2 * rows, HD), BF16),
            jax.ShapeDtypeStruct((2 * rows, 2 * HD), BF16),
        ],
        [by_row(HD), by_row(2 * HD)],
        (2,),
        "project",
    )


def turn_back(query_grad, kept, got, cosine, sine):
    rows = kept.shape[1]

    def kernel(_, q_ref, kept_ref, got_ref, cos_ref, sin_ref, out_ref):
        both = kept_ref[...] + got_ref[...].astype(F32)
        cosine, sine = cos_ref[...], -sin_ref[...]
        for n, head in enumerate((q_ref[...], both[:, :HD])):
            at = n * HD
            out_ref[:, at : at + LANES] = turned(head[:, :LANES], cosine, sine).astype(BF16)
            out_ref[:, at + LANES : at + HD] = head[:, LANES:].astype(BF16)
        out_ref[:, 2 * HD :] = both[:, HD:].astype(BF16)

    def by_row(columns):
        return pl.BlockSpec((rows, columns), lambda s, z: (s, 0))

    both_spec = pl.BlockSpec((None, rows, 2 * HD), lambda s, z: (s, 0, 0))
    return kernel_call(
        kernel,
        jnp.zeros((1,), jnp.int32),
        (query_grad, kept, got, cosine, sine),
        [by_row(HD), both_spec, both_spec, by_row(LANES), by_row(LANES)],
        jax.ShapeDtypeStruct((2 * rows, 3 * HD), BF16),
        by_row(3 * HD),
        (2,),
        "turn_back",
    )


def attended_grads(upstream, pieces, valid):
    rows = upstream.shape[0] // 2
    width = pieces[0].shape[0]

    def kernel(_, dy_ref, *refs):
        piece_refs, (valid_ref, out_ref) = refs[:4], refs[4:]
        total = dot(dy_ref[:, :width], piece_refs[0][...], ((1,), (0,)))
        for k in range(1, 4):
            cols = slice(k * width, (k + 1) * width)
            total = total + dot(dy_ref[:, cols], piece_refs[k][...], ((1,), (0,)))
        out_ref[...] = total.astype(BF16) * valid_ref[...].astype(BF16)

    def by_row(columns):
        return pl.BlockSpec((rows, columns), lambda s, z: (s, 0))

    return kernel_call(
        kernel,
        jnp.zeros((1,), jnp.int32),
        (upstream, *pieces, valid),
        [by_row(upstream.shape[1])]
        + [pl.BlockSpec((width, HD), lambda s, z: (0, 3))] * 4
        + [by_row(1)],
        jax.ShapeDtypeStruct((2 * rows, HD), BF16),
        by_row(HD),
        (2,),
        "attended_grads",
    )


def chances(query, keys, first, last, key_place):
    scores = []
    for part, place in zip(keys, key_place):
        score = dot(query, part, ((1,), (1,))) * (1.0 / math.sqrt(HD))
        scores.append(jnp.where((place >= first) & (place <= last), score, MASK_FLOOR))
    top = jnp.max(scores[0], axis=1, keepdims=True)
    for score in scores[1:]:
        top = jnp.maximum(top, jnp.max(score, axis=1, keepdims=True))
    exps = [jnp.exp(score - top) for score in scores]
    total = sum(jnp.sum(e, axis=1, keepdims=True) for e in exps)
    return [e / total for e in exps]


def attention_specs(rows, parts):
    return (
        [pl.BlockSpec((rows, HD), lambda n, s: (n + s[0], 0))]
        + [pl.BlockSpec((None, rows, 2 * HD), lambda n, s: (n + s[0], 0, 0))] * parts
        + [pl.BlockSpec((None, rows, 2), lambda n, s: (n + s[0], 0, 0))]
        + [pl.BlockSpec((None, 1, rows), lambda n, s: (n + s[0], 0, 0))] * parts
    )


def attend(queries, both, row_places, key_places, valid):
    rows = queries.shape[0] // 2
    parts = len(both)

    def kernel(_, q_ref, *refs):
        both_refs, place_ref, key_refs = refs[:parts], refs[parts], refs[parts + 1 : 2 * parts + 1]
        valid_ref, out_ref = refs[2 * parts + 1 :]
        step = rows // 2
        for c in range(2):
            at = slice(c * step, (c + 1) * step)
            probs = chances(
                q_ref[at, :],
                [ref[:, :HD] for ref in both_refs],
                place_ref[at, 0:1],
                place_ref[at, 1:2],
                [ref[...] for ref in key_refs],
            )
            total = 0.0
            for p, ref in zip(probs, both_refs):
                total = total + dot(p.astype(BF16), ref[:, HD:], ((1,), (0,)))
            out_ref[at, :] = (total * valid_ref[at, :]).astype(BF16)

    return kernel_call(
        kernel,
        jnp.zeros((1,), jnp.int32),
        (queries, *both, row_places, *key_places, valid),
        attention_specs(rows, parts) + [pl.BlockSpec((rows, 1), lambda n, s: (n, 0))],
        jax.ShapeDtypeStruct(queries.shape, BF16),
        pl.BlockSpec((rows, HD), lambda n, s: (n, 0)),
        (2,),
        "attend",
    )


def attend_back(s, queries, both, row_places, key_places, attended_grad, into=()):
    rows = queries.shape[0] // 2
    scale = 1.0 / math.sqrt(HD)

    def kernel(_, q_ref, own_ref, far_ref, place_ref, own_key_ref, far_key_ref, up_ref, *outs):
        query_ref, kept_ref, given_ref = outs[-3:]
        step = rows // 2
        sums = [[0.0, 0.0], [0.0, 0.0]]
        for c in range(2):
            at = slice(c * step, (c + 1) * step)
            query, up = q_ref[at, :], up_ref[at, :]
            probs = chances(
                query,
                [own_ref[:, :HD], far_ref[:, :HD]],
                place_ref[at, 0:1],
                place_ref[at, 1:2],
                [own_key_ref[...], far_key_ref[...]],
            )
            grads = [dot(up, ref[:, HD:], ((1,), (1,))) for ref in (own_ref, far_ref)]
            delta = sum(jnp.sum(p * g, axis=1, keepdims=True) for p, g in zip(probs, grads))
            total = 0.0
            for n, ref in enumerate((own_ref, far_ref)):
                score_grad = (probs[n] * (grads[n] - delta)).astype(BF16)
                total = total + dot(score_grad, ref[:, :HD], ((1,), (0,)))
                sums[n][0] = sums[n][0] + dot(score_grad, query, ((0,), (0,)))
                sums[n][1] = sums[n][1] + dot(probs[n].astype(BF16), up, ((0,), (0,)))
            query_ref[at, :] = total * scale
        for n, ref in enumerate((kept_ref, given_ref)):
            ref[:, :HD] = (sums[n][0] * scale).astype(ref.dtype)
            ref[:, HD:] = sums[n][1].astype(ref.dtype)

    both_spec = pl.BlockSpec((None, rows, 2 * HD), lambda n, s: (n + s[0], 0, 0))
    row_spec = pl.BlockSpec((rows, HD), lambda n, s: (n + s[0], 0))
    arrays = (queries, *both, row_places, *key_places, attended_grad)
    return kernel_call(
        kernel,
        jnp.full((1,), s, jnp.int32),
        (*arrays, *into),
        attention_specs(rows, 2) + [row_spec] + [pl.BlockSpec(memory_space=pl.ANY)] * len(into),
        [
            jax.ShapeDtypeStruct(queries.shape, F32),
            jax.ShapeDtypeStruct(both[0].shape, F32),
            jax.ShapeDtypeStruct(both[0].shape, BF16),
        ],
        [row_spec, both_spec, both_spec],
        (1,),
        "attend_back",
        aliases={1 + len(arrays) + n: n for n in range(len(into))},
    )


def pack_attention(qkv_weight, dense_weight, halves):
    rows = qkv_weight.shape[1]
    count = halves.shape[0]

    def kernel(h_ref, qkv_ref, dense_ref, *out_refs):
        for n in range(count):
            for t in range(3):
                out_refs[n][:, t * HD : (t + 1) * HD] = qkv_ref[t, :, aligned(h_ref[n], HD)]
            out_refs[n][:, 3 * HD :] = dense_ref[:, aligned(h_ref[n], HD)]

    def spec(columns):
        return pl.BlockSpec((rows // 2, columns), lambda r, h: (r, 0))

    return kernel_call(
        kernel,
        halves,
        (qkv_weight, dense_weight),
        [pl.BlockSpec((3, rows // 2, 2 * HD), lambda r, h: (0, r, 0)), spec(2 * HD)],
        [jax.ShapeDtypeStruct((rows, 4 * HD), BF16)] * count,
        [spec(4 * HD)] * count,
        (2,),
        "pack_attention",
    )


class Rounds:
    def __init__(self):
        self.last = ()

    def __call__(self, *arrays):
        got = lax.optimization_barrier((*arrays, *self.last))[: len(arrays)]
        return got if len(arrays) > 1 else got[0]

    def done(self, *arrays):
        self.last = arrays
        return arrays if len(arrays) > 1 else arrays[0]

    def close(self, *arrays):
        self.last = (*self.last, *arrays)


def per_device(
    tokens,
    lengths,
    block_order,
    ln_gain,
    ln_bias,
    qkv_weight,
    qkv_bias,
    dense_weight,
    dense_bias,
    fc1_weight,
    fc1_bias,
    fc2_weight,
    fc2_bias,
    cotangent,
):
    me = lax.axis_index("fsdp")
    core = me % 2
    tp_index = lax.axis_index("tp").astype(jnp.int32)
    tp_size = lax.axis_size("tp")
    ctx_index = lax.axis_index("ctx")
    ctx_size = lax.axis_size("ctx")
    pairs = ctx_size == 2
    side = ctx_index % 2 if pairs else 0 * ctx_index
    shard = ln_gain.shape[0]
    row_count = tokens.shape[1]
    block_rows = row_count // 2
    score_scale = 1.0 / math.sqrt(HD)
    order = jnp.stack([me, me ^ 1, me ^ (2 + side), me ^ (3 - side)]).astype(jnp.int32)
    near_bits, far_bits = ((2, 3), (3, 2)) if pairs else ((2, 2), (3, 3))
    inputs_low, upstream_low = tokens[0], cotangent[0]
    then = Rounds()

    halves = jnp.stack([core, 1 - core, core ^ side, core ^ 1 ^ side]).astype(jnp.int32)

    def relayed(name):
        return RELAY[name] and pairs

    def four(weight, name):
        return [half_of(weight, halves[n], 1) for n in range(3 if relayed(name) else 4)]

    def far_of(name, near, packs):
        return ctx_pair(near) if relayed(name) else fsdp_permute(then(packs[3]), far_bits)

    def joined(pieces):
        return jnp.concatenate(pieces, axis=0)

    seq_count, slots = lengths.shape[1], block_order.shape[1]
    fc1_packs = then.done(*four(fc1_weight, "fc1"))
    fc1_near = fsdp_permute(fc1_packs[2], near_bits)
    own_vectors = jnp.concatenate(
        [
            v.astype(F32)
            for v in (then(ln_gain), ln_bias, dense_bias, fc2_bias, lengths[0], block_order[0])
        ]
    )
    inputs_other = swap(inputs_low, 1)
    vectors = [
        own_vectors,
        swap(own_vectors, 1),
        fsdp_permute(own_vectors, near_bits),
        fsdp_permute(own_vectors, far_bits),
    ]
    packs = pack_attention(
        qkv_weight.transpose(1, 0, 2), then(dense_weight), halves[: 3 if relayed("attention") else 4]
    )
    then.done(*packs)
    fc2_packs = four(then(fc2_weight), "fc2")
    then.done(*fc2_packs)
    upstream_sum = jnp.sum(then(upstream_low).astype(F32), axis=0, keepdims=True)
    then.close(inputs_other, *vectors[1:], fc1_near)

    def over_features(n):
        return jnp.concatenate([v[n * shard : (n + 1) * shard] for v in vectors])[None, :]

    norm_gain, norm_bias = over_features(0), over_features(1)
    out_bias = over_features(2) + over_features(3)
    their_layout = vectors[1][4 * shard :].astype(jnp.int32)

    upstream_other = swap(then(upstream_low), 1)
    fc1_core, attention_core = swap(then(fc1_packs[1]), 1), swap(then(packs[1]), 1)
    attention_near = fsdp_permute(then(packs[2]), near_bits)
    fc1_far = far_of("fc1", then(fc1_near), fc1_packs)
    normed = then.done(frame_rows(inputs_low, then(inputs_other), order, (norm_gain, norm_bias)))
    layouts = [
        (then(lengths[0]), block_order[0]),
        (their_layout[:seq_count], their_layout[seq_count:]),
    ]
    local_slots = ctx_index * 2 + jnp.arange(2, dtype=jnp.int32)
    if pairs:
        key_slots = jnp.concatenate([local_slots, (1 - ctx_index) * 2 + jnp.arange(2)])
    else:
        key_slots = jnp.arange(slots, dtype=jnp.int32)
    allowed, valid, positions, row_places, key_places = [], [], [], [], []
    for lengths_row, order_row in layouts:
        local_packed = packed_rows(order_row, local_slots, block_rows)
        key_packed = packed_rows(order_row, key_slots, block_rows)
        segment, position = place_rows(local_packed, lengths_row)
        key_segment = place_rows(key_packed, lengths_row)[0]
        allowed.append(
            (segment[:, None] == key_segment[None, :])
            & (key_packed[None, :] <= local_packed[:, None])
        )
        valid.append((segment < seq_count).astype(F32)[:, None])
        positions.append(position)
        row_places.append(jnp.stack([local_packed - position, local_packed], axis=1))
        key_places.append(key_packed[None, :])
    cosine_table, sine_table = rotation_tables(jnp.concatenate(positions))
    valid = jnp.concatenate(valid)
    row_places, key_places = jnp.stack(row_places), jnp.stack(key_places)
    upstream_near, upstream_far = [
        jnp.concatenate(
            [lax.dynamic_slice_in_dim(upstream_sum, order[k] * shard, shard, axis=1) for k in blocks],
            axis=1,
        )
        for blocks in ((0, 1), (2 + side, 3 - side))
    ]
    then.done(cosine_table, sine_table, valid, upstream_near, upstream_far, row_places, key_places)
    then.close(upstream_other, fc1_core, attention_core, attention_near, fc1_far, out_bias)
    fc1_pieces = [fc1_packs[0], fc1_core, fc1_near, fc1_far]

    def grad_block(k, *products, kind=BF16):
        parts = []
        for left, right in products:
            rows = lax.dynamic_slice_in_dim(left, k * shard, shard, axis=1)
            parts.append(dot(rows, right, ((0,), (0,))).astype(kind))
        return jnp.concatenate(parts, axis=1)

    def grad_blocks(*products):
        far = grad_block(2 + side, *products)
        rest = [grad_block(k, *products) for k in (3 - side, 1)]
        return (far, *rest, grad_block(0, *products, kind=F32))

    def add_mine(own, far):
        return then.done((own + then(far).astype(F32)).astype(BF16))

    def add_theirs(near, farther):
        return then.done((near.astype(F32) + then(farther).astype(F32)).astype(BF16))

    def placed(mine, theirs, attention=False):
        parts = then(*mine, *theirs)
        return then.done(*place_grad(parts, core, attention))

    fc2_near = fsdp_permute(then(fc2_packs[2]), near_bits)
    fc2_core = swap(then(fc2_packs[1]), 1)
    attention_far = far_of("attention", then(attention_near), packs)
    attention = [packs[0], attention_core, attention_near, attention_far]
    pre_act = dot(then(normed), joined(fc1_pieces), ((1,), (0,)))
    pre_act = pre_act + half_of(fc1_bias, core, 0).astype(F32)[None, :]
    normal_cdf = 0.5 * (1.0 + lax.erf(pre_act * (1.0 / math.sqrt(2.0))))
    density = jnp.exp(-0.5 * pre_act * pre_act) * (1.0 / math.sqrt(2.0 * math.pi))
    hidden = (pre_act * normal_cdf).astype(BF16)
    slope = normal_cdf + pre_act * density
    hidden, slope = then.done(hidden, slope)
    upstream = then.done(frame_rows(upstream_low, then(upstream_other), order))
    fc2_blocks = then.done(*grad_blocks((then(upstream), hidden)))
    then.close(fc2_near, attention_far, fc2_core)

    def row_block_of(index):
        place, bit = 0 * index, 1
        while bit < tp_size:
            place = place * 2 + (index // bit) % 2
            bit *= 2
        return place

    def flips_to_places(flips):
        return jnp.stack([row_block_of(tp_index ^ f) for f in flips]).astype(jnp.int32)

    fc2_far = far_of("fc2", then(fc2_near), fc2_packs)
    fc2_pieces = [fc2_packs[0], fc2_core, fc2_near, fc2_far]
    fc2_grad_near = swap(then(fc2_blocks[2]), 1)
    qkv_bias_own = half_of(qkv_bias, core, 1).astype(F32).reshape(1, 3 * HD)
    queries, both_local = then.done(
        *project(then(normed), attention, qkv_bias_own, cosine_table, sine_table)
    )
    both_local = both_local.reshape(2, row_count, 2 * HD)
    if pairs:
        both_other = ctx_pair(both_local)
    else:
        both_other = lax.all_gather(both_local, "ctx", axis=1, tiled=True)
    attended_grad = then.done(attended_grads(then(upstream), attention, valid))
    then.close(fc2_far, fc2_grad_near)

    fc2_grad_far = swap(then(fc2_blocks[0]), 2)
    hidden_grad = dot(then(upstream), joined(fc2_pieces), ((1,), (0,)))
    pre_grad = then.done((hidden_grad * slope).astype(BF16))
    both_other = then(both_other)
    attended, probs_all = [], []
    if pairs:
        both = (both_local, both_other)
        key_parts = key_places[:, :, :row_count], key_places[:, :, row_count:]
        attended = then.done(attend(queries, both, row_places, key_parts, valid))
    else:
        for s in range(2):
            rows = slice(s * row_count, (s + 1) * row_count)
            keys, values = both_other[s, :, :HD], both_other[s, :, HD:]
            scores = dot(queries[rows], keys, ((1,), (1,))) * score_scale
            scores = jnp.where(allowed[s], scores, MASK_FLOOR)
            exp_scores = jnp.exp(scores - jnp.max(scores, axis=1, keepdims=True))
            probs = exp_scores / jnp.sum(exp_scores, axis=1, keepdims=True)
            probs_all.append(probs)
            attended.append(dot(probs.astype(BF16), values, ((1,), (0,))))
        attended = then.done((jnp.concatenate(attended) * valid).astype(BF16))
    hidden_size = hidden.shape[1]
    second = (hidden, fc2_pieces, 0, hidden_size)
    theirs = then.done(share_rows((attended, attention, 3, HD), second, row_count))
    then.close(fc2_grad_far)

    def attention_grads(s, into=()):
        if pairs:
            return then.done(
                *attend_back(s, queries, both, row_places, key_parts, then(attended_grad), into)
            )
        rows = slice(s * row_count, (s + 1) * row_count)
        keys, values = both_other[s, :, :HD], both_other[s, :, HD:]
        probs, head_grad = probs_all[s], then(attended_grad[rows])
        prob_grad = dot(head_grad, values, ((1,), (1,)))
        row_delta = jnp.sum(probs * prob_grad, axis=1, keepdims=True)
        score_grad = (probs * (prob_grad - row_delta)).astype(BF16)
        query_piece = dot(score_grad, keys, ((1,), (0,))) * score_scale
        key_piece = dot(score_grad, queries[rows], ((0,), (0,))) * score_scale
        value_piece = dot(probs.astype(BF16), head_grad, ((0,), (0,)))
        return then.done(query_piece, jnp.concatenate([key_piece, value_piece], axis=1))

    low = tp_index % 2

    def halve_on(kept, got, bit, row_block):
        while bit < tp_size:
            digit = (tp_index // bit) % 2
            given, kept = then.done(*halve_rows(digit, kept, got))
            got, row_block, bit = tp_pair(given, bit), row_block * 2 + digit, bit * 2
        return kept, got, row_block

    def double_up(part):
        pieces, flips, bit = [part], [0], tp_size // 2
        while bit > 1:
            pieces += [tp_pair(p, bit) for p in pieces]
            flips += [f ^ bit for f in flips]
            bit //= 2
        return pieces, flips + [f ^ 1 for f in flips]

    def fc1_block(k, kind=BF16):
        return weight_grad(k, shard, [(then(normed), pre_grad)], kind)

    fc2_grad_farther = swap(then(fc2_blocks[1]), 3)
    theirs = swap(then(theirs), 1)
    fc2_mine = ctx_terms(add_mine(fc2_blocks[3], fc2_grad_far))
    grads_first = attention_grads(0)
    first = (then(attended), attention, 3, HD)
    given, kept = then.done(*share_rows(first, second, row_count, theirs, low))
    fc1_far_block = then.done(grad_block(2 + side, (then(normed), pre_grad)))
    then.close(fc2_grad_farther)

    fc1_grad_far = swap(then(fc1_far_block), 2)
    out_got = tp_pair(then(given), 1)
    if pairs:
        query_grad, both_grad, both_given = attention_grads(1, grads_first)
        both_got = ctx_pair(both_given)
    else:
        grads_second = attention_grads(1)
        both_grad = jnp.stack([grads_first[1], grads_second[1]])
        query_grad = jnp.concatenate([grads_first[0], grads_second[0]])
        both_got = jnp.zeros((2, row_count, 2 * HD), BF16)
        both_grad = lax.psum_scatter(both_grad, "ctx", scatter_dimension=1, tiled=True)
        query_grad, both_grad = then.done(query_grad, both_grad)
    fc1_farther_block = then.done(grad_block(3 - side, (then(normed), pre_grad)))
    fc1_near_block = then.done(grad_block(1, (then(normed), pre_grad)))
    fc1_grad_near = swap(fc1_near_block, 1)
    fc1_own_block = then.done(fc1_block(0, F32))
    fc2_theirs = add_theirs(fc2_grad_near, fc2_grad_farther)
    then.close(fc1_grad_far, out_got, fc2_mine[1])

    fc1_grad_farther = swap(then(fc1_farther_block), 3)
    out_kept, out_got, out_block = halve_on(then(kept), out_got, 2, low)
    fc2_theirs = ctx_terms(then(fc2_theirs))
    proj_grad = then.done(
        turn_back(then(query_grad), both_grad, both_got, cosine_table, sine_table)
    )
    second = (pre_grad, fc1_pieces, 0, hidden_size)
    theirs = then.done(share_rows((proj_grad, attention, 0, 3 * HD), second, row_count))

    def attention_block(k, kind=BF16):
        return weight_grad(k, shard, [(then(normed), proj_grad), (upstream, attended)], kind)

    far_block = then.done(attention_block(2 + side))
    fc1_mine = add_mine(fc1_own_block, fc1_grad_far)
    then.close(fc1_grad_farther, out_got, fc2_theirs[1], fc1_grad_near)

    attention_grad_far = swap(then(far_block), 2)
    theirs = swap(then(theirs), 1)
    fc1_mine = ctx_terms(then(fc1_mine))
    out_part = then.done(
        finish_output(order, out_block, then(out_kept), out_got, inputs_low, out_bias)
    )
    out_pieces, flips = double_up(out_part)
    out_late = [tp_pair(out_part, 1)]
    first = (then(proj_grad), attention, 0, 3 * HD)
    given, kept = then.done(*share_rows(first, second, row_count, theirs, low))
    farther_block = then.done(attention_block(3 - side))
    fc1_theirs = add_theirs(fc1_grad_near, fc1_grad_farther)
    then.close(attention_grad_far, out_late[0], *out_pieces[1:], fc1_mine[1])

    attention_grad_farther = swap(then(farther_block), 3)
    got = tp_pair(then(given), 1)
    fc1_theirs = ctx_terms(then(fc1_theirs))
    norm_near, norm_far = then.done(*norm_grads(order, low, side, then(inputs_low), given, kept))
    sums, sums_given = then.done(
        *pack_sums(
            (norm_near, norm_far), (upstream_near, upstream_far), then(pre_grad), proj_grad
        )
    )
    sums_got = swap(sums_given, 2)
    near_block = then.done(attention_block(1))
    attention_grad_near = swap(near_block, 1)
    own_block = then.done(attention_block(0, kind=F32))
    attention_mine = add_mine(own_block, attention_grad_far)
    then.close(attention_grad_farther, got, fc1_theirs[1], sums_got)

    attention_mine = ctx_terms(then(attention_mine))
    kept, got, row_block = halve_on(then(kept), got, 2, low)
    out_late += [tp_pair(p, 1) for p in then(out_pieces[0], *out_pieces[1:])[1:]]
    sums = then(sums) + sums_got
    norm_sums, other_sums = sums[:2], sums[2:]
    norm_sums = norm_sums + tp_pair(norm_sums, 1)
    attention_theirs = add_theirs(attention_grad_near, attention_grad_farther)
    fc2_out = placed(fc2_mine, fc2_theirs)
    then.close(got, norm_sums, attention_mine[1], *out_late[1:])

    attention_theirs = ctx_terms(then(attention_theirs))
    input_part = then.done(
        finish_input_grad(order, row_block, then(kept), got, inputs_low, upstream_low, norm_gain)
    )
    pieces, _ = double_up(input_part)
    late = [tp_pair(input_part, 1)]
    bit = 2
    while bit < tp_size:
        norm_sums = norm_sums + tp_pair(then(norm_sums), bit)
        bit *= 2
    fc1_out = placed(fc1_mine, fc1_theirs)
    output = then.done(gather_rows(then(*out_pieces, *out_late), flips_to_places(flips), tp_size, BF16))
    then.close(*pieces[1:], late[0], norm_sums, attention_theirs[1])

    late += [tp_pair(p, 1) for p in then(*pieces, output)[1 : len(pieces)]]
    sums = sum(ctx_terms(jnp.concatenate([then(norm_sums), other_sums])))
    early = len(pieces) + 1
    places = flips_to_places(flips)
    input_grad = then.done(
        gather_rows(then(*pieces, late[0]), places[:early], tp_size, F32)
    )
    qkv_out, dense_out = placed(attention_mine, attention_theirs, True)
    then.close(*late[1:])

    other_core = swap(sums, 1)
    vector_sums = sums[:3, :shard] + other_core[:3, shard : 2 * shard]

    def column_sums(packed):
        return packed[3, :hidden_size], packed[4, : 3 * HD].reshape(3, HD)

    rest = then(*late)[1:]
    input_grad = gather_rows(rest, places[early:], tp_size, F32, (input_grad,))

    def in_order(mine, other, axis):
        return jnp.where(
            core == 0,
            jnp.concatenate([mine, other], axis=axis),
            jnp.concatenate([other, mine], axis=axis),
        )

    fc1_bias_grad, qkv_bias_grad = [
        in_order(mine, other, axis)
        for axis, mine, other in zip((0, 1), column_sums(sums), column_sums(other_core))
    ]
    return (
        output[None],
        input_grad[None],
        vector_sums[0],
        vector_sums[1],
        qkv_out.transpose(1, 0, 2),
        qkv_bias_grad,
        dense_out,
        vector_sums[2],
        fc1_out,
        fc1_bias_grad,
        fc2_out,
        vector_sums[2],
    )


def solution(mesh):
    placed = (
        P("fsdp", "ctx", None),
        P("fsdp", None),
        P("fsdp", None),
        P("fsdp"),
        P("fsdp"),
        P("fsdp", None, "tp"),
        P(None, "tp"),
        P("fsdp", "tp"),
        P("fsdp"),
        P("fsdp", "tp"),
        P("tp"),
        P("fsdp", "tp"),
        P("fsdp"),
        P("fsdp", "ctx", None),
    )
    return jax.shard_map(
        per_device,
        mesh=mesh,
        in_specs=placed,
        out_specs=(
            P("fsdp", "ctx", None),
            P("fsdp", "ctx", None),
            P("fsdp"),
            P("fsdp"),
            P("fsdp", None, "tp"),
            P(None, "tp"),
            P("fsdp", "tp"),
            P("fsdp"),
            P("fsdp", "tp"),
            P("tp"),
            P("fsdp", "tp"),
            P("fsdp"),
        ),
        check_vma=False,
    )
```
